512 devices in a mesh: dp: 64 (over z_hi, x, y), tile: 8 (over z_lo, core).
Axes of the slice: x: 4, y: 8, z: 8 (z_hi: 2, z_lo: 4; z = z_hi * 4 + z_lo), core: 2. Of those that a mesh axis runs over, the one named last changes fastest.
Arguments:
- feats: bfloat16 [4096, 2048], P('dp'), may hold values from -11 to 11
- jitter: bfloat16 [4096, 2048], P('dp'), may hold values from -1.5 to 1.5
- mask_ids: int32 [4096, 2], P('dp'), may hold values from 0 to 31
- proj_weight: bfloat16 [2048, 4096], P('dp', 'tile'), may hold values from -0.125 to 0.125
Outputs:
- feats_grad: float32 [4096, 2048], P('dp', 'tile')
- diag_corr: float32 [4096], P('tile')
- cross_power: float32 [], replicated
The draws below stay inside these ranges and needn't reach their ends.
All inputs are finite; a program needn't handle non-finite values.
Results may differ from the reference program's by a relative error of at most 0.02.
Values may be sent and summed in bfloat16 or wider, within the bound.
No kernel may reach another device: no remote copies, remote signals or barrier semaphores. Data moves between devices by JAX's collectives and lax.ppermute only.
A program may use at most 64 MiB of HBM per device.

```python
import jax
import jax.numpy as jnp
from jax import lax

D_IN = 2048
EMB = 4096
GROUPS = 32
BATCH = 4096


def draw_feats(key, part):
    first, second = jax.random.split(key, 2)
    positions = jnp.arange(BATCH, dtype=jnp.float32)
    rising = 0.6 * jnp.exp(jnp.log(3.0) * positions / BATCH)
    spread = jnp.exp(jax.random.uniform(second, (BATCH,), minval=-0.35, maxval=0.35))
    scales = (rising * spread)[:, None]
    values = jnp.clip(jax.random.normal(first, (BATCH, D_IN)), -4.0, 4.0) * scales
    return values.astype(jnp.bfloat16)


def place_ends(entries, rng, smallest, high):
    longest = entries.shape.index(max(entries.shape))
    spots = []
    for shift in (0, 1):
        where = [jax.random.randint(jax.random.fold_in(rng, axis), (), 0, length) for axis, length in enumerate(entries.shape)]
        where[longest] = (where[longest] + shift) % entries.shape[longest]
        spots.append(tuple(where))
    return entries.at[spots[0]].set(smallest).at[spots[1]].set(high)


def block_scale(rng, extent, shards, least, high):
    loudness, own = 1.0, jax.random.fold_in(rng, 6)
    for dim, blocks in shards:
        steps = jnp.exp(jax.random.uniform(jax.random.fold_in(own, dim), (blocks,), jnp.float32, least / len(shards), high / len(shards)))
        loudness = loudness * jnp.repeat(steps, extent[dim] // blocks).reshape([-1 if axis == dim else 1 for axis in range(len(extent))])
    return loudness


def scatter_about(key, dims, deviation, bound, shards=(), kind=jnp.bfloat16):
    array = deviation * jax.random.normal(key, dims, jnp.float32)
    if shards:
        array = array * block_scale(key, dims, shards, -0.22, 0.18)
    return jnp.clip(array, -bound, bound).astype(kind)


def setup_inputs(seed: int = 0) -> dict:
    key_of = jax.random.split(jax.random.key(seed), 5)
    return {
        "feats": draw_feats(jax.random.fold_in(key_of[4], 71), 0),
        "jitter": scatter_about(key_of[1], (BATCH, D_IN), 0.25, 1.5, ((0, 64),)),
        "mask_ids": place_ends(jax.random.randint(key_of[2], (BATCH, 2), 0, GROUPS), jax.random.fold_in(key_of[2], 1), 0, GROUPS - 1).astype(jnp.int32),
        "proj_weight": scatter_about(key_of[3], (D_IN, EMB), D_IN ** -0.5, 0.125, ((0, 64), (1, 8))),
    }


LAMBDA_OFF = 0.0051
NORM_EPS = 1e-05
LOSS_SCALE = 65536.0

def reference(feats, jitter, mask_ids, proj_weight):
    group_size = D_IN // GROUPS
    channel_group = jnp.arange(D_IN, dtype=jnp.int32)[None, :] // group_size
    keep_a = (channel_group != mask_ids[:, 0:1]).astype(jnp.float32)
    keep_b = (channel_group != mask_ids[:, 1:2]).astype(jnp.float32)
    view_a = (feats.astype(jnp.float32) * keep_a).astype(jnp.bfloat16)
    view_b = (feats.astype(jnp.float32) * keep_b + jitter.astype(jnp.float32)).astype(jnp.bfloat16)

    def project(view):
        raw = jnp.dot(view, proj_weight, preferred_element_type=jnp.float32).astype(jnp.bfloat16)
        values = raw.astype(jnp.float32)
        mean = lax.optimization_barrier(jnp.mean(values, axis=0))
        centered = values - mean
        inverse = lax.rsqrt(lax.optimization_barrier(jnp.mean(centered * centered, axis=0)) + NORM_EPS)
        return ((centered * inverse).astype(jnp.bfloat16), inverse)
    norm_a, inv_a = project(view_a)
    norm_b, inv_b = project(view_b)
    za = norm_a.astype(jnp.float32)
    zb = norm_b.astype(jnp.float32)
    diag_corr = lax.optimization_barrier(jnp.sum(za * zb, axis=0)) / BATCH
    gram_a = jnp.dot(norm_a, norm_a.T, preferred_element_type=jnp.float32)
    gram_b = jnp.dot(norm_b, norm_b.T, preferred_element_type=jnp.float32)
    cross_power = jnp.sum(gram_a * gram_b) / (BATCH * BATCH) / EMB
    coeff = -2.0 * (1.0 - diag_corr) - 2.0 * LAMBDA_OFF * diag_corr
    factor = 2.0 * LAMBDA_OFF / (BATCH * BATCH)
    grad_na = zb * coeff / BATCH + factor * jnp.dot(gram_b.astype(jnp.bfloat16), norm_a, preferred_element_type=jnp.float32)
    grad_nb = za * coeff / BATCH + factor * jnp.dot(gram_a.astype(jnp.bfloat16), norm_b, preferred_element_type=jnp.float32)

    def norm_back(grad, normed, inverse):
        first = lax.optimization_barrier(jnp.mean(grad, axis=0))
        second = lax.optimization_barrier(jnp.mean(grad * normed, axis=0))
        return (inverse * (grad - first - normed * second)).astype(jnp.bfloat16)
    dz_a = norm_back(grad_na, za, inv_a)
    dz_b = norm_back(grad_nb, zb, inv_b)
    back_a = jnp.dot(dz_a, proj_weight.T, preferred_element_type=jnp.float32)
    back_b = jnp.dot(dz_b, proj_weight.T, preferred_element_type=jnp.float32)
    feats_grad = LOSS_SCALE * (keep_a * back_a + keep_b * back_b)
    return (feats_grad, diag_corr, cross_power)
```

```python
import jax
import jax.numpy as jnp
from jax import lax
from jax.sharding import Mesh
from jax.sharding import PartitionSpec as P

GROUPS = 32
LAMBDA_OFF = 0.0051
NORM_EPS = 1e-05
LOSS_SCALE = 65536.0

DP_SHAPE = (2, 4, 8)
TILE_SHAPE = (4, 2)
DP = ("zh", "x", "y")
ROWS = "y"
COLS = ("zh", "x")
TILE = ("zl", "c")
BF = jnp.bfloat16
F32 = jnp.float32


def masked_views(feats, jitter, mask_ids):
    width = feats.shape[1]
    group_size = width // GROUPS
    channel_group = lax.broadcasted_iota(jnp.int32, (1, width), 1) // group_size
    keep_a = (channel_group != mask_ids[:, 0:1]).astype(F32)
    keep_b = (channel_group != mask_ids[:, 1:2]).astype(F32)
    values = feats.astype(F32)
    view_a = (values * keep_a).astype(BF)
    view_b = (values * keep_b + jitter.astype(F32)).astype(BF)
    return view_a, view_b, keep_a, keep_b


def pieces(value, count):
    out = []
    for _ in range(count):
        part = lax.reduce_precision(value, 8, 7)
        out.append(part.astype(BF))
        value = value - part
    return out


def joined(rows):
    total = rows[..., 0, :].astype(F32)
    for i in range(1, rows.shape[-2]):
        total = total + rows[..., i, :].astype(F32)
    return total


def stack_rows(rows, count):
    rows = [jnp.reshape(r, (1, -1)) for r in rows]
    width = rows[0].shape[1]
    if len(rows) < count:
        rows.append(jnp.zeros((count - len(rows), width), BF))
    return jnp.concatenate(rows, axis=0)


def exchange(blocks, extra, axes):
    parts = blocks.shape[0]
    tail = jnp.broadcast_to(extra[None], (parts,) + extra.shape)
    got = lax.all_to_all(jnp.concatenate([blocks, tail], axis=1), axes, 0, 0, tiled=True)
    return got[:, : blocks.shape[1]], got[:, blocks.shape[1] :]


def swap_pairs():
    y_n = DP_SHAPE[2]
    cols_n = DP_SHAPE[0] * DP_SHAPE[1]
    tile_n = TILE_SHAPE[0] * TILE_SHAPE[1]
    where = lambda c, y, t: (c * y_n + y) * tile_n + t
    return [
        (where(c, y, t), where(t, y, c))
        for c in range(cols_n)
        for y in range(y_n)
        for t in range(tile_n)
    ]


def dot(a, b, ca, cb):
    return lax.dot_general(a, b, (((ca,), (cb,)), ((), ())), preferred_element_type=F32)


def on_device(feats, jitter, mask_ids, weight):
    view_a, view_b, keep_a, keep_b = masked_views(feats, jitter, mask_ids)
    rows, width = feats.shape
    kt = weight.shape[1]
    zh_n, x_n, y_n = DP_SHAPE
    cols_n = zh_n * x_n
    tile_n = TILE_SHAPE[0] * TILE_SHAPE[1]
    total = rows * cols_n * y_n
    block = rows * cols_n
    sub = kt // y_n
    all_axes = DP + TILE
    pairs = swap_pairs()

    piece = lax.all_gather(weight, "x", axis=0, tiled=True)
    piece = lax.all_gather(piece, "zh", axis=0, tiled=True)
    piece = lax.all_gather(piece, "y", axis=0, tiled=True)
    piece = piece.reshape(y_n, cols_n, -1, kt).swapaxes(0, 1).reshape(width, kt)

    raw = dot(jnp.concatenate([view_a, view_b], axis=0), piece, 1, 0).astype(BF)
    raw_a, raw_b = raw[:rows], raw[rows:]

    own_b = lax.ppermute(raw_b, all_axes, pairs)
    big_a = lax.all_gather(raw_a, "x", axis=0, tiled=True)
    big_a = lax.all_gather(big_a, "zh", axis=0, tiled=True).astype(F32)
    big_b = lax.all_gather(own_b, TILE, axis=0, tiled=True).astype(F32)

    part_mean_a = jnp.mean(big_a, axis=0)
    part_mean_b = jnp.mean(big_b, axis=0)
    mid_a = big_a - part_mean_a
    mid_b = big_b - part_mean_b
    square_a = jnp.sum(mid_a * mid_a, axis=0)
    square_b = jnp.sum(mid_b * mid_b, axis=0)
    cross = jnp.sum(mid_a * mid_b, axis=0)
    gram = dot(mid_a.astype(BF), mid_b.astype(BF), 0, 0).astype(BF)

    stats = [part_mean_a, square_a, part_mean_b, square_b, cross]
    stat_rows = stack_rows([p for s in stats for p in pieces(s, 3)], 16)
    got, got_stats = exchange(gram.reshape(y_n, sub, kt), stat_rows, ROWS)
    means_a, squares_a, means_b, squares_b, crosses = (
        joined(got_stats[:, 3 * i : 3 * i + 3]) for i in range(5)
    )

    def moments(means, squares):
        mean = jnp.mean(means, axis=0)
        off = means - mean
        var = (jnp.sum(squares, axis=0) + block * jnp.sum(off * off, axis=0)) / total
        return mean, off, lax.rsqrt(var + NORM_EPS)

    mean_a, off_a, inv_a = moments(means_a, squares_a)
    mean_b, off_b, inv_b = moments(means_b, squares_b)
    y_at = lax.axis_index("y")
    cols_at = lax.axis_index(COLS)
    tile_at = lax.axis_index(TILE)
    on_diag = (cols_at == tile_at).astype(F32)
    diag = (jnp.sum(crosses, axis=0) + block * jnp.sum(off_a * off_b, axis=0)) * (
        inv_a * inv_b / total
    )
    coeff = -2.0 * (1.0 - diag) - 2.0 * LAMBDA_OFF * diag

    start = y_at * sub
    off_a_sub = lax.dynamic_slice_in_dim(off_a, start, sub, 1)
    inv_a_sub = lax.dynamic_slice_in_dim(inv_a, start, sub, 0)
    corr = jnp.sum(got.astype(F32), axis=0) + block * lax.dot_general(
        off_a_sub,
        off_b,
        (((0,), (0,)), ((), ())),
        precision=lax.Precision.HIGHEST,
        preferred_element_type=F32,
    )
    corr = corr * (inv_a_sub[:, None] * inv_b[None, :] / total)
    k_of = lax.broadcasted_iota(jnp.int32, (sub, kt), 0) + start
    l_of = lax.broadcasted_iota(jnp.int32, (sub, kt), 1)
    here = (k_of == l_of) & (cols_at == tile_at)
    mix = jnp.where(here, coeff + 2.0 * LAMBDA_OFF * diag, 2.0 * LAMBDA_OFF * corr)
    mix = lax.all_gather(mix.astype(BF), ROWS, axis=0, tiled=True)

    mix32 = mix.astype(F32)
    k_of = lax.broadcasted_iota(jnp.int32, (kt, kt), 0)
    l_of = lax.broadcasted_iota(jnp.int32, (kt, kt), 1)
    here = (k_of == l_of) & (cols_at == tile_at)
    corr = jnp.where(here, diag, mix32 * (0.5 / LAMBDA_OFF))
    product = mix32 * corr
    second_a = jnp.sum(product, axis=1)
    second_b = jnp.sum(product, axis=0)
    power = jnp.sum(corr * corr, axis=1)
    norm_mean_a = block * jnp.sum(off_a, axis=0) * inv_a / total
    norm_mean_b = block * jnp.sum(off_b, axis=0) * inv_b / total
    first_a = jnp.sum(mix32 * norm_mean_b[None, :], axis=1)
    first_b = jnp.sum(mix32 * norm_mean_a[:, None], axis=0)

    norm_a = ((big_a - mean_a) * inv_a).astype(BF)
    norm_b = ((big_b - mean_b) * inv_b).astype(BF)
    grad_a = dot(norm_b, mix, 1, 1).astype(BF)
    grad_b = dot(norm_a, mix, 1, 0).astype(BF)

    tail_b = stack_rows(pieces(second_b, 3) + pieces(first_b, 2), 8)
    got_b, tail_b = exchange(grad_b.reshape(tile_n, rows, kt), tail_b, TILE)
    second_b = jnp.sum(joined(tail_b[:, 0:3]), axis=0)
    first_b = jnp.sum(joined(tail_b[:, 3:5]), axis=0)
    own_norm_b = ((own_b.astype(F32) - mean_b) * inv_b).astype(BF).astype(F32)
    grad_b = jnp.sum(got_b.astype(F32), axis=0)
    dz_b = (inv_b * (grad_b - first_b - own_norm_b * second_b)).astype(BF)
    dz_b = lax.ppermute(dz_b, all_axes, pairs)

    tail_a = stack_rows(
        pieces(second_a, 2) + pieces(power, 2) + pieces(diag * on_diag, 3) + pieces(first_a, 1), 8
    )
    got_a, tail_a = exchange(grad_a.reshape(cols_n, rows, kt), tail_a, COLS)
    second_a = jnp.sum(joined(tail_a[:, 0:2]), axis=0)
    power = jnp.sum(joined(tail_a[:, 2:4]))
    diag_corr = jnp.sum(joined(tail_a[:, 4:7]), axis=0)
    first_a = jnp.sum(joined(tail_a[:, 7:8]), axis=0)
    own_norm_a = ((raw_a.astype(F32) - mean_a) * inv_a).astype(BF).astype(F32)
    grad_a = jnp.sum(got_a.astype(F32), axis=0)
    dz_a = (inv_a * (grad_a - first_a - own_norm_a * second_a)).astype(BF)

    combined = keep_a * dot(dz_a, piece, 1, 1) + keep_b * dot(dz_b, piece, 1, 1)
    share = combined.astype(BF).reshape(rows, tile_n, width // tile_n).swapaxes(0, 1)
    power_rows = stack_rows(pieces(jnp.broadcast_to(power, (width // tile_n,)), 3), 8)
    got, power_rows = exchange(share, power_rows, TILE)
    feats_grad = (LOSS_SCALE / total) * jnp.sum(got.astype(F32), axis=0)
    cross_power = jnp.sum(joined(power_rows[:, 0:3])[:, 0]) / (kt * tile_n)
    return feats_grad, diag_corr, cross_power


def solution(mesh):
    fine = Mesh(mesh.devices.reshape(DP_SHAPE + TILE_SHAPE), DP + TILE)
    in_specs = (P(DP, None), P(DP, None), P(DP, None), P(DP, TILE))
    out_specs = (P(DP, TILE), P(TILE), P())
    return jax.shard_map(
        on_device, mesh=fine, in_specs=in_specs, out_specs=out_specs, check_vma=False
    )
```

```python
import jax
import jax.numpy as jnp
from jax import lax
from jax.sharding import Mesh
from jax.sharding import PartitionSpec as P

GROUPS = 32
LAMBDA_OFF = 0.0051
NORM_EPS = 1e-05
LOSS_SCALE = 65536.0

DP_SHAPE = (2, 4, 8)
TILE_SHAPE = (4, 2)
DP = ("zh", "x", "y")
ROWS = "y"
COLS = ("zh", "x")
TILE = ("zl", "c")
BF = jnp.bfloat16
F32 = jnp.float32


def masked_views(feats, jitter, mask_ids):
    width = feats.shape[1]
    group_size = width // GROUPS
    channel_group = lax.broadcasted_iota(jnp.int32, (1, width), 1) // group_size
    keep_a = (channel_group != mask_ids[:, 0:1]).astype(F32)
    keep_b = (channel_group != mask_ids[:, 1:2]).astype(F32)
    values = feats.astype(F32)
    view_a = (values * keep_a).astype(BF)
    view_b = (values * keep_b + jitter.astype(F32)).astype(BF)
    return view_a, view_b, keep_a, keep_b


def pieces(value, count):
    out = []
    for _ in range(count):
        part = lax.reduce_precision(value, 8, 7)
        out.append(part.astype(BF))
        value = value - part
    return out


def joined(rows):
    total = rows[..., 0, :].astype(F32)
    for i in range(1, rows.shape[-2]):
        total = total + rows[..., i, :].astype(F32)
    return total


def stack_rows(rows, count):
    rows = [jnp.reshape(r, (1, -1)) for r in rows]
    width = rows[0].shape[1]
    if len(rows) < count:
        rows.append(jnp.zeros((count - len(rows), width), BF))
    return jnp.concatenate(rows, axis=0)


def exchange(blocks, extra, axes):
    parts = blocks.shape[0]
    tail = jnp.broadcast_to(extra[None], (parts,) + extra.shape)
    got = lax.all_to_all(jnp.concatenate([blocks, tail], axis=1), axes, 0, 0, tiled=True)
    return got[:, : blocks.shape[1]], got[:, blocks.shape[1] :]


def spread(value, axes):
    parts = lax.axis_size(axes)
    return lax.all_to_all(
        jnp.broadcast_to(value[None], (parts,) + value.shape), axes, 0, 0, tiled=True
    ).reshape((parts * value.shape[0],) + value.shape[1:])


def pick(blocks, at, axis):
    return lax.dynamic_index_in_dim(blocks, at, axis, keepdims=False)


def fold_core(blocks, tail, counts):
    at = lax.axis_index("c")
    own_tail = [pieces(r, n) for r, n in zip(tail, counts)]
    rows, width = blocks.shape[2:]
    sent = pick(blocks, 1 - at, 1).astype(BF).reshape(-1, width)
    sent = jnp.concatenate([sent, stack_rows([p for ps in own_tail for p in ps], 8)], axis=0)
    got = lax.ppermute(sent, "c", [(0, 1), (1, 0)])
    main = pick(blocks, at, 1) + got[: -8].reshape(-1, rows, width).astype(F32)
    out, start = [], got.shape[0] - 8
    for ps in own_tail:
        theirs = joined(got[start : start + len(ps)])
        out.append(joined(jnp.stack(ps)) + theirs)
        start += len(ps)
    return main, out


def fold_line(blocks, tail, counts):
    at = lax.axis_index("zl")
    n = blocks.shape[0]
    rows = blocks.shape[1]
    tail_rows = stack_rows([p for r, k in zip(tail, counts) for p in pieces(r, k)], 8)
    main, out = pick(blocks, at, 0), list(tail)
    for step in range(1, n):
        sent = jnp.concatenate([pick(blocks, at ^ step, 0).astype(BF), tail_rows], axis=0)
        got = lax.ppermute(sent, "zl", [(i, i ^ step) for i in range(n)])
        main = main + got[:rows].astype(F32)
        start = rows
        for i, k in enumerate(counts):
            out[i] = out[i] + joined(got[start : start + k])
            start += k
    return main, out


def swap_pairs():
    y_n = DP_SHAPE[2]
    cols_n = DP_SHAPE[0] * DP_SHAPE[1]
    tile_n = TILE_SHAPE[0] * TILE_SHAPE[1]
    where = lambda c, y, t: (c * y_n + y) * tile_n + t
    return [
        (where(c, y, t), where(t, y, c))
        for c in range(cols_n)
        for y in range(y_n)
        for t in range(tile_n)
    ]


def dot(a, b, ca, cb):
    return lax.dot_general(a, b, (((ca,), (cb,)), ((), ())), preferred_element_type=F32)


def on_device(feats, jitter, mask_ids, weight):
    view_a, view_b, keep_a, keep_b = masked_views(feats, jitter, mask_ids)
    rows, width = feats.shape
    kt = weight.shape[1]
    zh_n, x_n, y_n = DP_SHAPE
    cols_n = zh_n * x_n
    tile_n = TILE_SHAPE[0] * TILE_SHAPE[1]
    total = rows * cols_n * y_n
    block = rows * cols_n
    sub = kt // y_n
    all_axes = DP + TILE
    pairs = swap_pairs()

    piece = lax.all_gather(weight, "zh", axis=0, tiled=True)
    piece = spread(spread(piece, "y"), "x")
    piece = piece.reshape(x_n, y_n, zh_n, -1, kt).transpose(2, 0, 1, 3, 4).reshape(width, kt)

    raw = dot(jnp.concatenate([view_a, view_b], axis=0), piece, 1, 0).astype(BF)
    raw_a, raw_b = raw[:rows], raw[rows:]

    own_b = lax.ppermute(raw_b, all_axes, pairs)
    big_a = spread(raw_a, COLS).astype(F32)
    big_b = lax.all_gather(own_b, TILE, axis=0, tiled=True).astype(F32)

    part_mean_a = jnp.mean(big_a, axis=0)
    part_mean_b = jnp.mean(big_b, axis=0)
    mid_a = big_a - part_mean_a
    mid_b = big_b - part_mean_b
    square_a = jnp.sum(mid_a * mid_a, axis=0)
    square_b = jnp.sum(mid_b * mid_b, axis=0)
    cross = jnp.sum(mid_a * mid_b, axis=0)
    gram = dot(mid_a.astype(BF), mid_b.astype(BF), 0, 0).astype(BF)

    stats = [part_mean_a, square_a, part_mean_b, square_b, cross]
    stat_rows = stack_rows([p for s in stats for p in pieces(s, 3)], 16)
    got, got_stats = exchange(gram.reshape(y_n, sub, kt), stat_rows, ROWS)
    means_a, squares_a, means_b, squares_b, crosses = (
        joined(got_stats[:, 3 * i : 3 * i + 3]) for i in range(5)
    )

    def moments(means, squares):
        mean = jnp.mean(means, axis=0)
        off = means - mean
        var = (jnp.sum(squares, axis=0) + block * jnp.sum(off * off, axis=0)) / total
        return mean, off, lax.rsqrt(var + NORM_EPS)

    mean_a, off_a, inv_a = moments(means_a, squares_a)
    mean_b, off_b, inv_b = moments(means_b, squares_b)
    y_at = lax.axis_index("y")
    cols_at = lax.axis_index(COLS)
    tile_at = lax.axis_index(TILE)
    on_diag = (cols_at == tile_at).astype(F32)
    diag = (jnp.sum(crosses, axis=0) + block * jnp.sum(off_a * off_b, axis=0)) * (
        inv_a * inv_b / total
    )
    coeff = -2.0 * (1.0 - diag) - 2.0 * LAMBDA_OFF * diag

    start = y_at * sub
    off_a_sub = lax.dynamic_slice_in_dim(off_a, start, sub, 1)
    inv_a_sub = lax.dynamic_slice_in_dim(inv_a, start, sub, 0)
    corr = jnp.sum(got.astype(F32), axis=0) + block * lax.dot_general(
        off_a_sub,
        off_b,
        (((0,), (0,)), ((), ())),
        precision=lax.Precision.HIGHEST,
        preferred_element_type=F32,
    )
    corr = corr * (inv_a_sub[:, None] * inv_b[None, :] / total)
    k_of = lax.broadcasted_iota(jnp.int32, (sub, kt), 0) + start
    l_of = lax.broadcasted_iota(jnp.int32, (sub, kt), 1)
    here = (k_of == l_of) & (cols_at == tile_at)
    mix = jnp.where(here, coeff + 2.0 * LAMBDA_OFF * diag, 2.0 * LAMBDA_OFF * corr)
    mix = spread(mix.astype(BF), ROWS)

    mix32 = mix.astype(F32)
    k_of = lax.broadcasted_iota(jnp.int32, (kt, kt), 0)
    l_of = lax.broadcasted_iota(jnp.int32, (kt, kt), 1)
    here = (k_of == l_of) & (cols_at == tile_at)
    corr = jnp.where(here, diag, mix32 * (0.5 / LAMBDA_OFF))
    product = mix32 * corr
    second_a = jnp.sum(product, axis=1)
    second_b = jnp.sum(product, axis=0)
    power = jnp.sum(corr * corr, axis=1)
    norm_mean_a = block * jnp.sum(off_a, axis=0) * inv_a / total
    norm_mean_b = block * jnp.sum(off_b, axis=0) * inv_b / total
    first_a = jnp.sum(mix32 * norm_mean_b[None, :], axis=1)
    first_b = jnp.sum(mix32 * norm_mean_a[:, None], axis=0)

    norm_a = ((big_a - mean_a) * inv_a).astype(BF)
    norm_b = ((big_b - mean_b) * inv_b).astype(BF)
    grad_a = dot(norm_b, mix, 1, 1).astype(BF)
    grad_b = dot(norm_a, mix, 1, 0)

    grad_b, tail_b = fold_core(
        grad_b.reshape(TILE_SHAPE + (rows, kt)), (second_b, first_b), (3, 2)
    )
    grad_b, (second_b, first_b) = fold_line(grad_b, tail_b, (3, 2))
    own_norm_b = ((own_b.astype(F32) - mean_b) * inv_b).astype(BF).astype(F32)
    dz_b = (inv_b * (grad_b - first_b - own_norm_b * second_b)).astype(BF)
    dz_b = lax.ppermute(dz_b, all_axes, pairs)

    tail_a = stack_rows(
        pieces(second_a, 2) + pieces(power, 2) + pieces(diag * on_diag, 3) + pieces(first_a, 1), 8
    )
    got_a, tail_a = exchange(grad_a.reshape(cols_n, rows, kt), tail_a, COLS)
    second_a = jnp.sum(joined(tail_a[:, 0:2]), axis=0)
    power = jnp.sum(joined(tail_a[:, 2:4]))
    diag_corr = jnp.sum(joined(tail_a[:, 4:7]), axis=0)
    first_a = jnp.sum(joined(tail_a[:, 7:8]), axis=0)
    own_norm_a = ((raw_a.astype(F32) - mean_a) * inv_a).astype(BF).astype(F32)
    grad_a = jnp.sum(got_a.astype(F32), axis=0)
    dz_a = (inv_a * (grad_a - first_a - own_norm_a * second_a)).astype(BF)

    combined = keep_a * dot(dz_a, piece, 1, 1) + keep_b * dot(dz_b, piece, 1, 1)
    share = combined.reshape((rows,) + TILE_SHAPE + (width // tile_n,)).transpose(1, 2, 0, 3)
    share, (power,) = fold_core(share, (jnp.broadcast_to(power, (width // tile_n,)),), (3,))
    got, power_rows = exchange(share.astype(BF), stack_rows(pieces(power, 3), 8), "zl")
    feats_grad = (LOSS_SCALE / total) * jnp.sum(got.astype(F32), axis=0)
    cross_power = jnp.sum(joined(power_rows[:, 0:3])[:, 0]) / (kt * tile_n)
    return feats_grad, diag_corr, cross_power


def solution(mesh):
    fine = Mesh(mesh.devices.reshape(DP_SHAPE + TILE_SHAPE), DP + TILE)
    in_specs = (P(DP, None), P(DP, None), P(DP, None), P(DP, TILE))
    out_specs = (P(DP, TILE), P(TILE), P())
    return jax.shard_map(
        on_device, mesh=fine, in_specs=in_specs, out_specs=out_specs, check_vma=False
    )
```

```python
import jax
import jax.numpy as jnp
from jax import lax
from jax.sharding import Mesh
from jax.sharding import PartitionSpec as P

GROUPS = 32
LAMBDA_OFF = 0.0051
NORM_EPS = 1e-05
LOSS_SCALE = 65536.0

DP_SHAPE = (2, 4, 8)
TILE_SHAPE = (4, 2)
DP = ("zh", "x", "y")
ROWS = ("x", "zh")
COLS = "y"
TILE = ("zl", "c")
BF = jnp.bfloat16
F32 = jnp.float32


def masked_views(feats, jitter, mask_ids):
    width = feats.shape[1]
    group_size = width // GROUPS
    channel_group = lax.broadcasted_iota(jnp.int32, (1, width), 1) // group_size
    keep_a = (channel_group != mask_ids[:, 0:1]).astype(F32)
    keep_b = (channel_group != mask_ids[:, 1:2]).astype(F32)
    values = feats.astype(F32)
    view_a = (values * keep_a).astype(BF)
    view_b = (values * keep_b + jitter.astype(F32)).astype(BF)
    return view_a, view_b, keep_a, keep_b


def pieces(value, count):
    out = []
    for _ in range(count):
        part = lax.reduce_precision(value, 8, 7)
        out.append(part.astype(BF))
        value = value - part
    return out


def joined(rows):
    total = rows[..., 0, :].astype(F32)
    for i in range(1, rows.shape[-2]):
        total = total + rows[..., i, :].astype(F32)
    return total


def stack_rows(rows, count):
    rows = [jnp.reshape(r, (1, -1)) for r in rows]
    width = rows[0].shape[1]
    if len(rows) < count:
        rows.append(jnp.zeros((count - len(rows), width), BF))
    return jnp.concatenate(rows, axis=0)


def exchange(blocks, extra, axes):
    parts = blocks.shape[0]
    tail = jnp.broadcast_to(extra[None], (parts,) + extra.shape)
    got = lax.all_to_all(jnp.concatenate([blocks, tail], axis=1), axes, 0, 0, tiled=True)
    return got[:, : blocks.shape[1]], got[:, blocks.shape[1] :]


def spread(value, axes):
    parts = lax.axis_size(axes)
    return lax.all_to_all(
        jnp.broadcast_to(value[None], (parts,) + value.shape), axes, 0, 0, tiled=True
    ).reshape((parts * value.shape[0],) + value.shape[1:])


def pick(blocks, at, axis):
    return lax.dynamic_index_in_dim(blocks, at, axis, keepdims=False)


def fold_core(blocks, tail, counts):
    at = lax.axis_index("c")
    own_tail = [pieces(r, n) for r, n in zip(tail, counts)]
    rows, width = blocks.shape[2:]
    sent = pick(blocks, 1 - at, 1).astype(BF).reshape(-1, width)
    sent = jnp.concatenate([sent, stack_rows([p for ps in own_tail for p in ps], 8)], axis=0)
    got = lax.ppermute(sent, "c", [(0, 1), (1, 0)])
    main = pick(blocks, at, 1) + got[: -8].reshape(-1, rows, width).astype(F32)
    out, start = [], got.shape[0] - 8
    for ps in own_tail:
        theirs = joined(got[start : start + len(ps)])
        out.append(joined(jnp.stack(ps)) + theirs)
        start += len(ps)
    return main, out


def fold_line(blocks, tail, counts):
    at = lax.axis_index("zl")
    n = blocks.shape[0]
    rows = blocks.shape[1]
    tail_rows = stack_rows([p for r, k in zip(tail, counts) for p in pieces(r, k)], 8)
    main, out = pick(blocks, at, 0), list(tail)
    for step in range(1, n):
        sent = jnp.concatenate([pick(blocks, at ^ step, 0).astype(BF), tail_rows], axis=0)
        got = lax.ppermute(sent, "zl", [(i, i ^ step) for i in range(n)])
        main = main + got[:rows].astype(F32)
        start = rows
        for i, k in enumerate(counts):
            out[i] = out[i] + joined(got[start : start + k])
            start += k
    return main, out


def swap_pairs():
    rows_n = DP_SHAPE[0] * DP_SHAPE[1]
    n = DP_SHAPE[2]
    where = lambda r, y, t: (r * n + y) * n + t
    return [
        (where(r, y, t), where(r, t, y)) for r in range(rows_n) for y in range(n) for t in range(n)
    ]


def dot(a, b, ca, cb):
    return lax.dot_general(a, b, (((ca,), (cb,)), ((), ())), preferred_element_type=F32)


def on_device(feats, jitter, mask_ids, weight):
    view_a, view_b, keep_a, keep_b = masked_views(feats, jitter, mask_ids)
    rows, width = feats.shape
    kt = weight.shape[1]
    zh_n, x_n, y_n = DP_SHAPE
    rows_n = zh_n * x_n
    tile_n = TILE_SHAPE[0] * TILE_SHAPE[1]
    total = rows * rows_n * y_n
    block = rows * y_n
    sub = kt // rows_n
    all_axes = DP + TILE
    pairs = swap_pairs()

    piece = lax.all_gather(weight, "zh", axis=0, tiled=True)
    piece = spread(spread(piece, "y"), "x")
    piece = piece.reshape(x_n, y_n, zh_n, -1, kt).transpose(2, 0, 1, 3, 4).reshape(width, kt)

    raw = dot(jnp.concatenate([view_a, view_b], axis=0), piece, 1, 0).astype(BF)
    raw_a, raw_b = raw[:rows], raw[rows:]

    own_b = lax.ppermute(raw_b, all_axes, pairs)
    big_a = spread(raw_a, COLS).astype(F32)
    big_b = lax.all_gather(own_b, TILE, axis=0, tiled=True).astype(F32)

    part_mean_a = jnp.mean(big_a, axis=0)
    part_mean_b = jnp.mean(big_b, axis=0)
    mid_a = big_a - part_mean_a
    mid_b = big_b - part_mean_b
    square_a = jnp.sum(mid_a * mid_a, axis=0)
    square_b = jnp.sum(mid_b * mid_b, axis=0)
    cross = jnp.sum(mid_a * mid_b, axis=0)
    gram = dot(mid_a.astype(BF), mid_b.astype(BF), 0, 0).astype(BF)

    stats = [part_mean_a, square_a, part_mean_b, square_b, cross]
    stat_rows = stack_rows([p for s in stats for p in pieces(s, 3)], 16)
    got, got_stats = exchange(gram.reshape(x_n, zh_n * sub, kt), stat_rows, "x")
    got = jnp.sum(got.astype(F32), axis=0).astype(BF).reshape(zh_n, sub, kt)
    got, got_stats = exchange(got, got_stats.reshape(-1, kt), "zh")
    got_stats = got_stats.reshape(rows_n, 16, kt)
    means_a, squares_a, means_b, squares_b, crosses = (
        joined(got_stats[:, 3 * i : 3 * i + 3]) for i in range(5)
    )

    def moments(means, squares):
        mean = jnp.mean(means, axis=0)
        off = means - mean
        var = (jnp.sum(squares, axis=0) + block * jnp.sum(off * off, axis=0)) / total
        return mean, off, lax.rsqrt(var + NORM_EPS)

    mean_a, off_a, inv_a = moments(means_a, squares_a)
    mean_b, off_b, inv_b = moments(means_b, squares_b)
    cols_at = lax.axis_index(COLS)
    tile_at = lax.axis_index(TILE)
    on_diag = (cols_at == tile_at).astype(F32)
    diag = (jnp.sum(crosses, axis=0) + block * jnp.sum(off_a * off_b, axis=0)) * (
        inv_a * inv_b / total
    )
    coeff = -2.0 * (1.0 - diag) - 2.0 * LAMBDA_OFF * diag

    start = lax.axis_index(ROWS) * sub
    off_a_sub = lax.dynamic_slice_in_dim(off_a, start, sub, 1)
    inv_a_sub = lax.dynamic_slice_in_dim(inv_a, start, sub, 0)
    corr = jnp.sum(got.astype(F32), axis=0) + block * lax.dot_general(
        off_a_sub,
        off_b,
        (((0,), (0,)), ((), ())),
        precision=lax.Precision.HIGHEST,
        preferred_element_type=F32,
    )
    corr = corr * (inv_a_sub[:, None] * inv_b[None, :] / total)
    k_of = lax.broadcasted_iota(jnp.int32, (sub, kt), 0) + start
    l_of = lax.broadcasted_iota(jnp.int32, (sub, kt), 1)
    here = (k_of == l_of) & (cols_at == tile_at)
    mix = jnp.where(here, coeff + 2.0 * LAMBDA_OFF * diag, 2.0 * LAMBDA_OFF * corr)
    mix = spread(lax.all_gather(mix.astype(BF), "zh", axis=0, tiled=True), "x")

    mix32 = mix.astype(F32)
    k_of = lax.broadcasted_iota(jnp.int32, (kt, kt), 0)
    l_of = lax.broadcasted_iota(jnp.int32, (kt, kt), 1)
    here = (k_of == l_of) & (cols_at == tile_at)
    corr = jnp.where(here, diag, mix32 * (0.5 / LAMBDA_OFF))
    product = mix32 * corr
    second_a = jnp.sum(product, axis=1)
    second_b = jnp.sum(product, axis=0)
    power = jnp.sum(corr * corr, axis=1)
    norm_mean_a = block * jnp.sum(off_a, axis=0) * inv_a / total
    norm_mean_b = block * jnp.sum(off_b, axis=0) * inv_b / total
    first_a = jnp.sum(mix32 * norm_mean_b[None, :], axis=1)
    first_b = jnp.sum(mix32 * norm_mean_a[:, None], axis=0)

    norm_a = ((big_a - mean_a) * inv_a).astype(BF)
    norm_b = ((big_b - mean_b) * inv_b).astype(BF)
    grad_a = dot(norm_b, mix, 1, 1).astype(BF)
    grad_b = dot(norm_a, mix, 1, 0)

    grad_b, tail_b = fold_core(
        grad_b.reshape(TILE_SHAPE + (rows, kt)), (second_b, first_b), (3, 2)
    )
    grad_b, (second_b, first_b) = fold_line(grad_b, tail_b, (3, 2))
    own_norm_b = ((own_b.astype(F32) - mean_b) * inv_b).astype(BF).astype(F32)
    dz_b = (inv_b * (grad_b - first_b - own_norm_b * second_b)).astype(BF)
    dz_b = lax.ppermute(dz_b, all_axes, pairs)

    tail_a = stack_rows(
        pieces(second_a, 2) + pieces(power, 2) + pieces(diag * on_diag, 3) + pieces(first_a, 1), 8
    )
    got_a, tail_a = exchange(grad_a.reshape(y_n, rows, kt), tail_a, COLS)
    second_a = jnp.sum(joined(tail_a[:, 0:2]), axis=0)
    power = jnp.sum(joined(tail_a[:, 2:4]))
    diag_corr = jnp.sum(joined(tail_a[:, 4:7]), axis=0)
    first_a = jnp.sum(joined(tail_a[:, 7:8]), axis=0)
    own_norm_a = ((raw_a.astype(F32) - mean_a) * inv_a).astype(BF).astype(F32)
    grad_a = jnp.sum(got_a.astype(F32), axis=0)
    dz_a = (inv_a * (grad_a - first_a - own_norm_a * second_a)).astype(BF)

    combined = keep_a * dot(dz_a, piece, 1, 1) + keep_b * dot(dz_b, piece, 1, 1)
    share = combined.reshape((rows,) + TILE_SHAPE + (width // tile_n,)).transpose(1, 2, 0, 3)
    share, (power,) = fold_core(share, (jnp.broadcast_to(power, (width // tile_n,)),), (3,))
    got, power_rows = exchange(share.astype(BF), stack_rows(pieces(power, 3), 8), "zl")
    feats_grad = (LOSS_SCALE / total) * jnp.sum(got.astype(F32), axis=0)
    cross_power = jnp.sum(joined(power_rows[:, 0:3])[:, 0]) / (kt * tile_n)
    return feats_grad, diag_corr, cross_power


def solution(mesh):
    fine = Mesh(mesh.devices.reshape(DP_SHAPE + TILE_SHAPE), DP + TILE)
    in_specs = (P(DP, None), P(DP, None), P(DP, None), P(DP, TILE))
    out_specs = (P(DP, TILE), P(TILE), P())
    return jax.shard_map(
        on_device, mesh=fine, in_specs=in_specs, out_specs=out_specs, check_vma=False
    )
```

```python
import jax
import jax.numpy as jnp
from jax import lax
from jax.experimental import pallas as pl
from jax.experimental.pallas import tpu as pltpu
from jax.sharding import Mesh
from jax.sharding import PartitionSpec as P

GROUPS = 32
LAMBDA_OFF = 0.0051
NORM_EPS = 1e-05
LOSS_SCALE = 65536.0
INTERPRET = False

DP_SHAPE = (2, 4, 8)
TILE_SHAPE = (4, 2)
DP = ("zh", "x", "y")
TILE = ("zl", "c")
BF = jnp.bfloat16
F32 = jnp.float32
FAR = 1 << 20


def masked_views(feats, jitter, mask_ids):
    width = feats.shape[1]
    group_size = width // GROUPS
    channel_group = lax.broadcasted_iota(jnp.int32, (1, width), 1) // group_size
    keep_a = (channel_group != mask_ids[:, 0:1]).astype(F32)
    keep_b = (channel_group != mask_ids[:, 1:2]).astype(F32)
    values = feats.astype(F32)
    view_a = (values * keep_a).astype(BF)
    view_b = (values * keep_b + jitter.astype(F32)).astype(BF)
    return jnp.concatenate([view_a, view_b], axis=0), keep_a, keep_b


def spread(value, axes):
    parts = lax.axis_size(axes)
    return lax.all_to_all(
        jnp.broadcast_to(value[None], (parts,) + value.shape), axes, 0, 0, tiled=True
    )


def shift(value, axis, step):
    n = lax.axis_size(axis)
    return lax.ppermute(value, axis, [(i, (i + step) % n) for i in range(n)])


def flip(value, axis, step):
    n = lax.axis_size(axis)
    return lax.ppermute(value, axis, [(i, i ^ step) for i in range(n)])


def swap_pairs():
    rows_n = DP_SHAPE[0] * DP_SHAPE[1]
    n = DP_SHAPE[2]
    where = lambda r, y, t: (r * n + y) * n + t
    return [
        (where(r, y, t), where(r, t, y)) for r in range(rows_n) for y in range(n) for t in range(n)
    ]


def dot(a, b, ca, cb, precision=None):
    return lax.dot_general(
        a, b, (((ca,), (cb,)), ((), ())), precision=precision, preferred_element_type=F32
    )


def exact(a, b, ca, cb):
    return dot(a, b, ca, cb, lax.Precision.HIGHEST)


def put_pieces(ref, at, value, count):
    for i in range(count):
        part = value.astype(BF).astype(F32)
        ref[at + i : at + i + 1, :] = part
        value = value - part
    return at + count


def joined(rows, at, count):
    total = rows[at : at + 1]
    for i in range(1, count):
        total = total + rows[at + i : at + i + 1]
    return total


def call(body, name, outs, args, scratch=()):
    specs = [
        pl.BlockSpec(memory_space=pltpu.SMEM if a.dtype == jnp.int32 and a.ndim == 1 else pltpu.VMEM)
        for a in args
    ]
    return pl.pallas_call(
        body,
        name=name,
        out_shape=[jax.ShapeDtypeStruct(s, d) for s, d in outs],
        in_specs=specs,
        out_specs=[pl.BlockSpec(memory_space=pltpu.VMEM) for _ in outs],
        scratch_shapes=[pltpu.VMEM(s, d) for s, d in scratch],
        interpret=INTERPRET,
    )(*args)


def project_body(at, view, own, back, ahead, far_low, far_high, piece, wide_a, raw_b):
    zh_n, x_n, y_n, rows, kt = piece.shape
    x = at[0]
    half = y_n // 2
    for zh in range(zh_n):
        piece[zh, x] = own[:, zh]
        piece[zh, lax.rem(x + x_n - 1, x_n)] = back[:, zh]
        piece[zh, lax.rem(x + 1, x_n)] = ahead[:, zh]
        far = lax.rem(x + 2, x_n)
        piece[zh, far, :half] = far_low[:, zh]
        piece[zh, far, half:] = far_high[:, zh]
    weight = piece[...].reshape(zh_n * x_n * y_n * rows, kt)
    raw = dot(view[...], weight, 1, 0).astype(BF)
    n = raw_b.shape[0]
    for i in range(wide_a.shape[0]):
        wide_a[i] = raw[:n]
    raw_b[...] = raw[n:]


def gram_body(at, big_a, pair0, pair1, pair2, pair3, big_b, out, tail):
    zl, c = at[1], at[2]
    parts, rows, kt = big_a.shape
    block = parts * rows
    for step, pair in enumerate((pair0, pair1, pair2, pair3)):
        big_b[(zl ^ step) * 2 + c] = pair[0]
        big_b[(zl ^ step) * 2 + (1 - c)] = pair[1]
    a = big_a[...].reshape(block, kt).astype(F32)
    b = big_b[...].reshape(block, kt).astype(F32)
    mean_a = jnp.sum(a, axis=0, keepdims=True) / block
    mean_b = jnp.sum(b, axis=0, keepdims=True) / block
    a = a - mean_a
    b = b - mean_b
    gram = dot(a.astype(BF), b.astype(BF), 0, 0).astype(BF)
    tail[...] = jnp.zeros_like(tail)
    pos = put_pieces(tail, 0, mean_a, 3)
    pos = put_pieces(tail, pos, jnp.sum(a * a, axis=0, keepdims=True), 3)
    pos = put_pieces(tail, pos, mean_b, 3)
    pos = put_pieces(tail, pos, jnp.sum(b * b, axis=0, keepdims=True), 3)
    put_pieces(tail, pos, jnp.sum(a * b, axis=0, keepdims=True), 3)
    x_n = out.shape[0]
    deep = out.shape[1] - 16
    rows_out = tail[...].astype(BF)
    for x in range(x_n):
        out[x, :deep] = gram[x * deep : (x + 1) * deep]
        out[x, deep:] = rows_out


def merge_body(got, out):
    x_n = got.shape[0]
    zh_n, deep, kt = out.shape
    sub = deep - 16 * x_n
    for zh in range(zh_n):
        total = got[0, zh * sub : (zh + 1) * sub].astype(F32)
        for x in range(1, x_n):
            total = total + got[x, zh * sub : (zh + 1) * sub].astype(F32)
        out[zh, :sub] = total.astype(BF)
        for x in range(x_n):
            out[zh, sub + 16 * x : sub + 16 * (x + 1)] = got[x, zh_n * sub :]


def mix_body(at, got, mix, stats, table, offs, *, block):
    zh_n, deep, kt = got.shape
    sub = mix.shape[0]
    sets = zh_n * ((deep - sub) // 16)
    total = block * sets
    raws = []
    for zh in range(zh_n):
        for x in range((deep - sub) // 16):
            rows = got[zh, sub + 16 * x : sub + 16 * (x + 1)].astype(F32)
            raws.append([joined(rows, 3 * i, 3) for i in range(5)])
    summed = [sum(r[i] for r in raws[1:]) + raws[0][i] for i in range(5)]
    mean_a, mean_b = summed[0] / sets, summed[2] / sets
    square_a, square_b, cross = summed[1], summed[3], summed[4]
    drift_a = jnp.zeros_like(mean_a)
    drift_b = jnp.zeros_like(mean_b)
    table[...] = jnp.zeros_like(table)
    for i, r in enumerate(raws):
        off_a, off_b = r[0] - mean_a, r[2] - mean_b
        square_a = square_a + block * off_a * off_a
        square_b = square_b + block * off_b * off_b
        cross = cross + block * off_a * off_b
        drift_a, drift_b = drift_a + off_a, drift_b + off_b
        table[i : i + 1, :] = off_a
        offs[i : i + 1, :] = block * off_b
    inv_a = lax.rsqrt(square_a / total + NORM_EPS)
    inv_b = lax.rsqrt(square_b / total + NORM_EPS)
    table[sets : sets + 1, :] = inv_a
    diag = cross * (inv_a * inv_b / total)
    coeff = -2.0 * (1.0 - diag) - 2.0 * LAMBDA_OFF * diag
    k_of = lax.broadcasted_iota(jnp.int32, (sub, kt), 0)
    l_of = lax.broadcasted_iota(jnp.int32, (sub, kt), 1)
    chosen = exact((k_of + at[3] == l_of).astype(F32), table[...], 1, 1)
    corr = got[0, :sub].astype(F32)
    for zh in range(1, zh_n):
        corr = corr + got[zh, :sub].astype(F32)
    corr = corr + exact(chosen[:, :sets], offs[...], 1, 0)
    corr = corr * (chosen[:, sets : sets + 1] * (inv_b / total))
    here = k_of + (at[3] + at[4]) == l_of
    mix[...] = jnp.where(
        here, coeff + 2.0 * LAMBDA_OFF * diag, 2.0 * LAMBDA_OFF * corr
    ).astype(BF)
    stats[0:1, :] = mean_a
    stats[1:2, :] = inv_a
    stats[2:3, :] = mean_b
    stats[3:4, :] = inv_b
    stats[4:5, :] = diag
    stats[5:6, :] = drift_a * inv_a / sets
    stats[6:7, :] = drift_b * inv_b / sets
    stats[7:8, :] = diag * (at[4] == 0).astype(F32)


def correlation(at, mix, stats):
    kt = mix.shape[0]
    k_of = lax.broadcasted_iota(jnp.int32, (kt, kt), 0)
    l_of = lax.broadcasted_iota(jnp.int32, (kt, kt), 1)
    return jnp.where(k_of + at[4] == l_of, stats[4:5, :], mix * (0.5 / LAMBDA_OFF))


def grad_b_body(at, mix4, big_a, stats, sent, kept, grads, tail):
    c = at[2]
    parts, rows, kt = big_a.shape
    line = parts // 2
    mix = mix4[...].reshape(kt, kt)
    wide = mix.astype(F32)
    norm_a = (big_a[...].reshape(parts * rows, kt).astype(F32) - stats[0:1, :]) * stats[1:2, :]
    grads[...] = dot(norm_a.astype(BF), mix, 1, 0).reshape(parts, rows, kt)
    for z in range(line):
        sent[z * rows : (z + 1) * rows] = grads[z * 2 + (1 - c)].astype(BF)
        kept[z * rows : (z + 1) * rows] = grads[z * 2 + c]
    second = jnp.sum(wide * correlation(at, wide, stats), axis=0, keepdims=True)
    first = exact(stats[...], wide, 1, 0)[5:6]
    tail[...] = jnp.zeros_like(tail)
    pos = put_pieces(tail, 0, second, 3)
    put_pieces(tail, pos, first, 2)
    sent[line * rows :] = tail[...].astype(BF)
    kept[line * rows :] = jnp.zeros_like(tail)
    kept[line * rows : line * rows + 1] = second
    kept[line * rows + 1 : line * rows + 2] = first


def grad_a_body(at, mix4, big_b, stats, out, tail):
    parts, rows, kt = big_b.shape
    mix = mix4[...].reshape(kt, kt)
    wide = mix.astype(F32)
    norm_b = (big_b[...].reshape(parts * rows, kt).astype(F32) - stats[2:3, :]) * stats[3:4, :]
    grad = dot(norm_b.astype(BF), mix, 1, 1).astype(BF)
    corr = correlation(at, wide, stats)
    ones = jnp.ones((8, kt), F32)
    pos = put_pieces(tail, 0, exact(ones, wide * corr, 1, 1)[0:1], 2)
    pos = put_pieces(tail, pos, exact(ones, corr * corr, 1, 1)[0:1], 2)
    pos = put_pieces(tail, pos, stats[7:8, :], 3)
    put_pieces(tail, pos, exact(stats[...], wide, 1, 1)[6:7], 1)
    rows_out = tail[...].astype(BF)
    for i in range(parts):
        out[i, :rows] = grad[i * rows : (i + 1) * rows]
        out[i, rows:] = rows_out


def core_body(at, kept, got, own, out1, out2, out3, total, tail):
    zl = at[1]
    rows = own.shape[0] - 8
    deep = kept.shape[0] - 8
    total[...] = kept[:deep] + got[:deep].astype(F32)
    theirs = got[deep:].astype(F32)
    second = kept[deep : deep + 1] + joined(theirs, 0, 3)
    first = kept[deep + 1 : deep + 2] + joined(theirs, 3, 2)
    tail[...] = jnp.zeros_like(tail)
    pos = put_pieces(tail, 0, second, 3)
    put_pieces(tail, pos, first, 2)
    rows_out = tail[...].astype(BF)
    start = lambda step: pl.ds(pl.multiple_of((zl ^ step) * rows, rows), rows)
    for step, out in enumerate((out1, out2, out3), 1):
        out[:rows] = total[start(step), :].astype(BF)
        out[rows:] = rows_out
    own[:rows] = total[start(0), :]
    own[rows:] = jnp.zeros_like(tail)
    own[rows : rows + 1] = second
    own[rows + 1 : rows + 2] = first


def dz_b_body(own, got1, got2, got3, raw_b, stats, out):
    rows = out.shape[0]
    grad = own[:rows]
    second, first = own[rows : rows + 1], own[rows + 1 : rows + 2]
    for got in (got1, got2, got3):
        grad = grad + got[:rows].astype(F32)
        theirs = got[rows:].astype(F32)
        second = second + joined(theirs, 0, 3)
        first = first + joined(theirs, 3, 2)
    inv = stats[3:4, :]
    norm = ((raw_b[...].astype(F32) - stats[2:3, :]) * inv).astype(BF).astype(F32)
    out[...] = (inv * (grad - first - norm * second)).astype(BF)


def back_a_body(got, raw_a, stats, keep, weight, out, diag_out, power_out):
    parts, deep, kt = got.shape
    rows = deep - 8
    grad = got[0, :rows].astype(F32)
    tails = [got[i, rows:].astype(F32) for i in range(parts)]
    for i in range(1, parts):
        grad = grad + got[i, :rows].astype(F32)
    gather = lambda pos, count: sum(
        (joined(t, pos, count) for t in tails[1:]), joined(tails[0], pos, count)
    )
    second, power, diag, first = gather(0, 2), gather(2, 2), gather(4, 3), gather(7, 1)
    inv = stats[1:2, :]
    norm = ((raw_a[...].astype(F32) - stats[0:1, :]) * inv).astype(BF).astype(F32)
    dz = (inv * (grad - first - norm * second)).astype(BF)
    width = keep.shape[1]
    out[...] = keep[...] * dot(dz, weight[...].reshape(width, kt), 1, 1)
    diag_out[...] = diag
    power_out[...] = jnp.broadcast_to(jnp.sum(power, axis=1, keepdims=True), power_out.shape)


def back_b_body(at, part, dz, keep, weight, power, sent, kept, blocks, tail):
    c = at[2]
    rows, width = part.shape
    parts, _, chunk = blocks.shape
    line = parts // 2
    both = part[...] + keep[...] * dot(dz[...], weight[...].reshape(width, dz.shape[1]), 1, 1)
    for i in range(parts):
        blocks[i] = both[:, i * chunk : (i + 1) * chunk]
    for z in range(line):
        sent[z * rows : (z + 1) * rows] = blocks[z * 2 + (1 - c)].astype(BF)
        kept[z * rows : (z + 1) * rows] = blocks[z * 2 + c]
    tail[...] = jnp.zeros_like(tail)
    put_pieces(tail, 0, power[...], 3)
    sent[line * rows :] = tail[...].astype(BF)
    kept[line * rows :] = tail[...]


def last_body(kept, got, out, tail):
    line, deep, chunk = out.shape
    rows = deep - 8
    theirs = got[line * rows :].astype(F32)
    power = joined(kept[line * rows :], 0, 3) + joined(theirs, 0, 3)
    tail[...] = jnp.zeros_like(tail)
    put_pieces(tail, 0, power, 3)
    rows_out = tail[...].astype(BF)
    for z in range(line):
        at = slice(z * rows, (z + 1) * rows)
        out[z, :rows] = (kept[at] + got[at].astype(F32)).astype(BF)
        out[z, rows:] = rows_out


def end_body(got, out, power_out, *, scale, features):
    line, deep, _ = got.shape
    rows = deep - 8
    total = got[0, :rows].astype(F32)
    power = joined(got[0, rows:].astype(F32), 0, 3)
    for z in range(1, line):
        total = total + got[z, :rows].astype(F32)
        power = power + joined(got[z, rows:].astype(F32), 0, 3)
    out[...] = scale * total
    power_out[...] = power / features


def on_device(feats, jitter, mask_ids, weight):
    rows, width = feats.shape
    w_rows, kt = weight.shape
    zh_n, x_n, y_n = DP_SHAPE
    zl_n, c_n = TILE_SHAPE
    rows_n = zh_n * x_n
    tile_n = zl_n * c_n
    total = rows * rows_n * y_n
    block = rows * y_n
    sub = kt // rows_n
    chunk = width // tile_n
    every = DP + TILE
    pairs = swap_pairs()

    y_at = lax.axis_index("y")
    tile_at = lax.axis_index(TILE)
    at = jnp.stack(
        [
            lax.axis_index("x"),
            lax.axis_index("zl"),
            lax.axis_index("c"),
            lax.axis_index(("x", "zh")) * sub,
            jnp.where(y_at == tile_at, 0, FAR),
        ]
    ).astype(jnp.int32)
    view, keep_a, keep_b = masked_views(feats, jitter, mask_ids)

    own = lax.all_gather(weight, "zh", axis=0, tiled=True)
    own = spread(own, "y").reshape(y_n, zh_n, w_rows, kt)
    half = y_n // 2
    back = shift(own, "x", 1)
    ahead = shift(own, "x", x_n - 1)
    far_low = shift(back[:half], "x", 1)
    far_high = shift(ahead[half:], "x", x_n - 1)
    piece, wide_a, raw_b = call(
        project_body,
        "project",
        [((zh_n, x_n, y_n, w_rows, kt), BF), ((y_n, rows, kt), BF), ((rows, kt), BF)],
        (at, view, own, back, ahead, far_low, far_high),
    )

    raw_a = wide_a[0]
    big_a = lax.all_to_all(wide_a, "y", 0, 0, tiled=True)
    own_b = lax.ppermute(raw_b, every, pairs)
    pair = jnp.stack([own_b, flip(own_b, "c", 1)])
    others = [flip(pair, "zl", step) for step in range(1, zl_n)]
    big_b, gram = call(
        gram_body,
        "gram",
        [((tile_n, rows, kt), BF), ((x_n, zh_n * sub + 16, kt), BF)],
        (at, big_a, pair, *others),
        [((16, kt), F32)],
    )

    got = lax.all_to_all(gram, "x", 0, 0, tiled=True)
    (got,) = call(merge_body, "merge", [((zh_n, sub + 16 * x_n, kt), BF)], (got,))
    got = lax.all_to_all(got, "zh", 0, 0, tiled=True)
    mix, stats = call(
        lambda *refs: mix_body(*refs, block=block),
        "mix",
        [((sub, kt), BF), ((8, kt), F32)],
        (at, got),
        [((16, kt), F32), ((rows_n, kt), F32)],
    )
    mix = spread(lax.all_gather(mix, "zh", axis=0, tiled=True), "x")

    line_rows = zl_n * rows + 8
    sent, kept = call(
        grad_b_body,
        "grad_b",
        [((line_rows, kt), BF), ((line_rows, kt), F32)],
        (at, mix, big_a, stats),
        [((tile_n, rows, kt), F32), ((8, kt), F32)],
    )
    got_b = flip(sent, "c", 1)
    (grad_a,) = call(
        grad_a_body, "grad_a", [((y_n, rows + 8, kt), BF)], (at, mix, big_b, stats), [((8, kt), F32)]
    )
    got_a = lax.all_to_all(grad_a, "y", 0, 0, tiled=True)
    own, *outs = call(
        core_body,
        "core",
        [((rows + 8, kt), F32)] + [((rows + 8, kt), BF)] * 3,
        (at, kept, got_b),
        [((zl_n * rows, kt), F32), ((8, kt), F32)],
    )
    gots = [flip(o, "zl", step) for step, o in enumerate(outs, 1)]
    (dz_b,) = call(dz_b_body, "dz_b", [((rows, kt), BF)], (own, *gots, own_b, stats))
    dz_b = lax.ppermute(dz_b, every, pairs)
    part, diag_corr, power = call(
        back_a_body,
        "back_a",
        [((rows, width), F32), ((1, kt), F32), ((1, chunk), F32)],
        (got_a, raw_a, stats, keep_a, piece),
    )
    sent, kept = call(
        back_b_body,
        "back_b",
        [((line_rows, chunk), BF), ((line_rows, chunk), F32)],
        (at, part, dz_b, keep_b, piece, power),
        [((tile_n, rows, chunk), F32), ((8, chunk), F32)],
    )
    (share,) = call(
        last_body,
        "last",
        [((zl_n, rows + 8, chunk), BF)],
        (kept, flip(sent, "c", 1)),
        [((8, chunk), F32)],
    )
    got = lax.all_to_all(share, "zl", 0, 0, tiled=True)
    feats_grad, cross_power = call(
        lambda *refs: end_body(*refs, scale=LOSS_SCALE / total, features=kt * tile_n),
        "end",
        [((rows, chunk), F32), ((1, chunk), F32)],
        (got,),
    )
    return feats_grad, diag_corr[0], cross_power[0, 0]


def solution(mesh):
    fine = Mesh(mesh.devices.reshape(DP_SHAPE + TILE_SHAPE), DP + TILE)
    in_specs = (P(DP, None), P(DP, None), P(DP, None), P(DP, TILE))
    out_specs = (P(DP, TILE), P(TILE), P())
    return jax.shard_map(
        on_device, mesh=fine, in_specs=in_specs, out_specs=out_specs, check_vma=False
    )
```

```python
import jax
import jax.numpy as jnp
from jax import lax
from jax.experimental import pallas as pl
from jax.experimental.pallas import tpu as pltpu
from jax.sharding import Mesh
from jax.sharding import PartitionSpec as P

GROUPS = 32
LAMBDA_OFF = 0.0051
NORM_EPS = 1e-05
LOSS_SCALE = 65536.0
INTERPRET = False

DP_SHAPE = (2, 4, 8)
TILE_SHAPE = (4, 2)
DP = ("zh", "x", "y")
TILE = ("zl", "c")
BF = jnp.bfloat16
F32 = jnp.float32
FAR = 1 << 20


def masked_views(feats, jitter, mask_ids):
    width = feats.shape[1]
    group_size = width // GROUPS
    channel_group = lax.broadcasted_iota(jnp.int32, (1, width), 1) // group_size
    keep_a = (channel_group != mask_ids[:, 0:1]).astype(F32)
    keep_b = (channel_group != mask_ids[:, 1:2]).astype(F32)
    values = feats.astype(F32)
    view_a = (values * keep_a).astype(BF)
    view_b = (values * keep_b + jitter.astype(F32)).astype(BF)
    return jnp.concatenate([view_a, view_b], axis=0), keep_a, keep_b


def spread(value, axes):
    parts = lax.axis_size(axes)
    return lax.all_to_all(
        jnp.broadcast_to(value[None], (parts,) + value.shape), axes, 0, 0, tiled=True
    )


def shift(value, axis, step):
    n = lax.axis_size(axis)
    return lax.ppermute(value, axis, [(i, (i + step) % n) for i in range(n)])


def flip(value, axis, step):
    n = lax.axis_size(axis)
    return lax.ppermute(value, axis, [(i, i ^ step) for i in range(n)])


def swap_pairs(other):
    zh_n, x_n, n = DP_SHAPE
    where = lambda zh, x, y, t: ((zh * x_n + x) * n + y) * n + t
    return [
        (where(zh, x, y, t), where(zh ^ other, x, t, y))
        for zh in range(zh_n)
        for x in range(x_n)
        for y in range(n)
        for t in range(n)
    ]


def dot(a, b, ca, cb, precision=None):
    return lax.dot_general(
        a, b, (((ca,), (cb,)), ((), ())), precision=precision, preferred_element_type=F32
    )


def exact(a, b, ca, cb):
    return dot(a, b, ca, cb, lax.Precision.HIGHEST)


def put_pieces(ref, at, value, count):
    for i in range(count):
        part = value.astype(BF).astype(F32)
        ref[at + i : at + i + 1, :] = part
        value = value - part
    return at + count


def joined(rows, at, count):
    total = rows[at : at + 1]
    for i in range(1, count):
        total = total + rows[at + i : at + i + 1]
    return total


def call(body, name, outs, args, scratch=()):
    specs = [
        pl.BlockSpec(memory_space=pltpu.SMEM if a.dtype == jnp.int32 and a.ndim == 1 else pltpu.VMEM)
        for a in args
    ]
    return pl.pallas_call(
        body,
        name=name,
        out_shape=[jax.ShapeDtypeStruct(s, d) for s, d in outs],
        in_specs=specs,
        out_specs=[pl.BlockSpec(memory_space=pltpu.VMEM) for _ in outs],
        scratch_shapes=[pltpu.VMEM(s, d) for s, d in scratch],
        interpret=INTERPRET,
    )(*args)


def project_body(at, view, own, back, ahead, far_low, far_high, piece, wide_a, same_b, other_b):
    zh_n, x_n, y_n, rows, kt = piece.shape
    x = at[0]
    half = y_n // 2
    for zh in range(zh_n):
        piece[zh, x] = own[:, zh]
        piece[zh, lax.rem(x + x_n - 1, x_n)] = back[:, zh]
        piece[zh, lax.rem(x + 1, x_n)] = ahead[:, zh]
        far = lax.rem(x + 2, x_n)
        piece[zh, far, :half] = far_low[:, zh]
        piece[zh, far, half:] = far_high[:, zh]
    weight = piece[...].reshape(zh_n * x_n * y_n * rows, kt)
    raw = dot(view[...], weight, 1, 0).astype(BF)
    n, half_kt = same_b.shape
    for i in range(wide_a.shape[0]):
        wide_a[i] = raw[:n]
    low, high = raw[n:, :half_kt], raw[n:, half_kt:]
    first = at[5] == 0
    same_b[...] = jnp.where(first, low, high)
    other_b[...] = jnp.where(first, high, low)


def gram_body(at, big_a, big_b, out, tail):
    parts, rows, kt = big_a.shape
    block = parts * rows
    kl = big_b.shape[2]
    a = big_a[...].reshape(block, kt).astype(F32)
    b = big_b[...].reshape(block, kl).astype(F32)
    mean_a = jnp.sum(a, axis=0, keepdims=True) / block
    mean_b = jnp.sum(b, axis=0, keepdims=True) / block
    a = a - mean_a
    b = b - mean_b
    gram = dot(a.astype(BF), b.astype(BF), 0, 0).astype(BF)
    square_a = jnp.sum(a * a, axis=0, keepdims=True)
    facing = jnp.where(at[5] == 0, a[:, :kl], a[:, kl:])
    tail[...] = jnp.zeros_like(tail)
    pos = 0
    for row in (
        mean_a[:, :kl],
        mean_a[:, kl:],
        square_a[:, :kl],
        square_a[:, kl:],
        mean_b,
        jnp.sum(b * b, axis=0, keepdims=True),
        jnp.sum(facing * b, axis=0, keepdims=True),
    ):
        pos = put_pieces(tail, pos, row, 3)
    deep = out.shape[1] - tail.shape[0]
    rows_out = tail[...].astype(BF)
    for x in range(out.shape[0]):
        out[x, :deep] = gram[x * deep : (x + 1) * deep]
        out[x, deep:] = rows_out


def mix_body(at, got, mix, stats_a, stats_b, table, offs, *, block):
    sets, deep, kl = got.shape
    sub = mix.shape[0]
    kt = stats_a.shape[1]
    total = block * sets
    raws = []
    for x in range(sets):
        rows = got[x, sub:].astype(F32)
        r = [joined(rows, 3 * i, 3) for i in range(7)]
        wide = lambda i: jnp.concatenate([r[i], r[i + 1]], axis=1)
        raws.append((wide(0), wide(2), r[4], r[5], r[6]))
    summed = [sum((r[i] for r in raws[1:]), raws[0][i]) for i in range(5)]
    mean_a, mean_b = summed[0] / sets, summed[2] / sets
    square_a, square_b, cross = summed[1], summed[3], summed[4]
    drift_a = jnp.zeros_like(mean_a)
    drift_b = jnp.zeros_like(mean_b)
    first = at[5] == 0
    facing = lambda row: jnp.where(first, row[:, :kl], row[:, kl:])
    table[...] = jnp.zeros_like(table)
    offs[...] = jnp.zeros_like(offs)
    for i, r in enumerate(raws):
        off_a, off_b = r[0] - mean_a, r[2] - mean_b
        square_a = square_a + block * off_a * off_a
        square_b = square_b + block * off_b * off_b
        cross = cross + block * facing(off_a) * off_b
        drift_a, drift_b = drift_a + off_a, drift_b + off_b
        table[i : i + 1, :] = off_a
        offs[i : i + 1, :] = block * off_b
    inv_a = lax.rsqrt(square_a / total + NORM_EPS)
    inv_b = lax.rsqrt(square_b / total + NORM_EPS)
    table[sets : sets + 1, :] = inv_a
    diag = cross * (facing(inv_a) * inv_b / total)
    coeff = -2.0 * (1.0 - diag) - 2.0 * LAMBDA_OFF * diag
    k_of = lax.broadcasted_iota(jnp.int32, (sub, kt), 0)
    l_of = lax.broadcasted_iota(jnp.int32, (sub, kt), 1)
    chosen = exact((k_of + at[3] == l_of).astype(F32), table[...], 1, 1)
    corr = got[0, :sub].astype(F32)
    for x in range(1, sets):
        corr = corr + got[x, :sub].astype(F32)
    corr = corr + exact(chosen, offs[...], 1, 0)
    corr = corr * (chosen[:, sets : sets + 1] * (inv_b / total))
    k_of = lax.broadcasted_iota(jnp.int32, (sub, kl), 0)
    l_of = lax.broadcasted_iota(jnp.int32, (sub, kl), 1)
    here = k_of + at[3] == l_of + at[4]
    mix[...] = jnp.where(
        here, coeff + 2.0 * LAMBDA_OFF * diag, 2.0 * LAMBDA_OFF * corr
    ).astype(BF)
    held = diag * (at[4] != FAR).astype(F32)
    none = jnp.zeros_like(held)
    stats_a[...] = jnp.zeros_like(stats_a)
    stats_b[...] = jnp.zeros_like(stats_b)
    stats_a[0:1, :] = mean_a
    stats_a[1:2, :] = inv_a
    stats_a[2:3, :] = drift_a * inv_a / sets
    stats_a[3:4, :kl] = jnp.where(first, held, none)
    stats_a[3:4, kl:] = jnp.where(first, none, held)
    stats_b[0:1, :] = mean_b
    stats_b[1:2, :] = inv_b
    stats_b[2:3, :] = drift_b * inv_b / sets
    stats_b[3:4, :] = diag


def correlation(at, mix, stats_b):
    k_of = lax.broadcasted_iota(jnp.int32, mix.shape, 0)
    l_of = lax.broadcasted_iota(jnp.int32, mix.shape, 1)
    return jnp.where(k_of == l_of + at[4], stats_b[3:4, :], mix * (0.5 / LAMBDA_OFF))


def grad_b_body(at, mix4, big_a, stats_a, stats_b, sent, kept, grads, tail):
    c = at[2]
    parts, rows, kl = grads.shape
    kt = big_a.shape[2]
    line = parts // 2
    mix = mix4[...].reshape(kt, kl)
    wide = mix.astype(F32)
    norm_a = (big_a[...].reshape(parts * rows, kt).astype(F32) - stats_a[0:1, :]) * stats_a[1:2, :]
    grads[...] = dot(norm_a.astype(BF), mix, 1, 0).reshape(parts, rows, kl)
    for z in range(line):
        sent[z * rows : (z + 1) * rows] = grads[z * 2 + (1 - c)].astype(BF)
        kept[z * rows : (z + 1) * rows] = grads[z * 2 + c]
    second = jnp.sum(wide * correlation(at, wide, stats_b), axis=0, keepdims=True)
    first = exact(stats_a[...], wide, 1, 0)[2:3]
    tail[...] = jnp.zeros_like(tail)
    pos = put_pieces(tail, 0, second, 3)
    put_pieces(tail, pos, first, 2)
    sent[line * rows :] = tail[...].astype(BF)
    kept[line * rows :] = jnp.zeros_like(tail)
    kept[line * rows : line * rows + 1] = second
    kept[line * rows + 1 : line * rows + 2] = first


def grad_a_body(at, mix4, big_b, stats_a, stats_b, out, tail):
    parts, deep, kt = out.shape
    rows = deep - 8
    kl = big_b.shape[2]
    mix = mix4[...].reshape(kt, kl)
    wide = mix.astype(F32)
    norm_b = (big_b[...].reshape(parts * rows, kl).astype(F32) - stats_b[0:1, :]) * stats_b[1:2, :]
    grad = dot(norm_b.astype(BF), mix, 1, 1).astype(BF)
    corr = correlation(at, wide, stats_b)
    ones = jnp.ones((8, kl), F32)
    pos = put_pieces(tail, 0, exact(ones, wide * corr, 1, 1)[0:1], 2)
    pos = put_pieces(tail, pos, exact(ones, corr * corr, 1, 1)[0:1], 2)
    pos = put_pieces(tail, pos, stats_a[3:4, :], 3)
    put_pieces(tail, pos, exact(stats_b[...], wide, 1, 1)[2:3], 1)
    rows_out = tail[...].astype(BF)
    for i in range(parts):
        out[i, :rows] = grad[i * rows : (i + 1) * rows]
        out[i, rows:] = rows_out


def core_body(at, kept, got, own, out1, out2, out3, total, tail):
    zl = at[1]
    rows = own.shape[0] - 8
    deep = kept.shape[0] - 8
    total[...] = kept[:deep] + got[:deep].astype(F32)
    theirs = got[deep:].astype(F32)
    second = kept[deep : deep + 1] + joined(theirs, 0, 3)
    first = kept[deep + 1 : deep + 2] + joined(theirs, 3, 2)
    tail[...] = jnp.zeros_like(tail)
    pos = put_pieces(tail, 0, second, 3)
    put_pieces(tail, pos, first, 2)
    rows_out = tail[...].astype(BF)
    start = lambda step: pl.ds(pl.multiple_of((zl ^ step) * rows, rows), rows)
    for step, out in enumerate((out1, out2, out3), 1):
        out[:rows] = total[start(step), :].astype(BF)
        out[rows:] = rows_out
    own[:rows] = total[start(0), :]
    own[rows:] = jnp.zeros_like(tail)
    own[rows : rows + 1] = second
    own[rows + 1 : rows + 2] = first


def dz_b_body(at, own, got1, got2, got3, raw_b, stats_b, same, other, both):
    deep = both.shape[0]
    rows = same.shape[0]
    grad = own[:deep]
    second, first = own[deep : deep + 1], own[deep + 1 : deep + 2]
    for got in (got1, got2, got3):
        grad = grad + got[:deep].astype(F32)
        theirs = got[deep:].astype(F32)
        second = second + joined(theirs, 0, 3)
        first = first + joined(theirs, 3, 2)
    inv = stats_b[1:2, :]
    norm = ((raw_b[...].astype(F32) - stats_b[0:1, :]) * inv).astype(BF).astype(F32)
    both = (inv * (grad - first - norm * second)).astype(BF)
    low = at[5] == 0
    same[...] = jnp.where(low, both[:rows], both[rows:])
    other[...] = jnp.where(low, both[rows:], both[:rows])


def back_a_body(got, raw_a, stats_a, keep, weight, out, diag_out, power_out):
    parts, deep, kt = got.shape
    rows = deep - 8
    grad = got[0, :rows].astype(F32)
    tails = [got[i, rows:].astype(F32) for i in range(parts)]
    for i in range(1, parts):
        grad = grad + got[i, :rows].astype(F32)
    gather = lambda pos, count: sum(
        (joined(t, pos, count) for t in tails[1:]), joined(tails[0], pos, count)
    )
    second, power, diag, first = gather(0, 2), gather(2, 2), gather(4, 3), gather(7, 1)
    inv = stats_a[1:2, :]
    norm = ((raw_a[...].astype(F32) - stats_a[0:1, :]) * inv).astype(BF).astype(F32)
    dz = (inv * (grad - first - norm * second)).astype(BF)
    width = keep.shape[1]
    out[...] = keep[...] * dot(dz, weight[...].reshape(width, kt), 1, 1)
    diag_out[...] = diag
    power_out[...] = jnp.broadcast_to(jnp.sum(power, axis=1, keepdims=True), power_out.shape)


def back_b_body(at, part, same, other, keep, weight, power, out, tail):
    rows, width = part.shape
    parts, _, chunk = out.shape
    low = at[5] == 0
    dz = jnp.concatenate(
        [jnp.where(low, same[...], other[...]), jnp.where(low, other[...], same[...])], axis=1
    )
    both = part[...] + keep[...] * dot(dz, weight[...].reshape(width, dz.shape[1]), 1, 1)
    both = both.astype(BF)
    tail[...] = jnp.zeros_like(tail)
    put_pieces(tail, 0, power[...], 3)
    rows_out = tail[...].astype(BF)
    for i in range(parts):
        out[i, :rows] = both[:, i * chunk : (i + 1) * chunk]
        out[i, rows:] = rows_out


def end_body(got, out, power_out, *, scale, features):
    line, deep, _ = got.shape
    rows = deep - 8
    total = got[0, :rows].astype(F32)
    power = joined(got[0, rows:].astype(F32), 0, 3)
    for z in range(1, line):
        total = total + got[z, :rows].astype(F32)
        power = power + joined(got[z, rows:].astype(F32), 0, 3)
    out[...] = scale * total
    power_out[...] = power / features


def on_device(feats, jitter, mask_ids, weight):
    rows, width = feats.shape
    w_rows, kt = weight.shape
    zh_n, x_n, y_n = DP_SHAPE
    zl_n, c_n = TILE_SHAPE
    tile_n = zl_n * c_n
    parts = y_n * zh_n
    block = rows * parts
    total = block * x_n
    sub = kt // x_n
    kl = kt // zh_n
    chunk = width // tile_n
    every = DP + TILE
    zh_at = lax.axis_index("zh")
    at = jnp.stack(
        [
            lax.axis_index("x"),
            lax.axis_index("zl"),
            lax.axis_index("c"),
            lax.axis_index("x") * sub,
            jnp.where(lax.axis_index("y") == lax.axis_index(TILE), zh_at * kl, FAR),
            zh_at,
        ]
    ).astype(jnp.int32)
    view, keep_a, keep_b = masked_views(feats, jitter, mask_ids)

    own = lax.all_gather(weight, "zh", axis=0, tiled=True)
    own = spread(own, "y").reshape(y_n, zh_n, w_rows, kt)
    half = y_n // 2
    back = shift(own, "x", 1)
    ahead = shift(own, "x", x_n - 1)
    far_low = shift(back[:half], "x", 1)
    far_high = shift(ahead[half:], "x", x_n - 1)
    piece, wide_a, same_b, other_b = call(
        project_body,
        "project",
        [
            ((zh_n, x_n, y_n, w_rows, kt), BF),
            ((parts, rows, kt), BF),
            ((rows, kl), BF),
            ((rows, kl), BF),
        ],
        (at, view, own, back, ahead, far_low, far_high),
    )

    raw_a = wide_a[0]
    big_a = lax.all_to_all(wide_a, ("y", "zh"), 0, 0, tiled=True)
    same_b = lax.ppermute(same_b, every, swap_pairs(0))
    other_b = lax.ppermute(other_b, every, swap_pairs(1))
    own_b = jnp.concatenate(
        [jnp.where(zh_at == 0, same_b, other_b), jnp.where(zh_at == 0, other_b, same_b)], axis=0
    )
    big_b = lax.all_gather(own_b, TILE, axis=0)
    (gram,) = call(
        gram_body, "gram", [((x_n, sub + 32, kl), BF)], (at, big_a, big_b), [((32, kl), F32)]
    )

    got = lax.all_to_all(gram, "x", 0, 0, tiled=True)
    mix, stats_a, stats_b = call(
        lambda *refs: mix_body(*refs, block=block),
        "mix",
        [((sub, kl), BF), ((8, kt), F32), ((8, kl), F32)],
        (at, got),
        [((8, kt), F32), ((8, kl), F32)],
    )
    mix = spread(mix, "x")

    b_rows = rows * zh_n
    line_rows = zl_n * b_rows + 8
    sent, kept = call(
        grad_b_body,
        "grad_b",
        [((line_rows, kl), BF), ((line_rows, kl), F32)],
        (at, mix, big_a, stats_a, stats_b),
        [((tile_n, b_rows, kl), F32), ((8, kl), F32)],
    )
    got_b = flip(sent, "c", 1)
    (grad_a,) = call(
        grad_a_body,
        "grad_a",
        [((parts, rows + 8, kt), BF)],
        (at, mix, big_b, stats_a, stats_b),
        [((8, kt), F32)],
    )
    got_a = lax.all_to_all(grad_a, ("y", "zh"), 0, 0, tiled=True)
    own, *outs = call(
        core_body,
        "core",
        [((b_rows + 8, kl), F32)] + [((b_rows + 8, kl), BF)] * 3,
        (at, kept, got_b),
        [((zl_n * b_rows, kl), F32), ((8, kl), F32)],
    )
    gots = [flip(o, "zl", step) for step, o in enumerate(outs, 1)]
    same_b, other_b = call(
        dz_b_body,
        "dz_b",
        [((rows, kl), BF), ((rows, kl), BF)],
        (at, own, *gots, own_b, stats_b),
        [((b_rows, kl), BF)],
    )
    same_b = lax.ppermute(same_b, every, swap_pairs(0))
    other_b = lax.ppermute(other_b, every, swap_pairs(1))
    part, diag_corr, power = call(
        back_a_body,
        "back_a",
        [((rows, width), F32), ((1, kt), F32), ((1, chunk), F32)],
        (got_a, raw_a, stats_a, keep_a, piece),
    )
    (share,) = call(
        back_b_body,
        "back_b",
        [((tile_n, rows + 8, chunk), BF)],
        (at, part, same_b, other_b, keep_b, piece, power),
        [((8, chunk), F32)],
    )
    got = lax.all_to_all(share, TILE, 0, 0, tiled=True)
    feats_grad, cross_power = call(
        lambda *refs: end_body(*refs, scale=LOSS_SCALE / total, features=kt * tile_n),
        "end",
        [((rows, chunk), F32), ((1, chunk), F32)],
        (got,),
    )
    return feats_grad, diag_corr[0], cross_power[0, 0]


def solution(mesh):
    fine = Mesh(mesh.devices.reshape(DP_SHAPE + TILE_SHAPE), DP + TILE)
    in_specs = (P(DP, None), P(DP, None), P(DP, None), P(DP, TILE))
    out_specs = (P(DP, TILE), P(TILE), P())
    return jax.shard_map(
        on_device, mesh=fine, in_specs=in_specs, out_specs=out_specs, check_vma=False
    )
```

```python
import jax
import jax.numpy as jnp
from jax import lax
from jax.experimental import pallas as pl
from jax.experimental.pallas import tpu as pltpu
from jax.sharding import Mesh
from jax.sharding import PartitionSpec as P

GROUPS = 32
LAMBDA_OFF = 0.0051
NORM_EPS = 1e-05
LOSS_SCALE = 65536.0
INTERPRET = False

DP_SHAPE = (2, 4, 8)
TILE_SHAPE = (4, 2)
DP = ("zh", "x", "y")
TILE = ("zl", "c")
BF = jnp.bfloat16
F32 = jnp.float32
FAR = 1 << 20


def masked_views(feats, jitter, mask_ids):
    width = feats.shape[1]
    group_size = width // GROUPS
    channel_group = lax.broadcasted_iota(jnp.int32, (1, width), 1) // group_size
    keep_a = (channel_group != mask_ids[:, 0:1]).astype(F32)
    keep_b = (channel_group != mask_ids[:, 1:2]).astype(F32)
    values = feats.astype(F32)
    view_a = (values * keep_a).astype(BF)
    view_b = (values * keep_b + jitter.astype(F32)).astype(BF)
    return jnp.concatenate([view_a, view_b], axis=0), keep_a, keep_b


def spread(value, axes):
    parts = lax.axis_size(axes)
    return lax.all_to_all(
        jnp.broadcast_to(value[None], (parts,) + value.shape), axes, 0, 0, tiled=True
    )


def shift(value, axis, step):
    n = lax.axis_size(axis)
    return lax.ppermute(value, axis, [(i, (i + step) % n) for i in range(n)])


def flip(value, axis, step):
    n = lax.axis_size(axis)
    return lax.ppermute(value, axis, [(i, i ^ step) for i in range(n)])


def swap_pairs(other):
    zh_n, x_n, n = DP_SHAPE
    where = lambda zh, x, y, t: ((zh * x_n + x) * n + y) * n + t
    return [
        (where(zh, x, y, t), where(zh ^ other, x, t, y))
        for zh in range(zh_n)
        for x in range(x_n)
        for y in range(n)
        for t in range(n)
    ]


def dot(a, b, ca, cb, precision=None):
    return lax.dot_general(
        a, b, (((ca,), (cb,)), ((), ())), precision=precision, preferred_element_type=F32
    )


def exact(a, b, ca, cb):
    return dot(a, b, ca, cb, lax.Precision.HIGHEST)


def put_pieces(ref, at, value, count):
    for i in range(count):
        part = value.astype(BF).astype(F32)
        ref[at + i : at + i + 1, :] = part
        value = value - part
    return at + count


def joined(rows, at, count):
    total = rows[at : at + 1]
    for i in range(1, count):
        total = total + rows[at + i : at + i + 1]
    return total


def call(body, name, outs, args, scratch=()):
    specs = [
        pl.BlockSpec(memory_space=pltpu.SMEM if a.dtype == jnp.int32 and a.ndim == 1 else pltpu.VMEM)
        for a in args
    ]
    return pl.pallas_call(
        body,
        name=name,
        out_shape=[jax.ShapeDtypeStruct(s, d) for s, d in outs],
        in_specs=specs,
        out_specs=[pl.BlockSpec(memory_space=pltpu.VMEM) for _ in outs],
        scratch_shapes=[pltpu.VMEM(s, d) for s, d in scratch],
        interpret=INTERPRET,
    )(*args)


def project_body(
    at, view, view2, own, back, ahead, far_low, far_high, piece, wide_a, raw_a, half_b
):
    zh_n, x_n, y_n, rows, kt = piece.shape
    x = at[0]
    half = y_n // 2
    for zh in range(zh_n):
        piece[zh, x] = own[:, zh]
        piece[zh, lax.rem(x + x_n - 1, x_n)] = back[:, zh]
        piece[zh, lax.rem(x + 1, x_n)] = ahead[:, zh]
        far = lax.rem(x + 2, x_n)
        piece[zh, far, :half] = far_low[:, zh]
        piece[zh, far, half:] = far_high[:, zh]
    weight = piece[...].reshape(zh_n * x_n * y_n * rows, kt)
    raw = dot(view[...], weight, 1, 0).astype(BF)
    raw2 = dot(view2[...], weight, 1, 0).astype(BF)
    n, kt = raw_a.shape
    kl = kt // zh_n
    low = at[5] == 0
    raw_a[...] = raw[:n]
    low_a, high_a = jnp.where(low, raw[:n], raw2[:n]), jnp.where(low, raw2[:n], raw[:n])
    for i in range(wide_a.shape[0]):
        wide_a[i, :n] = low_a
        wide_a[i, n:] = high_a
    mine = jnp.where(low, raw[n:, :kl], raw[n:, kl:])
    theirs = jnp.where(low, raw2[n:, :kl], raw2[n:, kl:])
    half_b[:n] = jnp.where(low, mine, theirs)
    half_b[n:] = jnp.where(low, theirs, mine)


def gram_body(at, big_a, big_b, out, tail):
    parts, rows, kt = big_a.shape
    block = parts * rows
    kl = big_b.shape[2]
    a = big_a[...].reshape(block, kt).astype(F32)
    b = big_b[...].reshape(block, kl).astype(F32)
    mean_a = jnp.sum(a, axis=0, keepdims=True) / block
    mean_b = jnp.sum(b, axis=0, keepdims=True) / block
    a = a - mean_a
    b = b - mean_b
    gram = dot(a.astype(BF), b.astype(BF), 0, 0).astype(BF)
    square_a = jnp.sum(a * a, axis=0, keepdims=True)
    facing = jnp.where(at[5] == 0, a[:, :kl], a[:, kl:])
    tail[...] = jnp.zeros_like(tail)
    pos = 0
    for row in (
        mean_a[:, :kl],
        mean_a[:, kl:],
        square_a[:, :kl],
        square_a[:, kl:],
        mean_b,
        jnp.sum(b * b, axis=0, keepdims=True),
        jnp.sum(facing * b, axis=0, keepdims=True),
    ):
        pos = put_pieces(tail, pos, row, 3)
    deep = out.shape[1] - tail.shape[0]
    rows_out = tail[...].astype(BF)
    for x in range(out.shape[0]):
        out[x, :deep] = gram[x * deep : (x + 1) * deep]
        out[x, deep:] = rows_out


def mix_body(at, got, mix, stats_a, stats_b, table, offs, *, block):
    sets, deep, kl = got.shape
    sub = mix.shape[0]
    kt = stats_a.shape[1]
    total = block * sets
    raws = []
    for x in range(sets):
        rows = got[x, sub:].astype(F32)
        r = [joined(rows, 3 * i, 3) for i in range(7)]
        wide = lambda i: jnp.concatenate([r[i], r[i + 1]], axis=1)
        raws.append((wide(0), wide(2), r[4], r[5], r[6]))
    summed = [sum((r[i] for r in raws[1:]), raws[0][i]) for i in range(5)]
    mean_a, mean_b = summed[0] / sets, summed[2] / sets
    square_a, square_b, cross = summed[1], summed[3], summed[4]
    drift_a = jnp.zeros_like(mean_a)
    drift_b = jnp.zeros_like(mean_b)
    first = at[5] == 0
    facing = lambda row: jnp.where(first, row[:, :kl], row[:, kl:])
    table[...] = jnp.zeros_like(table)
    offs[...] = jnp.zeros_like(offs)
    for i, r in enumerate(raws):
        off_a, off_b = r[0] - mean_a, r[2] - mean_b
        square_a = square_a + block * off_a * off_a
        square_b = square_b + block * off_b * off_b
        cross = cross + block * facing(off_a) * off_b
        drift_a, drift_b = drift_a + off_a, drift_b + off_b
        table[i : i + 1, :] = off_a
        offs[i : i + 1, :] = block * off_b
    inv_a = lax.rsqrt(square_a / total + NORM_EPS)
    inv_b = lax.rsqrt(square_b / total + NORM_EPS)
    table[sets : sets + 1, :] = inv_a
    diag = cross * (facing(inv_a) * inv_b / total)
    coeff = -2.0 * (1.0 - diag) - 2.0 * LAMBDA_OFF * diag
    k_of = lax.broadcasted_iota(jnp.int32, (sub, kt), 0)
    l_of = lax.broadcasted_iota(jnp.int32, (sub, kt), 1)
    chosen = exact((k_of + at[3] == l_of).astype(F32), table[...], 1, 1)
    corr = got[0, :sub].astype(F32)
    for x in range(1, sets):
        corr = corr + got[x, :sub].astype(F32)
    corr = corr + exact(chosen, offs[...], 1, 0)
    corr = corr * (chosen[:, sets : sets + 1] * (inv_b / total))
    k_of = lax.broadcasted_iota(jnp.int32, (sub, kl), 0)
    l_of = lax.broadcasted_iota(jnp.int32, (sub, kl), 1)
    here = k_of + at[3] == l_of + at[4]
    mix[...] = jnp.where(
        here, coeff + 2.0 * LAMBDA_OFF * diag, 2.0 * LAMBDA_OFF * corr
    ).astype(BF)
    held = diag * (at[4] != FAR).astype(F32)
    none = jnp.zeros_like(held)
    stats_a[...] = jnp.zeros_like(stats_a)
    stats_b[...] = jnp.zeros_like(stats_b)
    stats_a[0:1, :] = mean_a
    stats_a[1:2, :] = inv_a
    stats_a[2:3, :] = drift_a * inv_a / sets
    stats_a[3:4, :kl] = jnp.where(first, held, none)
    stats_a[3:4, kl:] = jnp.where(first, none, held)
    stats_b[0:1, :] = mean_b
    stats_b[1:2, :] = inv_b
    stats_b[2:3, :] = drift_b * inv_b / sets
    stats_b[3:4, :] = diag


def correlation(at, mix, stats_b):
    k_of = lax.broadcasted_iota(jnp.int32, mix.shape, 0)
    l_of = lax.broadcasted_iota(jnp.int32, mix.shape, 1)
    return jnp.where(k_of == l_of + at[4], stats_b[3:4, :], mix * (0.5 / LAMBDA_OFF))


def grad_b_body(at, mix4, big_a, stats_a, stats_b, sent, kept, grads, tail):
    c = at[2]
    parts, rows, kl = grads.shape
    kt = big_a.shape[2]
    line = parts // 2
    mix = mix4[...].reshape(kt, kl)
    wide = mix.astype(F32)
    norm_a = (big_a[...].reshape(parts * rows, kt).astype(F32) - stats_a[0:1, :]) * stats_a[1:2, :]
    grads[...] = dot(norm_a.astype(BF), mix, 1, 0).reshape(parts, rows, kl)
    for z in range(line):
        sent[z * rows : (z + 1) * rows] = grads[z * 2 + (1 - c)].astype(BF)
        kept[z * rows : (z + 1) * rows] = grads[z * 2 + c]
    second = jnp.sum(wide * correlation(at, wide, stats_b), axis=0, keepdims=True)
    first = exact(stats_a[...], wide, 1, 0)[2:3]
    tail[...] = jnp.zeros_like(tail)
    pos = put_pieces(tail, 0, second, 3)
    put_pieces(tail, pos, first, 2)
    sent[line * rows :] = tail[...].astype(BF)
    kept[line * rows :] = jnp.zeros_like(tail)
    kept[line * rows : line * rows + 1] = second
    kept[line * rows + 1 : line * rows + 2] = first


def grad_a_body(at, mix4, big_b, stats_a, stats_b, out, tail):
    parts, deep, kt = out.shape
    rows = deep - 8
    kl = big_b.shape[2]
    mix = mix4[...].reshape(kt, kl)
    wide = mix.astype(F32)
    norm_b = (big_b[...].reshape(parts * rows, kl).astype(F32) - stats_b[0:1, :]) * stats_b[1:2, :]
    grad = dot(norm_b.astype(BF), mix, 1, 1).astype(BF)
    corr = correlation(at, wide, stats_b)
    ones = jnp.ones((8, kl), F32)
    pos = put_pieces(tail, 0, exact(ones, wide * corr, 1, 1)[0:1], 2)
    pos = put_pieces(tail, pos, exact(ones, corr * corr, 1, 1)[0:1], 2)
    pos = put_pieces(tail, pos, stats_a[3:4, :], 3)
    put_pieces(tail, pos, exact(stats_b[...], wide, 1, 1)[2:3], 1)
    rows_out = tail[...].astype(BF)
    for i in range(parts):
        out[i, :rows] = grad[i * rows : (i + 1) * rows]
        out[i, rows:] = rows_out


def core_body(at, kept, got, own, out1, out2, out3, total, tail):
    zl = at[1]
    rows = own.shape[0] - 8
    deep = kept.shape[0] - 8
    total[...] = kept[:deep] + got[:deep].astype(F32)
    theirs = got[deep:].astype(F32)
    second = kept[deep : deep + 1] + joined(theirs, 0, 3)
    first = kept[deep + 1 : deep + 2] + joined(theirs, 3, 2)
    tail[...] = jnp.zeros_like(tail)
    pos = put_pieces(tail, 0, second, 3)
    put_pieces(tail, pos, first, 2)
    rows_out = tail[...].astype(BF)
    start = lambda step: pl.ds(pl.multiple_of((zl ^ step) * rows, rows), rows)
    for step, out in enumerate((out1, out2, out3), 1):
        out[:rows] = total[start(step), :].astype(BF)
        out[rows:] = rows_out
    own[:rows] = total[start(0), :]
    own[rows:] = jnp.zeros_like(tail)
    own[rows : rows + 1] = second
    own[rows + 1 : rows + 2] = first


def dz_b_body(at, own, got1, got2, got3, raw_b, stats_b, same, other, both):
    deep = both.shape[0]
    rows = same.shape[0]
    grad = own[:deep]
    second, first = own[deep : deep + 1], own[deep + 1 : deep + 2]
    for got in (got1, got2, got3):
        grad = grad + got[:deep].astype(F32)
        theirs = got[deep:].astype(F32)
        second = second + joined(theirs, 0, 3)
        first = first + joined(theirs, 3, 2)
    inv = stats_b[1:2, :]
    norm = ((raw_b[...].astype(F32) - stats_b[0:1, :]) * inv).astype(BF).astype(F32)
    both = (inv * (grad - first - norm * second)).astype(BF)
    low = at[5] == 0
    same[...] = jnp.where(low, both[:rows], both[rows:])
    other[...] = jnp.where(low, both[rows:], both[:rows])


def sum_a_body(at, got, sent, kept, tail):
    parts, deep, _ = got.shape
    both = deep - 8
    rows = both // 2
    grad = got[0, :both].astype(F32)
    tails = [got[i, both:].astype(F32) for i in range(parts)]
    for i in range(1, parts):
        grad = grad + got[i, :both].astype(F32)
    pos, start = 0, 0
    for count in (2, 2, 3, 1):
        row = sum((joined(t, start, count) for t in tails[1:]), joined(tails[0], start, count))
        start += count
        pos = put_pieces(tail, pos, row, count)
    low = at[5] == 0
    sent[:rows] = jnp.where(low, grad[rows:], grad[:rows]).astype(BF)
    sent[rows:] = tail[...].astype(BF)
    kept[:rows] = jnp.where(low, grad[:rows], grad[rows:])
    kept[rows:] = tail[...]


def back_a_body(kept, got, raw_a, stats_a, keep, weight, out, diag_out, power_out):
    rows, kt = raw_a.shape
    grad = kept[:rows] + got[:rows].astype(F32)
    mine, theirs = kept[rows:], got[rows:].astype(F32)
    gather = lambda pos, count: joined(mine, pos, count) + joined(theirs, pos, count)
    second, power, diag, first = gather(0, 2), gather(2, 2), gather(4, 3), gather(7, 1)
    inv = stats_a[1:2, :]
    norm = ((raw_a[...].astype(F32) - stats_a[0:1, :]) * inv).astype(BF).astype(F32)
    dz = (inv * (grad - first - norm * second)).astype(BF)
    width = keep.shape[1]
    out[...] = keep[...] * dot(dz, weight[...].reshape(width, kt), 1, 1)
    diag_out[...] = diag
    power_out[...] = jnp.broadcast_to(jnp.sum(power, axis=1, keepdims=True), power_out.shape)


def back_b_body(at, part, same, other, keep, weight, power, out, tail):
    rows, width = part.shape
    parts, _, chunk = out.shape
    low = at[5] == 0
    dz = jnp.concatenate(
        [jnp.where(low, same[...], other[...]), jnp.where(low, other[...], same[...])], axis=1
    )
    both = part[...] + keep[...] * dot(dz, weight[...].reshape(width, dz.shape[1]), 1, 1)
    both = both.astype(BF)
    tail[...] = jnp.zeros_like(tail)
    put_pieces(tail, 0, power[...], 3)
    rows_out = tail[...].astype(BF)
    for i in range(parts):
        out[i, :rows] = both[:, i * chunk : (i + 1) * chunk]
        out[i, rows:] = rows_out


def end_body(got, out, power_out, *, scale, features):
    line, deep, _ = got.shape
    rows = deep - 8
    total = got[0, :rows].astype(F32)
    power = joined(got[0, rows:].astype(F32), 0, 3)
    for z in range(1, line):
        total = total + got[z, :rows].astype(F32)
        power = power + joined(got[z, rows:].astype(F32), 0, 3)
    out[...] = scale * total
    power_out[...] = power / features


def on_device(feats, jitter, mask_ids, weight):
    rows, width = feats.shape
    w_rows, kt = weight.shape
    zh_n, x_n, y_n = DP_SHAPE
    zl_n, c_n = TILE_SHAPE
    tile_n = zl_n * c_n
    parts = y_n * zh_n
    block = rows * parts
    total = block * x_n
    sub = kt // x_n
    kl = kt // zh_n
    chunk = width // tile_n
    every = DP + TILE
    zh_at = lax.axis_index("zh")
    at = jnp.stack(
        [
            lax.axis_index("x"),
            lax.axis_index("zl"),
            lax.axis_index("c"),
            lax.axis_index("x") * sub,
            jnp.where(lax.axis_index("y") == lax.axis_index(TILE), zh_at * kl, FAR),
            zh_at,
        ]
    ).astype(jnp.int32)
    view, keep_a, keep_b = masked_views(feats, jitter, mask_ids)
    view2 = flip(view, "zh", 1)

    own = lax.all_gather(weight, "zh", axis=0, tiled=True)
    own = spread(own, "y").reshape(y_n, zh_n, w_rows, kt)
    half = y_n // 2
    back = shift(own, "x", 1)
    ahead = shift(own, "x", x_n - 1)
    far_low = shift(back[:half], "x", 1)
    far_high = shift(ahead[half:], "x", x_n - 1)
    piece, wide_a, raw_a, half_b = call(
        project_body,
        "project",
        [
            ((zh_n, x_n, y_n, w_rows, kt), BF),
            ((y_n, zh_n * rows, kt), BF),
            ((rows, kt), BF),
            ((zh_n * rows, kl), BF),
        ],
        (at, view, view2, own, back, ahead, far_low, far_high),
    )

    big_a = lax.all_to_all(wide_a, "y", 0, 0, tiled=True)
    own_b = lax.ppermute(half_b, every, swap_pairs(0))
    big_b = lax.all_gather(own_b, TILE, axis=0)
    (gram,) = call(
        gram_body, "gram", [((x_n, sub + 32, kl), BF)], (at, big_a, big_b), [((32, kl), F32)]
    )

    got = lax.all_to_all(gram, "x", 0, 0, tiled=True)
    mix, stats_a, stats_b = call(
        lambda *refs: mix_body(*refs, block=block),
        "mix",
        [((sub, kl), BF), ((8, kt), F32), ((8, kl), F32)],
        (at, got),
        [((8, kt), F32), ((8, kl), F32)],
    )
    mix = spread(mix, "x")

    b_rows = rows * zh_n
    line_rows = zl_n * b_rows + 8
    sent, kept = call(
        grad_b_body,
        "grad_b",
        [((line_rows, kl), BF), ((line_rows, kl), F32)],
        (at, mix, big_a, stats_a, stats_b),
        [((tile_n, b_rows, kl), F32), ((8, kl), F32)],
    )
    got_b = flip(sent, "c", 1)
    (grad_a,) = call(
        grad_a_body,
        "grad_a",
        [((y_n, zh_n * rows + 8, kt), BF)],
        (at, mix, big_b, stats_a, stats_b),
        [((8, kt), F32)],
    )
    got_a = lax.all_to_all(grad_a, "y", 0, 0, tiled=True)
    sent_a, kept_a = call(
        sum_a_body,
        "sum_a",
        [((rows + 8, kt), BF), ((rows + 8, kt), F32)],
        (at, got_a),
        [((8, kt), F32)],
    )
    got_a = flip(sent_a, "zh", 1)
    own, *outs = call(
        core_body,
        "core",
        [((b_rows + 8, kl), F32)] + [((b_rows + 8, kl), BF)] * 3,
        (at, kept, got_b),
        [((zl_n * b_rows, kl), F32), ((8, kl), F32)],
    )
    gots = [flip(o, "zl", step) for step, o in enumerate(outs, 1)]
    same_b, other_b = call(
        dz_b_body,
        "dz_b",
        [((rows, kl), BF), ((rows, kl), BF)],
        (at, own, *gots, own_b, stats_b),
        [((b_rows, kl), BF)],
    )
    same_b = lax.ppermute(same_b, every, swap_pairs(0))
    other_b = lax.ppermute(other_b, every, swap_pairs(1))
    part, diag_corr, power = call(
        back_a_body,
        "back_a",
        [((rows, width), F32), ((1, kt), F32), ((1, chunk), F32)],
        (kept_a, got_a, raw_a, stats_a, keep_a, piece),
    )
    (share,) = call(
        back_b_body,
        "back_b",
        [((tile_n, rows + 8, chunk), BF)],
        (at, part, same_b, other_b, keep_b, piece, power),
        [((8, chunk), F32)],
    )
    got = lax.all_to_all(share, TILE, 0, 0, tiled=True)
    feats_grad, cross_power = call(
        lambda *refs: end_body(*refs, scale=LOSS_SCALE / total, features=kt * tile_n),
        "end",
        [((rows, chunk), F32), ((1, chunk), F32)],
        (got,),
    )
    return feats_grad, diag_corr[0], cross_power[0, 0]


def solution(mesh):
    fine = Mesh(mesh.devices.reshape(DP_SHAPE + TILE_SHAPE), DP + TILE)
    in_specs = (P(DP, None), P(DP, None), P(DP, None), P(DP, TILE))
    out_specs = (P(DP, TILE), P(TILE), P())
    return jax.shard_map(
        on_device, mesh=fine, in_specs=in_specs, out_specs=out_specs, check_vma=False
    )
```

```python
import jax
import jax.numpy as jnp
from jax import lax
from jax.experimental import pallas as pl
from jax.experimental.pallas import tpu as pltpu
from jax.sharding import Mesh
from jax.sharding import PartitionSpec as P

GROUPS = 32
LAMBDA_OFF = 0.0051
NORM_EPS = 1e-05
LOSS_SCALE = 65536.0
INTERPRET = False

DP_SHAPE = (2, 4, 8)
TILE_SHAPE = (4, 2)
DP = ("zh", "x", "y")
TILE = ("zl", "c")
BF = jnp.bfloat16
F32 = jnp.float32
FAR = 1 << 20


def masked_views(feats, jitter, mask_ids):
    width = feats.shape[1]
    group_size = width // GROUPS
    channel_group = lax.broadcasted_iota(jnp.int32, (1, width), 1) // group_size
    keep_a = (channel_group != mask_ids[:, 0:1]).astype(F32)
    keep_b = (channel_group != mask_ids[:, 1:2]).astype(F32)
    values = feats.astype(F32)
    view_a = (values * keep_a).astype(BF)
    view_b = (values * keep_b + jitter.astype(F32)).astype(BF)
    return jnp.concatenate([view_a, view_b], axis=0), keep_a, keep_b


def spread(value, axes):
    parts = lax.axis_size(axes)
    return lax.all_to_all(
        jnp.broadcast_to(value[None], (parts,) + value.shape), axes, 0, 0, tiled=True
    )


def shift(value, axis, step):
    n = lax.axis_size(axis)
    return lax.ppermute(value, axis, [(i, (i + step) % n) for i in range(n)])


def flip(value, axis, step):
    n = lax.axis_size(axis)
    return lax.ppermute(value, axis, [(i, i ^ step) for i in range(n)])


def swap_pairs():
    rows_n = DP_SHAPE[0] * DP_SHAPE[1]
    n = DP_SHAPE[2]
    where = lambda r, y, t: (r * n + y) * n + t
    return [
        (where(r, y, t), where(r, t, y)) for r in range(rows_n) for y in range(n) for t in range(n)
    ]


def dot(a, b, ca, cb, precision=None):
    return lax.dot_general(
        a, b, (((ca,), (cb,)), ((), ())), precision=precision, preferred_element_type=F32
    )


def exact(a, b, ca, cb):
    return dot(a, b, ca, cb, lax.Precision.HIGHEST)


def put_pieces(ref, at, value, count):
    for i in range(count):
        part = value.astype(BF).astype(F32)
        ref[at + i : at + i + 1, :] = part
        value = value - part
    return at + count


def joined(rows, at, count):
    total = rows[at : at + 1]
    for i in range(1, count):
        total = total + rows[at + i : at + i + 1]
    return total


def call(body, name, outs, args, scratch=()):
    specs = [
        pl.BlockSpec(memory_space=pltpu.SMEM if a.dtype == jnp.int32 and a.ndim == 1 else pltpu.VMEM)
        for a in args
    ]
    return pl.pallas_call(
        body,
        name=name,
        out_shape=[jax.ShapeDtypeStruct(s, d) for s, d in outs],
        in_specs=specs,
        out_specs=[pl.BlockSpec(memory_space=pltpu.VMEM) for _ in outs],
        scratch_shapes=[pltpu.VMEM(s, d) for s, d in scratch],
        interpret=INTERPRET,
    )(*args)


def project_body(at, view, own, back, ahead, far_low, far_high, piece, wide_a, raw_b):
    zh_n, x_n, y_n, rows, kt = piece.shape
    x = at[0]
    half = y_n // 2
    for zh in range(zh_n):
        piece[zh, x] = own[:, zh]
        piece[zh, lax.rem(x + x_n - 1, x_n)] = back[:, zh]
        piece[zh, lax.rem(x + 1, x_n)] = ahead[:, zh]
        far = lax.rem(x + 2, x_n)
        piece[zh, far, :half] = far_low[:, zh]
        piece[zh, far, half:] = far_high[:, zh]
    weight = piece[...].reshape(zh_n * x_n * y_n * rows, kt)
    raw = dot(view[...], weight, 1, 0).astype(BF)
    n = raw_b.shape[0]
    for i in range(wide_a.shape[0]):
        wide_a[i] = raw[:n]
    raw_b[...] = raw[n:]


def gram_body(big_a, big_b, out, tail):
    parts, rows, kt = big_a.shape
    block = parts * rows
    a = big_a[...].reshape(block, kt).astype(F32)
    b = big_b[...].reshape(block, kt).astype(F32)
    mean_a = jnp.sum(a, axis=0, keepdims=True) / block
    mean_b = jnp.sum(b, axis=0, keepdims=True) / block
    a = a - mean_a
    b = b - mean_b
    gram = dot(a.astype(BF), b.astype(BF), 0, 0).astype(BF)
    tail[...] = jnp.zeros_like(tail)
    pos = put_pieces(tail, 0, mean_a, 3)
    pos = put_pieces(tail, pos, jnp.sum(a * a, axis=0, keepdims=True), 3)
    pos = put_pieces(tail, pos, mean_b, 3)
    pos = put_pieces(tail, pos, jnp.sum(b * b, axis=0, keepdims=True), 3)
    put_pieces(tail, pos, jnp.sum(a * b, axis=0, keepdims=True), 3)
    deep = out.shape[1] - 16
    rows_out = tail[...].astype(BF)
    for i in range(out.shape[0]):
        out[i, :deep] = gram[i * deep : (i + 1) * deep]
        out[i, deep:] = rows_out


def mix_body(at, got, mix, stats, table, offs, *, block):
    sets, deep, kt = got.shape
    sub = mix.shape[0]
    total = block * sets
    raws = []
    for i in range(sets):
        rows = got[i, sub:].astype(F32)
        raws.append([joined(rows, 3 * j, 3) for j in range(5)])
    summed = [sum(r[i] for r in raws[1:]) + raws[0][i] for i in range(5)]
    mean_a, mean_b = summed[0] / sets, summed[2] / sets
    square_a, square_b, cross = summed[1], summed[3], summed[4]
    drift_a = jnp.zeros_like(mean_a)
    drift_b = jnp.zeros_like(mean_b)
    table[...] = jnp.zeros_like(table)
    for i, r in enumerate(raws):
        off_a, off_b = r[0] - mean_a, r[2] - mean_b
        square_a = square_a + block * off_a * off_a
        square_b = square_b + block * off_b * off_b
        cross = cross + block * off_a * off_b
        drift_a, drift_b = drift_a + off_a, drift_b + off_b
        table[i : i + 1, :] = off_a
        offs[i : i + 1, :] = block * off_b
    inv_a = lax.rsqrt(square_a / total + NORM_EPS)
    inv_b = lax.rsqrt(square_b / total + NORM_EPS)
    table[sets : sets + 1, :] = inv_a
    diag = cross * (inv_a * inv_b / total)
    coeff = -2.0 * (1.0 - diag) - 2.0 * LAMBDA_OFF * diag
    k_of = lax.broadcasted_iota(jnp.int32, (sub, kt), 0)
    l_of = lax.broadcasted_iota(jnp.int32, (sub, kt), 1)
    chosen = exact((k_of + at[3] == l_of).astype(F32), table[...], 1, 1)
    corr = got[0, :sub].astype(F32)
    for i in range(1, sets):
        corr = corr + got[i, :sub].astype(F32)
    corr = corr + exact(chosen[:, :sets], offs[...], 1, 0)
    corr = corr * (chosen[:, sets : sets + 1] * (inv_b / total))
    here = k_of + (at[3] + at[4]) == l_of
    mix[...] = jnp.where(
        here, coeff + 2.0 * LAMBDA_OFF * diag, 2.0 * LAMBDA_OFF * corr
    ).astype(BF)
    stats[0:1, :] = mean_a
    stats[1:2, :] = inv_a
    stats[2:3, :] = mean_b
    stats[3:4, :] = inv_b
    stats[4:5, :] = diag
    stats[5:6, :] = drift_a * inv_a / sets
    stats[6:7, :] = drift_b * inv_b / sets
    stats[7:8, :] = diag * (at[4] == 0).astype(F32)


def thirds(value):
    out = []
    for _ in range(3):
        out.append(value.astype(BF))
        value = value - out[-1].astype(F32)
    return out


def correlation(at, mix, stats):
    kt = mix.shape[0]
    k_of = lax.broadcasted_iota(jnp.int32, (kt, kt), 0)
    l_of = lax.broadcasted_iota(jnp.int32, (kt, kt), 1)
    return jnp.where(k_of + at[4] == l_of, stats[4:5, :], mix * (0.5 / LAMBDA_OFF))


def grad_b_body(at, mix4, big_a, stats, sent, kept, grads, tail):
    c = at[2]
    parts, rows, kt = big_a.shape
    line = parts // 2
    mix = mix4[...].reshape(kt, kt)
    wide = mix.astype(F32)
    norm_a = (big_a[...].reshape(parts * rows, kt).astype(F32) - stats[0:1, :]) * stats[1:2, :]
    grads[...] = dot(norm_a.astype(BF), mix, 1, 0).reshape(parts, rows, kt)
    for z in range(line):
        sent[z * rows : (z + 1) * rows] = grads[z * 2 + (1 - c)].astype(BF)
        kept[z * rows : (z + 1) * rows] = grads[z * 2 + c]
    second = jnp.sum(wide * correlation(at, wide, stats), axis=0, keepdims=True)
    first = sum(dot(p, mix, 1, 0) for p in thirds(stats[...]))[5:6]
    tail[...] = jnp.zeros_like(tail)
    pos = put_pieces(tail, 0, second, 3)
    put_pieces(tail, pos, first, 2)
    sent[line * rows :] = tail[...].astype(BF)
    kept[line * rows :] = jnp.zeros_like(tail)
    kept[line * rows : line * rows + 1] = second
    kept[line * rows + 1 : line * rows + 2] = first


def grad_a_body(at, mix4, big_b, stats, out, tail):
    parts, rows, kt = big_b.shape
    mix = mix4[...].reshape(kt, kt)
    wide = mix.astype(F32)
    norm_b = (big_b[...].reshape(parts * rows, kt).astype(F32) - stats[2:3, :]) * stats[3:4, :]
    grad = dot(norm_b.astype(BF), mix, 1, 1).astype(BF)
    k_of = lax.broadcasted_iota(jnp.int32, (kt, kt), 0)
    l_of = lax.broadcasted_iota(jnp.int32, (kt, kt), 1)
    square = jnp.where(k_of + at[4] == l_of, 0.0, wide * wide)
    ones = jnp.ones((8, kt), BF)
    square = sum(dot(ones, p, 1, 1) for p in thirds(square)[:2])[0:1]
    diag = stats[7:8, :]
    on = (at[4] == 0).astype(F32)
    coeff = -2.0 * (on - diag) - 2.0 * LAMBDA_OFF * diag
    centre = (coeff + 2.0 * LAMBDA_OFF * diag).astype(BF).astype(F32)
    pos = put_pieces(tail, 0, square * (0.5 / LAMBDA_OFF) + centre * diag, 2)
    pos = put_pieces(tail, pos, square * (0.25 / LAMBDA_OFF**2) + diag * diag, 2)
    pos = put_pieces(tail, pos, diag, 3)
    put_pieces(tail, pos, sum(dot(p, mix, 1, 1) for p in thirds(stats[...]))[6:7], 1)
    rows_out = tail[...].astype(BF)
    for i in range(parts):
        out[i, :rows] = grad[i * rows : (i + 1) * rows]
        out[i, rows:] = rows_out


def core_body(at, kept, got, own, out1, out2, out3, total, tail):
    zl = at[1]
    rows = own.shape[0] - 8
    deep = kept.shape[0] - 8
    total[...] = kept[:deep] + got[:deep].astype(F32)
    theirs = got[deep:].astype(F32)
    second = kept[deep : deep + 1] + joined(theirs, 0, 3)
    first = kept[deep + 1 : deep + 2] + joined(theirs, 3, 2)
    tail[...] = jnp.zeros_like(tail)
    pos = put_pieces(tail, 0, second, 3)
    put_pieces(tail, pos, first, 2)
    rows_out = tail[...].astype(BF)
    start = lambda step: pl.ds(pl.multiple_of((zl ^ step) * rows, rows), rows)
    for step, out in enumerate((out1, out2, out3), 1):
        out[:rows] = total[start(step), :].astype(BF)
        out[rows:] = rows_out
    own[:rows] = total[start(0), :]
    own[rows:] = jnp.zeros_like(tail)
    own[rows : rows + 1] = second
    own[rows + 1 : rows + 2] = first


def dz_b_body(own, got1, got2, got3, raw_b, stats, out):
    rows = out.shape[0]
    grad = own[:rows]
    second, first = own[rows : rows + 1], own[rows + 1 : rows + 2]
    for got in (got1, got2, got3):
        grad = grad + got[:rows].astype(F32)
        theirs = got[rows:].astype(F32)
        second = second + joined(theirs, 0, 3)
        first = first + joined(theirs, 3, 2)
    inv = stats[3:4, :]
    norm = ((raw_b[...].astype(F32) - stats[2:3, :]) * inv).astype(BF).astype(F32)
    out[...] = (inv * (grad - first - norm * second)).astype(BF)


def back_a_body(got, raw_a, stats, keep, weight, out, diag_out, power_out):
    parts, deep, kt = got.shape
    rows = deep - 8
    grad = got[0, :rows].astype(F32)
    tails = [got[i, rows:].astype(F32) for i in range(parts)]
    for i in range(1, parts):
        grad = grad + got[i, :rows].astype(F32)
    gather = lambda pos, count: sum(
        (joined(t, pos, count) for t in tails[1:]), joined(tails[0], pos, count)
    )
    second, power, diag, first = gather(0, 2), gather(2, 2), gather(4, 3), gather(7, 1)
    inv = stats[1:2, :]
    norm = ((raw_a[...].astype(F32) - stats[0:1, :]) * inv).astype(BF).astype(F32)
    dz = (inv * (grad - first - norm * second)).astype(BF)
    width = keep.shape[1]
    out[...] = keep[...] * dot(dz, weight[...].reshape(width, kt), 1, 1)
    diag_out[...] = diag
    power_out[...] = jnp.broadcast_to(jnp.sum(power, axis=1, keepdims=True), power_out.shape)


def back_b_body(part, dz, keep, weight, power, out, tail):
    rows, width = part.shape
    parts, _, chunk = out.shape
    both = part[...] + keep[...] * dot(dz[...], weight[...].reshape(width, dz.shape[1]), 1, 1)
    both = both.astype(BF)
    tail[...] = jnp.zeros_like(tail)
    put_pieces(tail, 0, power[...], 3)
    rows_out = tail[...].astype(BF)
    for i in range(parts):
        out[i, :rows] = both[:, i * chunk : (i + 1) * chunk]
        out[i, rows:] = rows_out


def end_body(got, out, power_out, *, scale, features):
    line, deep, _ = got.shape
    rows = deep - 8
    total = got[0, :rows].astype(F32)
    power = joined(got[0, rows:].astype(F32), 0, 3)
    for z in range(1, line):
        total = total + got[z, :rows].astype(F32)
        power = power + joined(got[z, rows:].astype(F32), 0, 3)
    out[...] = scale * total
    power_out[...] = power / features


def on_device(feats, jitter, mask_ids, weight):
    rows, width = feats.shape
    w_rows, kt = weight.shape
    zh_n, x_n, y_n = DP_SHAPE
    zl_n, c_n = TILE_SHAPE
    rows_n = zh_n * x_n
    tile_n = zl_n * c_n
    total = rows * rows_n * y_n
    block = rows * y_n
    sub = kt // rows_n
    chunk = width // tile_n
    every = DP + TILE
    pairs = swap_pairs()

    y_at = lax.axis_index("y")
    tile_at = lax.axis_index(TILE)
    at = jnp.stack(
        [
            lax.axis_index("x"),
            lax.axis_index("zl"),
            lax.axis_index("c"),
            lax.axis_index(("x", "zh")) * sub,
            jnp.where(y_at == tile_at, 0, FAR),
        ]
    ).astype(jnp.int32)
    view, keep_a, keep_b = masked_views(feats, jitter, mask_ids)

    own = spread(weight, ("y", "zh")).reshape(y_n, zh_n, w_rows, kt)
    half = y_n // 2
    back = shift(own, "x", 1)
    ahead = shift(own, "x", x_n - 1)
    far_low = shift(back[:half], "x", 1)
    far_high = shift(ahead[half:], "x", x_n - 1)
    piece, wide_a, raw_b = call(
        project_body,
        "project",
        [((zh_n, x_n, y_n, w_rows, kt), BF), ((y_n, rows, kt), BF), ((rows, kt), BF)],
        (at, view, own, back, ahead, far_low, far_high),
    )

    raw_a = wide_a[0]
    big_a = lax.all_to_all(wide_a, "y", 0, 0, tiled=True)
    own_b = lax.ppermute(raw_b, every, pairs)
    big_b = lax.all_gather(own_b, TILE, axis=0)
    (gram,) = call(
        gram_body, "gram", [((rows_n, sub + 16, kt), BF)], (big_a, big_b), [((16, kt), F32)]
    )

    got = lax.all_to_all(gram, ("x", "zh"), 0, 0, tiled=True)
    mix, stats = call(
        lambda *refs: mix_body(*refs, block=block),
        "mix",
        [((sub, kt), BF), ((8, kt), F32)],
        (at, got),
        [((16, kt), F32), ((rows_n, kt), F32)],
    )
    mix = spread(lax.all_gather(mix, "zh", axis=0, tiled=True), "x")

    line_rows = zl_n * rows + 8
    sent, kept = call(
        grad_b_body,
        "grad_b",
        [((line_rows, kt), BF), ((line_rows, kt), F32)],
        (at, mix, big_a, stats),
        [((tile_n, rows, kt), F32), ((8, kt), F32)],
    )
    got_b = flip(sent, "c", 1)
    (grad_a,) = call(
        grad_a_body, "grad_a", [((y_n, rows + 8, kt), BF)], (at, mix, big_b, stats), [((8, kt), F32)]
    )
    got_a = lax.all_to_all(grad_a, "y", 0, 0, tiled=True)
    own, *outs = call(
        core_body,
        "core",
        [((rows + 8, kt), F32)] + [((rows + 8, kt), BF)] * 3,
        (at, kept, got_b),
        [((zl_n * rows, kt), F32), ((8, kt), F32)],
    )
    gots = [flip(o, "zl", step) for step, o in enumerate(outs, 1)]
    (dz_b,) = call(dz_b_body, "dz_b", [((rows, kt), BF)], (own, *gots, own_b, stats))
    dz_b = lax.ppermute(dz_b, every, pairs)
    part, diag_corr, power = call(
        back_a_body,
        "back_a",
        [((rows, width), F32), ((1, kt), F32), ((1, chunk), F32)],
        (got_a, raw_a, stats, keep_a, piece),
    )
    (share,) = call(
        back_b_body,
        "back_b",
        [((tile_n, rows + 8, chunk), BF)],
        (part, dz_b, keep_b, piece, power),
        [((8, chunk), F32)],
    )
    got = lax.all_to_all(share, TILE, 0, 0, tiled=True)
    feats_grad, cross_power = call(
        lambda *refs: end_body(*refs, scale=LOSS_SCALE / total, features=kt * tile_n),
        "end",
        [((rows, chunk), F32), ((1, chunk), F32)],
        (got,),
    )
    return feats_grad, diag_corr[0], cross_power[0, 0]


def solution(mesh):
    fine = Mesh(mesh.devices.reshape(DP_SHAPE + TILE_SHAPE), DP + TILE)
    in_specs = (P(DP, None), P(DP, None), P(DP, None), P(DP, TILE))
    out_specs = (P(DP, TILE), P(TILE), P())
    return jax.shard_map(
        on_device, mesh=fine, in_specs=in_specs, out_specs=out_specs, check_vma=False
    )
```

```python
import jax
import jax.numpy as jnp
from jax import lax
from jax.experimental import pallas as pl
from jax.experimental.pallas import tpu as pltpu
from jax.sharding import Mesh
from jax.sharding import PartitionSpec as P

GROUPS = 32
LAMBDA_OFF = 0.0051
NORM_EPS = 1e-05
LOSS_SCALE = 65536.0
INTERPRET = False

DP_SHAPE = (2, 4, 8)
TILE_SHAPE = (4, 2)
DP = ("zh", "x", "y")
TILE = ("zl", "c")
BF = jnp.bfloat16
F32 = jnp.float32
FAR = 1 << 20


def masked_views(feats, jitter, mask_ids):
    width = feats.shape[1]
    group_size = width // GROUPS
    channel_group = lax.broadcasted_iota(jnp.int32, (1, width), 1) // group_size
    keep_a = (channel_group != mask_ids[:, 0:1]).astype(F32)
    keep_b = (channel_group != mask_ids[:, 1:2]).astype(F32)
    values = feats.astype(F32)
    view_a = (values * keep_a).astype(BF)
    view_b = (values * keep_b + jitter.astype(F32)).astype(BF)
    return jnp.concatenate([view_a, view_b], axis=0), keep_a, keep_b


def spread(value, axes):
    parts = lax.axis_size(axes)
    return lax.all_to_all(
        jnp.broadcast_to(value[None], (parts,) + value.shape), axes, 0, 0, tiled=True
    )


def shift(value, axis, step):
    n = lax.axis_size(axis)
    return lax.ppermute(value, axis, [(i, (i + step) % n) for i in range(n)])


def flip(value, axis, step):
    n = lax.axis_size(axis)
    return lax.ppermute(value, axis, [(i, i ^ step) for i in range(n)])


def swap_pairs():
    rows_n = DP_SHAPE[0] * DP_SHAPE[1]
    n = DP_SHAPE[2]
    where = lambda r, y, t: (r * n + y) * n + t
    return [
        (where(r, y, t), where(r, t, y)) for r in range(rows_n) for y in range(n) for t in range(n)
    ]


def dot(a, b, ca, cb, precision=None):
    return lax.dot_general(
        a, b, (((ca,), (cb,)), ((), ())), precision=precision, preferred_element_type=F32
    )


def exact(a, b, ca, cb):
    return dot(a, b, ca, cb, lax.Precision.HIGHEST)


def put_pieces(ref, at, value, count):
    for i in range(count):
        part = value.astype(BF).astype(F32)
        ref[at + i : at + i + 1, :] = part
        value = value - part
    return at + count


def joined(rows, at, count):
    total = rows[at : at + 1]
    for i in range(1, count):
        total = total + rows[at + i : at + i + 1]
    return total


def call(body, name, outs, args, scratch=()):
    specs = [
        pl.BlockSpec(memory_space=pltpu.SMEM if a.dtype == jnp.int32 and a.ndim == 1 else pltpu.VMEM)
        for a in args
    ]
    return pl.pallas_call(
        body,
        name=name,
        out_shape=[jax.ShapeDtypeStruct(s, d) for s, d in outs],
        in_specs=specs,
        out_specs=[
            pl.BlockSpec(memory_space=pltpu.SMEM if s == (1, 1) else pltpu.VMEM) for s, _ in outs
        ],
        scratch_shapes=[pltpu.VMEM(s, d) for s, d in scratch],
        interpret=INTERPRET,
    )(*args)


def project_body(at, view, own, back, ahead, far_low, far_high, right, piece, wide_a, raw_b):
    zh_n, x_n, y_n, rows, kt = piece.shape
    x = at[0]
    half = y_n // 2
    left = kt // 2
    after, before, far = lax.rem(x + 1, x_n), lax.rem(x + x_n - 1, x_n), lax.rem(x + 2, x_n)
    for zh in range(zh_n):
        piece[zh, x, :, :, :left] = own[:, zh]
        piece[zh, before, :, :, :left] = back[:, zh]
        piece[zh, after, :, :, :left] = ahead[:, zh]
        piece[zh, far, :half, :, :left] = far_low[:, zh]
        piece[zh, far, half:, :, :left] = far_high[:, zh]
        for step in range(x_n):
            piece[zh, x ^ step, :, :, left:] = right[:, step, zh]
    weight = piece[...].reshape(zh_n * x_n * y_n * rows, kt)
    raw = dot(view[...], weight, 1, 0).astype(BF)
    n = raw_b.shape[0]
    for i in range(wide_a.shape[0]):
        wide_a[i] = raw[:n]
    raw_b[...] = raw[n:]


def gram_body(big_a, big_b, out, tail):
    parts, rows, kt = big_a.shape
    block = parts * rows
    a = big_a[...].reshape(block, kt).astype(F32)
    b = big_b[...].reshape(block, kt).astype(F32)
    mean_a = jnp.sum(a, axis=0, keepdims=True) / block
    mean_b = jnp.sum(b, axis=0, keepdims=True) / block
    a = a - mean_a
    b = b - mean_b
    gram = dot(a.astype(BF), b.astype(BF), 0, 0).astype(BF)
    tail[...] = jnp.zeros_like(tail)
    pos = put_pieces(tail, 0, mean_a, 3)
    pos = put_pieces(tail, pos, jnp.sum(a * a, axis=0, keepdims=True), 3)
    pos = put_pieces(tail, pos, mean_b, 3)
    pos = put_pieces(tail, pos, jnp.sum(b * b, axis=0, keepdims=True), 3)
    put_pieces(tail, pos, jnp.sum(a * b, axis=0, keepdims=True), 3)
    deep = out.shape[1] - 16
    rows_out = tail[...].astype(BF)
    for i in range(out.shape[0]):
        out[i, :deep] = gram[i * deep : (i + 1) * deep]
        out[i, deep:] = rows_out


def mix_body(at, got, mix, stats, table, offs, *, block):
    sets, deep, kt = got.shape
    sub = mix.shape[0]
    total = block * sets
    raws = []
    for i in range(sets):
        rows = got[i, sub:].astype(F32)
        raws.append([joined(rows, 3 * j, 3) for j in range(5)])
    summed = [sum(r[i] for r in raws[1:]) + raws[0][i] for i in range(5)]
    mean_a, mean_b = summed[0] / sets, summed[2] / sets
    square_a, square_b, cross = summed[1], summed[3], summed[4]
    drift_a = jnp.zeros_like(mean_a)
    drift_b = jnp.zeros_like(mean_b)
    table[...] = jnp.zeros_like(table)
    for i, r in enumerate(raws):
        off_a, off_b = r[0] - mean_a, r[2] - mean_b
        square_a = square_a + block * off_a * off_a
        square_b = square_b + block * off_b * off_b
        cross = cross + block * off_a * off_b
        drift_a, drift_b = drift_a + off_a, drift_b + off_b
        table[i : i + 1, :] = off_a
        offs[i : i + 1, :] = block * off_b
    inv_a = lax.rsqrt(square_a / total + NORM_EPS)
    inv_b = lax.rsqrt(square_b / total + NORM_EPS)
    table[sets : sets + 1, :] = inv_a
    diag = cross * (inv_a * inv_b / total)
    coeff = -2.0 * (1.0 - diag) - 2.0 * LAMBDA_OFF * diag
    k_of = lax.broadcasted_iota(jnp.int32, (sub, kt), 0)
    l_of = lax.broadcasted_iota(jnp.int32, (sub, kt), 1)
    chosen = exact((k_of + at[3] == l_of).astype(F32), table[...], 1, 1)
    corr = got[0, :sub].astype(F32)
    for i in range(1, sets):
        corr = corr + got[i, :sub].astype(F32)
    corr = corr + exact(chosen[:, :sets], offs[...], 1, 0)
    corr = corr * (chosen[:, sets : sets + 1] * (inv_b / total))
    here = k_of + (at[3] + at[4]) == l_of
    mix[...] = jnp.where(
        here, coeff + 2.0 * LAMBDA_OFF * diag, 2.0 * LAMBDA_OFF * corr
    ).astype(BF)
    stats[0:1, :] = mean_a
    stats[1:2, :] = inv_a
    stats[2:3, :] = mean_b
    stats[3:4, :] = inv_b
    stats[4:5, :] = diag
    stats[5:6, :] = drift_a * inv_a / sets
    stats[6:7, :] = drift_b * inv_b / sets
    stats[7:8, :] = diag * (at[4] == 0).astype(F32)


def thirds(value):
    out = []
    for _ in range(3):
        out.append(value.astype(BF))
        value = value - out[-1].astype(F32)
    return out


def correlation(at, mix, stats):
    kt = mix.shape[0]
    k_of = lax.broadcasted_iota(jnp.int32, (kt, kt), 0)
    l_of = lax.broadcasted_iota(jnp.int32, (kt, kt), 1)
    return jnp.where(k_of + at[4] == l_of, stats[4:5, :], mix * (0.5 / LAMBDA_OFF))


def grad_b_body(at, mix4, big_a, stats, sent, kept, grads, tail):
    c = at[2]
    parts, rows, kt = big_a.shape
    line = parts // 2
    mix = mix4[...].reshape(kt, kt)
    wide = mix.astype(F32)
    norm_a = (big_a[...].reshape(parts * rows, kt).astype(F32) - stats[0:1, :]) * stats[1:2, :]
    grads[...] = dot(norm_a.astype(BF), mix, 1, 0).reshape(parts, rows, kt)
    for z in range(line):
        sent[z * rows : (z + 1) * rows] = grads[z * 2 + (1 - c)].astype(BF)
        kept[z * rows : (z + 1) * rows] = grads[z * 2 + c]
    second = jnp.sum(wide * correlation(at, wide, stats), axis=0, keepdims=True)
    first = sum(dot(p, mix, 1, 0) for p in thirds(stats[...]))[5:6]
    tail[...] = jnp.zeros_like(tail)
    pos = put_pieces(tail, 0, second, 3)
    put_pieces(tail, pos, first, 2)
    sent[line * rows :] = tail[...].astype(BF)
    kept[line * rows :] = jnp.zeros_like(tail)
    kept[line * rows : line * rows + 1] = second
    kept[line * rows + 1 : line * rows + 2] = first


def grad_a_body(at, mix4, big_b, stats, out, tail):
    parts, rows, kt = big_b.shape
    mix = mix4[...].reshape(kt, kt)
    wide = mix.astype(F32)
    norm_b = (big_b[...].reshape(parts * rows, kt).astype(F32) - stats[2:3, :]) * stats[3:4, :]
    grad = dot(norm_b.astype(BF), mix, 1, 1).astype(BF)
    k_of = lax.broadcasted_iota(jnp.int32, (kt, kt), 0)
    l_of = lax.broadcasted_iota(jnp.int32, (kt, kt), 1)
    square = jnp.where(k_of + at[4] == l_of, 0.0, wide * wide)
    ones = jnp.ones((8, kt), BF)
    square = sum(dot(ones, p, 1, 1) for p in thirds(square)[:2])[0:1]
    diag = stats[7:8, :]
    on = (at[4] == 0).astype(F32)
    coeff = -2.0 * (on - diag) - 2.0 * LAMBDA_OFF * diag
    centre = (coeff + 2.0 * LAMBDA_OFF * diag).astype(BF).astype(F32)
    pos = put_pieces(tail, 0, square * (0.5 / LAMBDA_OFF) + centre * diag, 2)
    pos = put_pieces(tail, pos, square * (0.25 / LAMBDA_OFF**2) + diag * diag, 2)
    pos = put_pieces(tail, pos, diag, 3)
    put_pieces(tail, pos, sum(dot(p, mix, 1, 1) for p in thirds(stats[...]))[6:7], 1)
    rows_out = tail[...].astype(BF)
    for i in range(parts):
        out[i, :rows] = grad[i * rows : (i + 1) * rows]
        out[i, rows:] = rows_out


def core_body(at, kept, got, own, out1, out2, out3, total, tail):
    zl = at[1]
    rows = own.shape[0] - 8
    deep = kept.shape[0] - 8
    total[...] = kept[:deep] + got[:deep].astype(F32)
    theirs = got[deep:].astype(F32)
    second = kept[deep : deep + 1] + joined(theirs, 0, 3)
    first = kept[deep + 1 : deep + 2] + joined(theirs, 3, 2)
    tail[...] = jnp.zeros_like(tail)
    pos = put_pieces(tail, 0, second, 3)
    put_pieces(tail, pos, first, 2)
    rows_out = tail[...].astype(BF)
    start = lambda step: pl.ds(pl.multiple_of((zl ^ step) * rows, rows), rows)
    for step, out in enumerate((out1, out2, out3), 1):
        out[:rows] = total[start(step), :].astype(BF)
        out[rows:] = rows_out
    own[:rows] = total[start(0), :]
    own[rows:] = jnp.zeros_like(tail)
    own[rows : rows + 1] = second
    own[rows + 1 : rows + 2] = first


def dz_b_body(own, got1, got2, got3, raw_b, stats, out):
    rows = out.shape[0]
    grad = own[:rows]
    second, first = own[rows : rows + 1], own[rows + 1 : rows + 2]
    for got in (got1, got2, got3):
        grad = grad + got[:rows].astype(F32)
        theirs = got[rows:].astype(F32)
        second = second + joined(theirs, 0, 3)
        first = first + joined(theirs, 3, 2)
    inv = stats[3:4, :]
    norm = ((raw_b[...].astype(F32) - stats[2:3, :]) * inv).astype(BF).astype(F32)
    out[...] = (inv * (grad - first - norm * second)).astype(BF)


def back_a_body(got, raw_a, stats, keep, weight, out, diag_out, power_out):
    parts, deep, kt = got.shape
    rows = deep - 8
    grad = got[0, :rows].astype(F32)
    tails = [got[i, rows:].astype(F32) for i in range(parts)]
    for i in range(1, parts):
        grad = grad + got[i, :rows].astype(F32)
    gather = lambda pos, count: sum(
        (joined(t, pos, count) for t in tails[1:]), joined(tails[0], pos, count)
    )
    second, power, diag, first = gather(0, 2), gather(2, 2), gather(4, 3), gather(7, 1)
    inv = stats[1:2, :]
    norm = ((raw_a[...].astype(F32) - stats[0:1, :]) * inv).astype(BF).astype(F32)
    dz = (inv * (grad - first - norm * second)).astype(BF)
    width = keep.shape[1]
    out[...] = keep[...] * dot(dz, weight[...].reshape(width, kt), 1, 1)
    diag_out[...] = diag
    power_out[...] = jnp.broadcast_to(jnp.sum(power, axis=1, keepdims=True), power_out.shape)


def back_b_body(part, dz, keep, weight, power, out, tail):
    rows, width = part.shape
    parts, _, chunk = out.shape
    both = part[...] + keep[...] * dot(dz[...], weight[...].reshape(width, dz.shape[1]), 1, 1)
    both = both.astype(BF)
    tail[...] = jnp.zeros_like(tail)
    put_pieces(tail, 0, power[...], 3)
    rows_out = tail[...].astype(BF)
    for i in range(parts):
        out[i, :rows] = both[:, i * chunk : (i + 1) * chunk]
        out[i, rows:] = rows_out


def end_body(got, out, power_out, *, scale, features):
    line, deep, _ = got.shape
    rows = deep - 8
    total = got[0, :rows].astype(F32)
    power = joined(got[0, rows:].astype(F32), 0, 3)
    for z in range(1, line):
        total = total + got[z, :rows].astype(F32)
        power = power + joined(got[z, rows:].astype(F32), 0, 3)
    out[...] = scale * total
    power_out[0, 0] = jnp.max(power[:, :128]) / features


def on_device(feats, jitter, mask_ids, weight):
    rows, width = feats.shape
    w_rows, kt = weight.shape
    zh_n, x_n, y_n = DP_SHAPE
    zl_n, c_n = TILE_SHAPE
    rows_n = zh_n * x_n
    tile_n = zl_n * c_n
    total = rows * rows_n * y_n
    block = rows * y_n
    sub = kt // rows_n
    chunk = width // tile_n
    every = DP + TILE
    pairs = swap_pairs()

    y_at = lax.axis_index("y")
    tile_at = lax.axis_index(TILE)
    at = jnp.stack(
        [
            lax.axis_index("x"),
            lax.axis_index("zl"),
            lax.axis_index("c"),
            lax.axis_index(("x", "zh")) * sub,
            jnp.where(y_at == tile_at, 0, FAR),
        ]
    ).astype(jnp.int32)
    view, keep_a, keep_b = masked_views(feats, jitter, mask_ids)

    own = lax.all_gather(weight, "zh", axis=0)
    right = own[:, :, kt // 2 :]
    right = jnp.stack([right] + [flip(right, "x", step) for step in range(1, x_n)])
    own = spread(own[:, :, : kt // 2], "y").reshape(y_n, zh_n, w_rows, kt // 2)
    right = spread(right, "y").reshape(y_n, x_n, zh_n, w_rows, kt // 2)
    half = y_n // 2
    back = shift(own, "x", 1)
    ahead = shift(own, "x", x_n - 1)
    far_low = shift(back[:half], "x", 1)
    far_high = shift(ahead[half:], "x", x_n - 1)
    piece, wide_a, raw_b = call(
        project_body,
        "project",
        [((zh_n, x_n, y_n, w_rows, kt), BF), ((y_n, rows, kt), BF), ((rows, kt), BF)],
        (at, view, own, back, ahead, far_low, far_high, right),
    )

    raw_a = wide_a[0]
    big_a = lax.all_to_all(wide_a, "y", 0, 0, tiled=True)
    own_b = lax.ppermute(raw_b, every, pairs)
    big_b = lax.all_gather(own_b, TILE, axis=0)
    (gram,) = call(
        gram_body, "gram", [((rows_n, sub + 16, kt), BF)], (big_a, big_b), [((16, kt), F32)]
    )

    got = lax.all_to_all(gram, ("x", "zh"), 0, 0, tiled=True)
    mix, stats = call(
        lambda *refs: mix_body(*refs, block=block),
        "mix",
        [((sub, kt), BF), ((8, kt), F32)],
        (at, got),
        [((16, kt), F32), ((rows_n, kt), F32)],
    )
    mix = spread(lax.all_gather(mix, "zh", axis=0, tiled=True), "x")

    line_rows = zl_n * rows + 8
    sent, kept = call(
        grad_b_body,
        "grad_b",
        [((line_rows, kt), BF), ((line_rows, kt), F32)],
        (at, mix, big_a, stats),
        [((tile_n, rows, kt), F32), ((8, kt), F32)],
    )
    got_b = flip(sent, "c", 1)
    (grad_a,) = call(
        grad_a_body, "grad_a", [((y_n, rows + 8, kt), BF)], (at, mix, big_b, stats), [((8, kt), F32)]
    )
    got_a = lax.all_to_all(grad_a, "y", 0, 0, tiled=True)
    own, *outs = call(
        core_body,
        "core",
        [((rows + 8, kt), F32)] + [((rows + 8, kt), BF)] * 3,
        (at, kept, got_b),
        [((zl_n * rows, kt), F32), ((8, kt), F32)],
    )
    gots = [flip(o, "zl", step) for step, o in enumerate(outs, 1)]
    (dz_b,) = call(dz_b_body, "dz_b", [((rows, kt), BF)], (own, *gots, own_b, stats))
    dz_b = lax.ppermute(dz_b, every, pairs)
    part, diag_corr, power = call(
        back_a_body,
        "back_a",
        [((rows, width), F32), ((1, kt), F32), ((1, chunk), F32)],
        (got_a, raw_a, stats, keep_a, piece),
    )
    (share,) = call(
        back_b_body,
        "back_b",
        [((tile_n, rows + 8, chunk), BF)],
        (part, dz_b, keep_b, piece, power),
        [((8, chunk), F32)],
    )
    got = lax.all_to_all(share, TILE, 0, 0, tiled=True)
    feats_grad, cross_power = call(
        lambda *refs: end_body(*refs, scale=LOSS_SCALE / total, features=kt * tile_n),
        "end",
        [((rows, chunk), F32), ((1, 1), F32)],
        (got,),
    )
    return feats_grad, diag_corr.reshape(kt), cross_power.reshape(())


def solution(mesh):
    fine = Mesh(mesh.devices.reshape(DP_SHAPE + TILE_SHAPE), DP + TILE)
    in_specs = (P(DP, None), P(DP, None), P(DP, None), P(DP, TILE))
    out_specs = (P(DP, TILE), P(TILE), P())
    return jax.shard_map(
        on_device, mesh=fine, in_specs=in_specs, out_specs=out_specs, check_vma=False
    )
```

```python
import jax
import jax.numpy as jnp
from jax import lax
from jax.experimental import pallas as pl
from jax.experimental.pallas import tpu as pltpu
from jax.sharding import Mesh
from jax.sharding import PartitionSpec as P

GROUPS = 32
LAMBDA_OFF = 0.0051
NORM_EPS = 1e-05
LOSS_SCALE = 65536.0
INTERPRET = False

DP_SHAPE = (2, 4, 8)
TILE_SHAPE = (4, 2)
DP = ("zh", "x", "y")
TILE = ("zl", "c")
BF = jnp.bfloat16
F32 = jnp.float32
FAR = 1 << 20


def masked_views(feats, jitter, mask_ids):
    width = feats.shape[1]
    group_size = width // GROUPS
    channel_group = lax.broadcasted_iota(jnp.int32, (1, width), 1) // group_size
    keep_a = (channel_group != mask_ids[:, 0:1]).astype(F32)
    keep_b = (channel_group != mask_ids[:, 1:2]).astype(F32)
    values = feats.astype(F32)
    view_a = (values * keep_a).astype(BF)
    view_b = (values * keep_b + jitter.astype(F32)).astype(BF)
    return jnp.concatenate([view_a, view_b], axis=0), keep_a, keep_b


def spread(value, axes):
    parts = lax.axis_size(axes)
    return lax.all_to_all(
        jnp.broadcast_to(value[None], (parts,) + value.shape), axes, 0, 0, tiled=True
    )


def shift(value, axis, step):
    n = lax.axis_size(axis)
    return lax.ppermute(value, axis, [(i, (i + step) % n) for i in range(n)])


def flip(value, axis, step):
    n = lax.axis_size(axis)
    return lax.ppermute(value, axis, [(i, i ^ step) for i in range(n)])


def swap_pairs():
    rows_n = DP_SHAPE[0] * DP_SHAPE[1]
    n = DP_SHAPE[2]
    where = lambda r, y, t: (r * n + y) * n + t
    return [
        (where(r, y, t), where(r, t, y)) for r in range(rows_n) for y in range(n) for t in range(n)
    ]


def dot(a, b, ca, cb, precision=None):
    return lax.dot_general(
        a, b, (((ca,), (cb,)), ((), ())), precision=precision, preferred_element_type=F32
    )


def exact(a, b, ca, cb):
    return dot(a, b, ca, cb, lax.Precision.HIGHEST)


def put_pieces(ref, at, value, count):
    for i in range(count):
        part = value.astype(BF).astype(F32)
        ref[at + i : at + i + 1, :] = part
        value = value - part
    return at + count


def joined(rows, at, count):
    total = rows[at : at + 1]
    for i in range(1, count):
        total = total + rows[at + i : at + i + 1]
    return total


def call(body, name, outs, args, scratch=()):
    specs = [
        pl.BlockSpec(memory_space=pltpu.SMEM if a.dtype == jnp.int32 and a.ndim == 1 else pltpu.VMEM)
        for a in args
    ]
    return pl.pallas_call(
        body,
        name=name,
        out_shape=[jax.ShapeDtypeStruct(s, d) for s, d in outs],
        in_specs=specs,
        out_specs=[
            pl.BlockSpec(memory_space=pltpu.SMEM if s == (1, 1) else pltpu.VMEM) for s, _ in outs
        ],
        scratch_shapes=[pltpu.VMEM(s, d) for s, d in scratch],
        interpret=INTERPRET,
    )(*args)


def project_body(at, view, own, back, ahead, far_low, far_high, piece, wide_a, raw_b):
    zh_n, x_n, y_n, rows, kt = piece.shape
    x = at[0]
    half = y_n // 2
    after, before, far = lax.rem(x + 1, x_n), lax.rem(x + x_n - 1, x_n), lax.rem(x + 2, x_n)
    for zh in range(zh_n):
        piece[zh, x] = own[:, zh]
        piece[zh, before] = back[:, zh]
        piece[zh, after] = ahead[:, zh]
        piece[zh, far, :half] = far_low[:, zh]
        piece[zh, far, half:] = far_high[:, zh]
    weight = piece[...].reshape(zh_n * x_n * y_n * rows, kt)
    raw = dot(view[...], weight, 1, 0).astype(BF)
    n = raw_b.shape[0]
    for i in range(wide_a.shape[0]):
        wide_a[i] = raw[:n]
    raw_b[...] = raw[n:]


def gram_body(big_a, big_b, out, tail):
    parts, rows, kt = big_a.shape
    block = parts * rows
    a = big_a[...].reshape(block, kt).astype(F32)
    b = big_b[...].reshape(block, kt).astype(F32)
    mean_a = jnp.sum(a, axis=0, keepdims=True) / block
    mean_b = jnp.sum(b, axis=0, keepdims=True) / block
    a = a - mean_a
    b = b - mean_b
    gram = dot(a.astype(BF), b.astype(BF), 0, 0).astype(BF)
    tail[...] = jnp.zeros_like(tail)
    pos = put_pieces(tail, 0, mean_a, 3)
    pos = put_pieces(tail, pos, jnp.sum(a * a, axis=0, keepdims=True), 3)
    pos = put_pieces(tail, pos, mean_b, 3)
    pos = put_pieces(tail, pos, jnp.sum(b * b, axis=0, keepdims=True), 3)
    put_pieces(tail, pos, jnp.sum(a * b, axis=0, keepdims=True), 3)
    deep = out.shape[1] - 16
    rows_out = tail[...].astype(BF)
    for i in range(out.shape[0]):
        out[i, :deep] = gram[i * deep : (i + 1) * deep]
        out[i, deep:] = rows_out


def merge_body(got, out):
    x_n, deep, _ = got.shape
    sub = deep - 16
    total = got[0, :sub].astype(F32)
    for x in range(1, x_n):
        total = total + got[x, :sub].astype(F32)
    out[:sub] = total.astype(BF)
    for x in range(x_n):
        out[sub + 16 * x : sub + 16 * (x + 1)] = got[x, sub:]


def mix_body(at, mine, theirs, mix, stats, table, offs, *, block):
    sub, kt = mix.shape
    each = (mine.shape[0] - sub) // 16
    sets = 2 * each
    total = block * sets
    low = at[5] == 0
    own, other = mine[sub:].astype(F32), theirs[sub:].astype(F32)
    raws = []
    for tails in (jnp.where(low, own, other), jnp.where(low, other, own)):
        for i in range(each):
            raws.append([joined(tails, 16 * i + 3 * j, 3) for j in range(5)])
    summed = [sum(r[i] for r in raws[1:]) + raws[0][i] for i in range(5)]
    mean_a, mean_b = summed[0] / sets, summed[2] / sets
    square_a, square_b, cross = summed[1], summed[3], summed[4]
    drift_a = jnp.zeros_like(mean_a)
    drift_b = jnp.zeros_like(mean_b)
    table[...] = jnp.zeros_like(table)
    for i, r in enumerate(raws):
        off_a, off_b = r[0] - mean_a, r[2] - mean_b
        square_a = square_a + block * off_a * off_a
        square_b = square_b + block * off_b * off_b
        cross = cross + block * off_a * off_b
        drift_a, drift_b = drift_a + off_a, drift_b + off_b
        table[i : i + 1, :] = off_a
        offs[i : i + 1, :] = block * off_b
    inv_a = lax.rsqrt(square_a / total + NORM_EPS)
    inv_b = lax.rsqrt(square_b / total + NORM_EPS)
    table[sets : sets + 1, :] = inv_a
    diag = cross * (inv_a * inv_b / total)
    coeff = -2.0 * (1.0 - diag) - 2.0 * LAMBDA_OFF * diag
    k_of = lax.broadcasted_iota(jnp.int32, (sub, kt), 0)
    l_of = lax.broadcasted_iota(jnp.int32, (sub, kt), 1)
    chosen = exact((k_of + at[3] == l_of).astype(F32), table[...], 1, 1)
    corr = mine[:sub].astype(F32) + theirs[:sub].astype(F32)
    corr = corr + exact(chosen[:, :sets], offs[...], 1, 0)
    corr = corr * (chosen[:, sets : sets + 1] * (inv_b / total))
    here = k_of + (at[3] + at[4]) == l_of
    mix[...] = jnp.where(
        here, coeff + 2.0 * LAMBDA_OFF * diag, 2.0 * LAMBDA_OFF * corr
    ).astype(BF)
    stats[0:1, :] = mean_a
    stats[1:2, :] = inv_a
    stats[2:3, :] = mean_b
    stats[3:4, :] = inv_b
    stats[4:5, :] = diag
    stats[5:6, :] = drift_a * inv_a / sets
    stats[6:7, :] = drift_b * inv_b / sets
    stats[7:8, :] = diag * (at[4] == 0).astype(F32)


def thirds(value):
    out = []
    for _ in range(3):
        out.append(value.astype(BF))
        value = value - out[-1].astype(F32)
    return out


def correlation(at, mix, stats):
    kt = mix.shape[0]
    k_of = lax.broadcasted_iota(jnp.int32, (kt, kt), 0)
    l_of = lax.broadcasted_iota(jnp.int32, (kt, kt), 1)
    return jnp.where(k_of + at[4] == l_of, stats[4:5, :], mix * (0.5 / LAMBDA_OFF))


def grad_b_body(at, mix4, big_a, stats, sent, kept, grads, tail):
    c = at[2]
    parts, rows, kt = big_a.shape
    line = parts // 2
    mix = mix4[...].reshape(kt, kt)
    wide = mix.astype(F32)
    norm_a = (big_a[...].reshape(parts * rows, kt).astype(F32) - stats[0:1, :]) * stats[1:2, :]
    grads[...] = dot(norm_a.astype(BF), mix, 1, 0).reshape(parts, rows, kt)
    for z in range(line):
        sent[z * rows : (z + 1) * rows] = grads[z * 2 + (1 - c)].astype(BF)
        kept[z * rows : (z + 1) * rows] = grads[z * 2 + c]
    second = jnp.sum(wide * correlation(at, wide, stats), axis=0, keepdims=True)
    first = sum(dot(p, mix, 1, 0) for p in thirds(stats[...]))[5:6]
    tail[...] = jnp.zeros_like(tail)
    pos = put_pieces(tail, 0, second, 3)
    put_pieces(tail, pos, first, 2)
    sent[line * rows :] = tail[...].astype(BF)
    kept[line * rows :] = jnp.zeros_like(tail)
    kept[line * rows : line * rows + 1] = second
    kept[line * rows + 1 : line * rows + 2] = first


def grad_a_body(at, mix4, big_b, stats, out, tail):
    parts, rows, kt = big_b.shape
    mix = mix4[...].reshape(kt, kt)
    wide = mix.astype(F32)
    norm_b = (big_b[...].reshape(parts * rows, kt).astype(F32) - stats[2:3, :]) * stats[3:4, :]
    grad = dot(norm_b.astype(BF), mix, 1, 1).astype(BF)
    k_of = lax.broadcasted_iota(jnp.int32, (kt, kt), 0)
    l_of = lax.broadcasted_iota(jnp.int32, (kt, kt), 1)
    square = jnp.where(k_of + at[4] == l_of, 0.0, wide * wide)
    ones = jnp.ones((8, kt), BF)
    square = sum(dot(ones, p, 1, 1) for p in thirds(square)[:2])[0:1]
    diag = stats[7:8, :]
    on = (at[4] == 0).astype(F32)
    coeff = -2.0 * (on - diag) - 2.0 * LAMBDA_OFF * diag
    centre = (coeff + 2.0 * LAMBDA_OFF * diag).astype(BF).astype(F32)
    pos = put_pieces(tail, 0, square * (0.5 / LAMBDA_OFF) + centre * diag, 2)
    pos = put_pieces(tail, pos, square * (0.25 / LAMBDA_OFF**2) + diag * diag, 2)
    pos = put_pieces(tail, pos, diag, 3)
    put_pieces(tail, pos, sum(dot(p, mix, 1, 1) for p in thirds(stats[...]))[6:7], 1)
    rows_out = tail[...].astype(BF)
    for i in range(parts):
        out[i, :rows] = grad[i * rows : (i + 1) * rows]
        out[i, rows:] = rows_out


def core_body(at, kept, got, own, out1, out2, out3, total, tail):
    zl = at[1]
    rows = own.shape[0] - 8
    deep = kept.shape[0] - 8
    total[...] = kept[:deep] + got[:deep].astype(F32)
    theirs = got[deep:].astype(F32)
    second = kept[deep : deep + 1] + joined(theirs, 0, 3)
    first = kept[deep + 1 : deep + 2] + joined(theirs, 3, 2)
    tail[...] = jnp.zeros_like(tail)
    pos = put_pieces(tail, 0, second, 3)
    put_pieces(tail, pos, first, 2)
    rows_out = tail[...].astype(BF)
    start = lambda step: pl.ds(pl.multiple_of((zl ^ step) * rows, rows), rows)
    for step, out in enumerate((out1, out2, out3), 1):
        out[:rows] = total[start(step), :].astype(BF)
        out[rows:] = rows_out
    own[:rows] = total[start(0), :]
    own[rows:] = jnp.zeros_like(tail)
    own[rows : rows + 1] = second
    own[rows + 1 : rows + 2] = first


def dz_b_body(own, got1, got2, got3, raw_b, stats, out):
    rows = out.shape[0]
    grad = own[:rows]
    second, first = own[rows : rows + 1], own[rows + 1 : rows + 2]
    for got in (got1, got2, got3):
        grad = grad + got[:rows].astype(F32)
        theirs = got[rows:].astype(F32)
        second = second + joined(theirs, 0, 3)
        first = first + joined(theirs, 3, 2)
    inv = stats[3:4, :]
    norm = ((raw_b[...].astype(F32) - stats[2:3, :]) * inv).astype(BF).astype(F32)
    out[...] = (inv * (grad - first - norm * second)).astype(BF)


def back_a_body(got, raw_a, stats, keep, weight, out, diag_out, power_out):
    parts, deep, kt = got.shape
    rows = deep - 8
    grad = got[0, :rows].astype(F32)
    tails = [got[i, rows:].astype(F32) for i in range(parts)]
    for i in range(1, parts):
        grad = grad + got[i, :rows].astype(F32)
    gather = lambda pos, count: sum(
        (joined(t, pos, count) for t in tails[1:]), joined(tails[0], pos, count)
    )
    second, power, diag, first = gather(0, 2), gather(2, 2), gather(4, 3), gather(7, 1)
    inv = stats[1:2, :]
    norm = ((raw_a[...].astype(F32) - stats[0:1, :]) * inv).astype(BF).astype(F32)
    dz = (inv * (grad - first - norm * second)).astype(BF)
    width = keep.shape[1]
    out[...] = keep[...] * dot(dz, weight[...].reshape(width, kt), 1, 1)
    diag_out[...] = diag
    power_out[...] = jnp.broadcast_to(jnp.sum(power, axis=1, keepdims=True), power_out.shape)


def back_b_body(part, dz, keep, weight, power, out, tail):
    rows, width = part.shape
    parts, _, chunk = out.shape
    both = part[...] + keep[...] * dot(dz[...], weight[...].reshape(width, dz.shape[1]), 1, 1)
    both = both.astype(BF)
    tail[...] = jnp.zeros_like(tail)
    put_pieces(tail, 0, power[...], 3)
    rows_out = tail[...].astype(BF)
    for i in range(parts):
        out[i, :rows] = both[:, i * chunk : (i + 1) * chunk]
        out[i, rows:] = rows_out


def end_body(got, out, power_out, *, scale, features):
    line, deep, _ = got.shape
    rows = deep - 8
    total = got[0, :rows].astype(F32)
    power = joined(got[0, rows:].astype(F32), 0, 3)
    for z in range(1, line):
        total = total + got[z, :rows].astype(F32)
        power = power + joined(got[z, rows:].astype(F32), 0, 3)
    out[...] = scale * total
    power_out[0, 0] = jnp.max(power[:, :128]) / features


def on_device(feats, jitter, mask_ids, weight):
    rows, width = feats.shape
    w_rows, kt = weight.shape
    zh_n, x_n, y_n = DP_SHAPE
    zl_n, c_n = TILE_SHAPE
    rows_n = zh_n * x_n
    tile_n = zl_n * c_n
    total = rows * rows_n * y_n
    block = rows * y_n
    sub = kt // x_n
    chunk = width // tile_n
    every = DP + TILE
    pairs = swap_pairs()

    y_at = lax.axis_index("y")
    tile_at = lax.axis_index(TILE)
    at = jnp.stack(
        [
            lax.axis_index("x"),
            lax.axis_index("zl"),
            lax.axis_index("c"),
            lax.axis_index("x") * sub,
            jnp.where(y_at == tile_at, 0, FAR),
            lax.axis_index("zh"),
        ]
    ).astype(jnp.int32)
    view, keep_a, keep_b = masked_views(feats, jitter, mask_ids)

    own = lax.all_gather(weight, "zh", axis=0, tiled=True)
    own = spread(own, "y").reshape(y_n, zh_n, w_rows, kt)
    half = y_n // 2
    back = shift(own, "x", 1)
    ahead = shift(own, "x", x_n - 1)
    far_low = shift(back[:half], "x", 1)
    far_high = shift(ahead[half:], "x", x_n - 1)
    piece, wide_a, raw_b = call(
        project_body,
        "project",
        [((zh_n, x_n, y_n, w_rows, kt), BF), ((y_n, rows, kt), BF), ((rows, kt), BF)],
        (at, view, own, back, ahead, far_low, far_high),
    )

    raw_a = wide_a[0]
    big_a = lax.all_to_all(wide_a, "y", 0, 0, tiled=True)
    own_b = lax.ppermute(raw_b, every, pairs)
    big_b = lax.all_gather(own_b, TILE, axis=0)
    (gram,) = call(
        gram_body, "gram", [((x_n, sub + 16, kt), BF)], (big_a, big_b), [((16, kt), F32)]
    )

    got = lax.all_to_all(gram, "x", 0, 0, tiled=True)
    (got,) = call(merge_body, "merge", [((sub + 16 * x_n, kt), BF)], (got,))
    mix, stats = call(
        lambda *refs: mix_body(*refs, block=block),
        "mix",
        [((sub, kt), BF), ((8, kt), F32)],
        (at, got, flip(got, "zh", 1)),
        [((16, kt), F32), ((rows_n, kt), F32)],
    )
    mix = spread(mix, "x")

    line_rows = zl_n * rows + 8
    sent, kept = call(
        grad_b_body,
        "grad_b",
        [((line_rows, kt), BF), ((line_rows, kt), F32)],
        (at, mix, big_a, stats),
        [((tile_n, rows, kt), F32), ((8, kt), F32)],
    )
    got_b = flip(sent, "c", 1)
    (grad_a,) = call(
        grad_a_body, "grad_a", [((y_n, rows + 8, kt), BF)], (at, mix, big_b, stats), [((8, kt), F32)]
    )
    got_a = lax.all_to_all(grad_a, "y", 0, 0, tiled=True)
    own, *outs = call(
        core_body,
        "core",
        [((rows + 8, kt), F32)] + [((rows + 8, kt), BF)] * 3,
        (at, kept, got_b),
        [((zl_n * rows, kt), F32), ((8, kt), F32)],
    )
    gots = [flip(o, "zl", step) for step, o in enumerate(outs, 1)]
    (dz_b,) = call(dz_b_body, "dz_b", [((rows, kt), BF)], (own, *gots, own_b, stats))
    dz_b = lax.ppermute(dz_b, every, pairs)
    part, diag_corr, power = call(
        back_a_body,
        "back_a",
        [((rows, width), F32), ((1, kt), F32), ((1, chunk), F32)],
        (got_a, raw_a, stats, keep_a, piece),
    )
    (share,) = call(
        back_b_body,
        "back_b",
        [((tile_n, rows + 8, chunk), BF)],
        (part, dz_b, keep_b, piece, power),
        [((8, chunk), F32)],
    )
    got = lax.all_to_all(share, TILE, 0, 0, tiled=True)
    feats_grad, cross_power = call(
        lambda *refs: end_body(*refs, scale=LOSS_SCALE / total, features=kt * tile_n),
        "end",
        [((rows, chunk), F32), ((1, 1), F32)],
        (got,),
    )
    return feats_grad, diag_corr.reshape(kt), cross_power.reshape(())


def solution(mesh):
    fine = Mesh(mesh.devices.reshape(DP_SHAPE + TILE_SHAPE), DP + TILE)
    in_specs = (P(DP, None), P(DP, None), P(DP, None), P(DP, TILE))
    out_specs = (P(DP, TILE), P(TILE), P())
    return jax.shard_map(
        on_device, mesh=fine, in_specs=in_specs, out_specs=out_specs, check_vma=False
    )
```

```python
import jax
import jax.numpy as jnp
from jax import lax
from jax.experimental import pallas as pl
from jax.experimental.pallas import tpu as pltpu
from jax.sharding import Mesh
from jax.sharding import PartitionSpec as P

GROUPS = 32
LAMBDA_OFF = 0.0051
NORM_EPS = 1e-05
LOSS_SCALE = 65536.0
INTERPRET = False

DP_SHAPE = (2, 4, 8)
TILE_SHAPE = (4, 2)
DP = ("zh", "x", "y")
TILE = ("zl", "c")
BF = jnp.bfloat16
F32 = jnp.float32
FAR = 1 << 20


def masked_views(feats, jitter, mask_ids):
    width = feats.shape[1]
    group_size = width // GROUPS
    channel_group = lax.broadcasted_iota(jnp.int32, (1, width), 1) // group_size
    keep_a = (channel_group != mask_ids[:, 0:1]).astype(F32)
    keep_b = (channel_group != mask_ids[:, 1:2]).astype(F32)
    values = feats.astype(F32)
    view_a = (values * keep_a).astype(BF)
    view_b = (values * keep_b + jitter.astype(F32)).astype(BF)
    return jnp.concatenate([view_a, view_b], axis=0), keep_a, keep_b


def spread(value, axes):
    parts = lax.axis_size(axes)
    return lax.all_to_all(
        jnp.broadcast_to(value[None], (parts,) + value.shape), axes, 0, 0, tiled=True
    )


def shift(value, axis, step):
    n = lax.axis_size(axis)
    return lax.ppermute(value, axis, [(i, (i + step) % n) for i in range(n)])


def flip(value, axis, step):
    n = lax.axis_size(axis)
    return lax.ppermute(value, axis, [(i, i ^ step) for i in range(n)])


def swap_pairs():
    rows_n = DP_SHAPE[0] * DP_SHAPE[1]
    n = DP_SHAPE[2]
    where = lambda r, y, t: (r * n + y) * n + t
    return [
        (where(r, y, t), where(r, t, y)) for r in range(rows_n) for y in range(n) for t in range(n)
    ]


def dot(a, b, ca, cb, precision=None):
    return lax.dot_general(
        a, b, (((ca,), (cb,)), ((), ())), precision=precision, preferred_element_type=F32
    )


def exact(a, b, ca, cb):
    return dot(a, b, ca, cb, lax.Precision.HIGHEST)


def put_pieces(ref, at, value, count):
    for i in range(count):
        part = value.astype(BF).astype(F32)
        ref[at + i : at + i + 1, :] = part
        value = value - part
    return at + count


def joined(rows, at, count):
    total = rows[at : at + 1]
    for i in range(1, count):
        total = total + rows[at + i : at + i + 1]
    return total


def call(body, name, outs, args, scratch=()):
    specs = [
        pl.BlockSpec(memory_space=pltpu.SMEM if a.dtype == jnp.int32 and a.ndim == 1 else pltpu.VMEM)
        for a in args
    ]
    return pl.pallas_call(
        body,
        name=name,
        out_shape=[jax.ShapeDtypeStruct(s, d) for s, d in outs],
        in_specs=specs,
        out_specs=[
            pl.BlockSpec(memory_space=pltpu.SMEM if s == (1, 1) else pltpu.VMEM) for s, _ in outs
        ],
        scratch_shapes=[pltpu.VMEM(s, d) for s, d in scratch],
        interpret=INTERPRET,
    )(*args)


def project_b_body(at, view, own, back, ahead, far_low, far_high, piece, raw_b):
    zh_n, x_n, y_n, rows, kt = piece.shape
    x = at[0]
    half = y_n // 2
    after, before, far = lax.rem(x + 1, x_n), lax.rem(x + x_n - 1, x_n), lax.rem(x + 2, x_n)
    for zh in range(zh_n):
        piece[zh, x] = own[:, zh]
        piece[zh, before] = back[:, zh]
        piece[zh, after] = ahead[:, zh]
        piece[zh, far, :half] = far_low[:, zh]
        piece[zh, far, half:] = far_high[:, zh]
    weight = piece[...].reshape(zh_n * x_n * y_n * rows, kt)
    raw_b[...] = dot(view[raw_b.shape[0] :], weight, 1, 0).astype(BF)


def project_a_body(view, weight, wide_a, raw_a):
    n, kt = raw_a.shape
    raw = dot(view[:n], weight[...].reshape(view.shape[1], kt), 1, 0).astype(BF)
    raw_a[...] = raw
    for i in range(wide_a.shape[0]):
        wide_a[i] = raw


def gram_body(big_a, big_b, out, tail):
    parts, rows, kt = big_a.shape
    block = parts * rows
    a = big_a[...].reshape(block, kt).astype(F32)
    b = big_b[...].reshape(block, kt).astype(F32)
    mean_a = jnp.sum(a, axis=0, keepdims=True) / block
    mean_b = jnp.sum(b, axis=0, keepdims=True) / block
    a = a - mean_a
    b = b - mean_b
    gram = dot(a.astype(BF), b.astype(BF), 0, 0).astype(BF)
    tail[...] = jnp.zeros_like(tail)
    pos = put_pieces(tail, 0, mean_a, 3)
    pos = put_pieces(tail, pos, jnp.sum(a * a, axis=0, keepdims=True), 3)
    pos = put_pieces(tail, pos, mean_b, 3)
    pos = put_pieces(tail, pos, jnp.sum(b * b, axis=0, keepdims=True), 3)
    put_pieces(tail, pos, jnp.sum(a * b, axis=0, keepdims=True), 3)
    deep = out.shape[1] - 16
    rows_out = tail[...].astype(BF)
    for i in range(out.shape[0]):
        out[i, :deep] = gram[i * deep : (i + 1) * deep]
        out[i, deep:] = rows_out


def merge_body(got, out):
    x_n, deep, _ = got.shape
    sub = deep - 16
    total = got[0, :sub].astype(F32)
    for x in range(1, x_n):
        total = total + got[x, :sub].astype(F32)
    out[:sub] = total.astype(BF)
    for x in range(x_n):
        out[sub + 16 * x : sub + 16 * (x + 1)] = got[x, sub:]


def mix_body(at, mine, theirs, mix, stats, table, offs, *, block):
    sub, kt = mix.shape
    each = (mine.shape[0] - sub) // 16
    sets = 2 * each
    total = block * sets
    low = at[5] == 0
    own, other = mine[sub:].astype(F32), theirs[sub:].astype(F32)
    raws = []
    for tails in (jnp.where(low, own, other), jnp.where(low, other, own)):
        for i in range(each):
            raws.append([joined(tails, 16 * i + 3 * j, 3) for j in range(5)])
    summed = [sum(r[i] for r in raws[1:]) + raws[0][i] for i in range(5)]
    mean_a, mean_b = summed[0] / sets, summed[2] / sets
    square_a, square_b, cross = summed[1], summed[3], summed[4]
    drift_a = jnp.zeros_like(mean_a)
    drift_b = jnp.zeros_like(mean_b)
    table[...] = jnp.zeros_like(table)
    for i, r in enumerate(raws):
        off_a, off_b = r[0] - mean_a, r[2] - mean_b
        square_a = square_a + block * off_a * off_a
        square_b = square_b + block * off_b * off_b
        cross = cross + block * off_a * off_b
        drift_a, drift_b = drift_a + off_a, drift_b + off_b
        table[i : i + 1, :] = off_a
        offs[i : i + 1, :] = block * off_b
    inv_a = lax.rsqrt(square_a / total + NORM_EPS)
    inv_b = lax.rsqrt(square_b / total + NORM_EPS)
    table[sets : sets + 1, :] = inv_a
    diag = cross * (inv_a * inv_b / total)
    coeff = -2.0 * (1.0 - diag) - 2.0 * LAMBDA_OFF * diag
    k_of = lax.broadcasted_iota(jnp.int32, (sub, kt), 0)
    l_of = lax.broadcasted_iota(jnp.int32, (sub, kt), 1)
    chosen = exact((k_of + at[3] == l_of).astype(F32), table[...], 1, 1)
    corr = mine[:sub].astype(F32) + theirs[:sub].astype(F32)
    corr = corr + exact(chosen[:, :sets], offs[...], 1, 0)
    corr = corr * (chosen[:, sets : sets + 1] * (inv_b / total))
    here = k_of + (at[3] + at[4]) == l_of
    mix[...] = jnp.where(
        here, coeff + 2.0 * LAMBDA_OFF * diag, 2.0 * LAMBDA_OFF * corr
    ).astype(BF)
    stats[0:1, :] = mean_a
    stats[1:2, :] = inv_a
    stats[2:3, :] = mean_b
    stats[3:4, :] = inv_b
    stats[4:5, :] = diag
    stats[5:6, :] = drift_a * inv_a / sets
    stats[6:7, :] = drift_b * inv_b / sets
    stats[7:8, :] = diag * (at[4] == 0).astype(F32)


def thirds(value):
    out = []
    for _ in range(3):
        out.append(value.astype(BF))
        value = value - out[-1].astype(F32)
    return out


def correlation(at, mix, stats):
    kt = mix.shape[0]
    k_of = lax.broadcasted_iota(jnp.int32, (kt, kt), 0)
    l_of = lax.broadcasted_iota(jnp.int32, (kt, kt), 1)
    return jnp.where(k_of + at[4] == l_of, stats[4:5, :], mix * (0.5 / LAMBDA_OFF))


def grad_b_body(at, mix4, big_a, stats, sent, kept, stats_out, grads, tail):
    c = at[2]
    parts, rows, kt = big_a.shape
    line = parts // 2
    mix = mix4[...].reshape(kt, kt)
    wide = mix.astype(F32)
    norm_a = (big_a[...].reshape(parts * rows, kt).astype(F32) - stats[0:1, :]) * stats[1:2, :]
    grads[...] = dot(norm_a.astype(BF), mix, 1, 0).reshape(parts, rows, kt)
    for z in range(line):
        sent[z * rows : (z + 1) * rows] = grads[z * 2 + (1 - c)].astype(BF)
        kept[z * rows : (z + 1) * rows] = grads[z * 2 + c]
    stats_out[...] = stats[...]
    second = jnp.sum(wide * correlation(at, wide, stats), axis=0, keepdims=True)
    first = sum(dot(p, mix, 1, 0) for p in thirds(stats[...]))[5:6]
    tail[...] = jnp.zeros_like(tail)
    pos = put_pieces(tail, 0, second, 3)
    put_pieces(tail, pos, first, 2)
    sent[line * rows :] = tail[...].astype(BF)
    kept[line * rows :] = jnp.zeros_like(tail)
    kept[line * rows : line * rows + 1] = second
    kept[line * rows + 1 : line * rows + 2] = first


def grad_a_body(at, mix4, big_b, stats, out, tail):
    parts, rows, kt = big_b.shape
    mix = mix4[...].reshape(kt, kt)
    wide = mix.astype(F32)
    norm_b = (big_b[...].reshape(parts * rows, kt).astype(F32) - stats[2:3, :]) * stats[3:4, :]
    grad = dot(norm_b.astype(BF), mix, 1, 1).astype(BF)
    k_of = lax.broadcasted_iota(jnp.int32, (kt, kt), 0)
    l_of = lax.broadcasted_iota(jnp.int32, (kt, kt), 1)
    square = jnp.where(k_of + at[4] == l_of, 0.0, wide * wide)
    ones = jnp.ones((8, kt), BF)
    square = sum(dot(ones, p, 1, 1) for p in thirds(square)[:2])[0:1]
    diag = stats[7:8, :]
    on = (at[4] == 0).astype(F32)
    coeff = -2.0 * (on - diag) - 2.0 * LAMBDA_OFF * diag
    centre = (coeff + 2.0 * LAMBDA_OFF * diag).astype(BF).astype(F32)
    pos = put_pieces(tail, 0, square * (0.5 / LAMBDA_OFF) + centre * diag, 2)
    pos = put_pieces(tail, pos, square * (0.25 / LAMBDA_OFF**2) + diag * diag, 2)
    pos = put_pieces(tail, pos, diag, 3)
    put_pieces(tail, pos, sum(dot(p, mix, 1, 1) for p in thirds(stats[...]))[6:7], 1)
    rows_out = tail[...].astype(BF)
    for i in range(parts):
        out[i, :rows] = grad[i * rows : (i + 1) * rows]
        out[i, rows:] = rows_out


def core_body(at, kept, got, own, out1, out2, out3, total, tail):
    zl = at[1]
    rows = own.shape[0] - 8
    deep = kept.shape[0] - 8
    total[...] = kept[:deep] + got[:deep].astype(F32)
    theirs = got[deep:].astype(F32)
    second = kept[deep : deep + 1] + joined(theirs, 0, 3)
    first = kept[deep + 1 : deep + 2] + joined(theirs, 3, 2)
    tail[...] = jnp.zeros_like(tail)
    pos = put_pieces(tail, 0, second, 3)
    put_pieces(tail, pos, first, 2)
    rows_out = tail[...].astype(BF)
    start = lambda step: pl.ds(pl.multiple_of((zl ^ step) * rows, rows), rows)
    for step, out in enumerate((out1, out2, out3), 1):
        out[:rows] = total[start(step), :].astype(BF)
        out[rows:] = rows_out
    own[:rows] = total[start(0), :]
    own[rows:] = jnp.zeros_like(tail)
    own[rows : rows + 1] = second
    own[rows + 1 : rows + 2] = first


def dz_b_body(own, got1, got2, got3, raw_b, stats, out):
    rows = out.shape[0]
    grad = own[:rows]
    second, first = own[rows : rows + 1], own[rows + 1 : rows + 2]
    for got in (got1, got2, got3):
        grad = grad + got[:rows].astype(F32)
        theirs = got[rows:].astype(F32)
        second = second + joined(theirs, 0, 3)
        first = first + joined(theirs, 3, 2)
    inv = stats[3:4, :]
    norm = ((raw_b[...].astype(F32) - stats[2:3, :]) * inv).astype(BF).astype(F32)
    out[...] = (inv * (grad - first - norm * second)).astype(BF)


def back_a_body(got, raw_a, stats, keep, weight, out, diag_out, power_out):
    parts, deep, kt = got.shape
    rows = deep - 8
    grad = got[0, :rows].astype(F32)
    tails = [got[i, rows:].astype(F32) for i in range(parts)]
    for i in range(1, parts):
        grad = grad + got[i, :rows].astype(F32)
    gather = lambda pos, count: sum(
        (joined(t, pos, count) for t in tails[1:]), joined(tails[0], pos, count)
    )
    second, power, diag, first = gather(0, 2), gather(2, 2), gather(4, 3), gather(7, 1)
    inv = stats[1:2, :]
    norm = ((raw_a[...].astype(F32) - stats[0:1, :]) * inv).astype(BF).astype(F32)
    dz = (inv * (grad - first - norm * second)).astype(BF)
    width = keep.shape[1]
    out[...] = keep[...] * dot(dz, weight[...].reshape(width, kt), 1, 1)
    diag_out[...] = diag
    power_out[...] = jnp.broadcast_to(jnp.sum(power, axis=1, keepdims=True), power_out.shape)


def back_b_body(part, dz, keep, weight, power, out, tail):
    rows, width = part.shape
    parts, _, chunk = out.shape
    both = part[...] + keep[...] * dot(dz[...], weight[...].reshape(width, dz.shape[1]), 1, 1)
    both = both.astype(BF)
    tail[...] = jnp.zeros_like(tail)
    put_pieces(tail, 0, power[...], 3)
    rows_out = tail[...].astype(BF)
    for i in range(parts):
        out[i, :rows] = both[:, i * chunk : (i + 1) * chunk]
        out[i, rows:] = rows_out


def end_body(got, out, power_out, *, scale, features):
    line, deep, _ = got.shape
    rows = deep - 8
    total = got[0, :rows].astype(F32)
    power = joined(got[0, rows:].astype(F32), 0, 3)
    for z in range(1, line):
        total = total + got[z, :rows].astype(F32)
        power = power + joined(got[z, rows:].astype(F32), 0, 3)
    out[...] = scale * total
    power_out[0, 0] = jnp.max(power[:, :128]) / features


def on_device(feats, jitter, mask_ids, weight):
    rows, width = feats.shape
    w_rows, kt = weight.shape
    zh_n, x_n, y_n = DP_SHAPE
    zl_n, c_n = TILE_SHAPE
    rows_n = zh_n * x_n
    tile_n = zl_n * c_n
    total = rows * rows_n * y_n
    block = rows * y_n
    sub = kt // x_n
    chunk = width // tile_n
    every = DP + TILE
    pairs = swap_pairs()

    y_at = lax.axis_index("y")
    tile_at = lax.axis_index(TILE)
    at = jnp.stack(
        [
            lax.axis_index("x"),
            lax.axis_index("zl"),
            lax.axis_index("c"),
            lax.axis_index("x") * sub,
            jnp.where(y_at == tile_at, 0, FAR),
            lax.axis_index("zh"),
        ]
    ).astype(jnp.int32)
    view, keep_a, keep_b = masked_views(feats, jitter, mask_ids)

    own = lax.all_gather(weight, "zh", axis=0, tiled=True)
    own = spread(own, "y").reshape(y_n, zh_n, w_rows, kt)
    half = y_n // 2
    back = shift(own, "x", 1)
    ahead = shift(own, "x", x_n - 1)
    far_low = shift(back[:half], "x", 1)
    far_high = shift(ahead[half:], "x", x_n - 1)
    piece, raw_b = call(
        project_b_body,
        "project_b",
        [((zh_n, x_n, y_n, w_rows, kt), BF), ((rows, kt), BF)],
        (at, view, own, back, ahead, far_low, far_high),
    )

    own_b = lax.ppermute(raw_b, every, pairs)
    wide_a, raw_a = call(
        project_a_body,
        "project_a",
        [((y_n, rows, kt), BF), ((rows, kt), BF)],
        (view, piece),
    )
    own_b, wide_a = lax.optimization_barrier((own_b, wide_a))
    big_a = lax.all_to_all(wide_a, "y", 0, 0, tiled=True)
    big_b = lax.all_gather(own_b, TILE, axis=0)
    (gram,) = call(
        gram_body, "gram", [((x_n, sub + 16, kt), BF)], (big_a, big_b), [((16, kt), F32)]
    )

    got = lax.all_to_all(gram, "x", 0, 0, tiled=True)
    (got,) = call(merge_body, "merge", [((sub + 16 * x_n, kt), BF)], (got,))
    mix, stats = call(
        lambda *refs: mix_body(*refs, block=block),
        "mix",
        [((sub, kt), BF), ((8, kt), F32)],
        (at, got, flip(got, "zh", 1)),
        [((16, kt), F32), ((rows_n, kt), F32)],
    )
    mix = spread(mix, "x")

    line_rows = zl_n * rows + 8
    sent, kept, stats_a = call(
        grad_b_body,
        "grad_b",
        [((line_rows, kt), BF), ((line_rows, kt), F32), ((8, kt), F32)],
        (at, mix, big_a, stats),
        [((tile_n, rows, kt), F32), ((8, kt), F32)],
    )
    got_b = flip(sent, "c", 1)
    (grad_a,) = call(
        grad_a_body, "grad_a", [((y_n, rows + 8, kt), BF)], (at, mix, big_b, stats_a), [((8, kt), F32)]
    )
    got_b, grad_a = lax.optimization_barrier((got_b, grad_a))
    got_a = lax.all_to_all(grad_a, "y", 0, 0, tiled=True)
    own, *outs = call(
        core_body,
        "core",
        [((rows + 8, kt), F32)] + [((rows + 8, kt), BF)] * 3,
        (at, kept, got_b),
        [((zl_n * rows, kt), F32), ((8, kt), F32)],
    )
    gots = [flip(o, "zl", step) for step, o in enumerate(outs, 1)]
    (dz_b,) = call(dz_b_body, "dz_b", [((rows, kt), BF)], (own, *gots, own_b, stats))
    dz_b = lax.ppermute(dz_b, every, pairs)
    part, diag_corr, power = call(
        back_a_body,
        "back_a",
        [((rows, width), F32), ((1, kt), F32), ((1, chunk), F32)],
        (got_a, raw_a, stats, keep_a, piece),
    )
    (share,) = call(
        back_b_body,
        "back_b",
        [((tile_n, rows + 8, chunk), BF)],
        (part, dz_b, keep_b, piece, power),
        [((8, chunk), F32)],
    )
    got = lax.all_to_all(share, TILE, 0, 0, tiled=True)
    feats_grad, cross_power = call(
        lambda *refs: end_body(*refs, scale=LOSS_SCALE / total, features=kt * tile_n),
        "end",
        [((rows, chunk), F32), ((1, 1), F32)],
        (got,),
    )
    return feats_grad, diag_corr.reshape(kt), cross_power.reshape(())


def solution(mesh):
    fine = Mesh(mesh.devices.reshape(DP_SHAPE + TILE_SHAPE), DP + TILE)
    in_specs = (P(DP, None), P(DP, None), P(DP, None), P(DP, TILE))
    out_specs = (P(DP, TILE), P(TILE), P())
    return jax.shard_map(
        on_device, mesh=fine, in_specs=in_specs, out_specs=out_specs, check_vma=False
    )
```

```python
import jax
import jax.numpy as jnp
from jax import lax
from jax.experimental import pallas as pl
from jax.experimental.pallas import tpu as pltpu
from jax.sharding import Mesh
from jax.sharding import PartitionSpec as P

GROUPS = 32
LAMBDA_OFF = 0.0051
NORM_EPS = 1e-05
LOSS_SCALE = 65536.0
INTERPRET = False

DP_SHAPE = (2, 4, 8)
TILE_SHAPE = (4, 2)
DP = ("zh", "x", "y")
TILE = ("zl", "c")
BF = jnp.bfloat16
F32 = jnp.float32
FAR = 1 << 20


def masked_views(feats, jitter, mask_ids):
    width = feats.shape[1]
    group_size = width // GROUPS
    channel_group = lax.broadcasted_iota(jnp.int32, (1, width), 1) // group_size
    keep_a = (channel_group != mask_ids[:, 0:1]).astype(F32)
    keep_b = (channel_group != mask_ids[:, 1:2]).astype(F32)
    values = feats.astype(F32)
    view_a = (values * keep_a).astype(BF)
    view_b = (values * keep_b + jitter.astype(F32)).astype(BF)
    return jnp.concatenate([view_a, view_b], axis=0), keep_a, keep_b


def spread(value, axes):
    parts = lax.axis_size(axes)
    return lax.all_to_all(
        jnp.broadcast_to(value[None], (parts,) + value.shape), axes, 0, 0, tiled=True
    )


def shift(value, axis, step):
    n = lax.axis_size(axis)
    return lax.ppermute(value, axis, [(i, (i + step) % n) for i in range(n)])


def flip(value, axis, step):
    n = lax.axis_size(axis)
    return lax.ppermute(value, axis, [(i, i ^ step) for i in range(n)])


def swap_pairs():
    rows_n = DP_SHAPE[0] * DP_SHAPE[1]
    n = DP_SHAPE[2]
    where = lambda r, y, t: (r * n + y) * n + t
    return [
        (where(r, y, t), where(r, t, y)) for r in range(rows_n) for y in range(n) for t in range(n)
    ]


def dot(a, b, ca, cb, precision=None):
    return lax.dot_general(
        a, b, (((ca,), (cb,)), ((), ())), precision=precision, preferred_element_type=F32
    )


def exact(a, b, ca, cb):
    return dot(a, b, ca, cb, lax.Precision.HIGHEST)


def put_pieces(ref, at, value, count):
    for i in range(count):
        part = value.astype(BF).astype(F32)
        ref[at + i : at + i + 1, :] = part
        value = value - part
    return at + count


def joined(rows, at, count):
    total = rows[at : at + 1]
    for i in range(1, count):
        total = total + rows[at + i : at + i + 1]
    return total


def call(body, name, outs, args, scratch=()):
    specs = [
        pl.BlockSpec(memory_space=pltpu.SMEM if a.dtype == jnp.int32 and a.ndim == 1 else pltpu.VMEM)
        for a in args
    ]
    return pl.pallas_call(
        body,
        name=name,
        out_shape=[jax.ShapeDtypeStruct(s, d) for s, d in outs],
        in_specs=specs,
        out_specs=[
            pl.BlockSpec(memory_space=pltpu.SMEM if s == (1, 1) else pltpu.VMEM) for s, _ in outs
        ],
        scratch_shapes=[pltpu.VMEM(s, d) for s, d in scratch],
        interpret=INTERPRET,
    )(*args)


def project_b_body(at, view, own, back, ahead, far_low, far_high, piece, raw_b):
    zh_n, x_n, y_n, rows, kt = piece.shape
    x = at[0]
    half = y_n // 2
    after, before, far = lax.rem(x + 1, x_n), lax.rem(x + x_n - 1, x_n), lax.rem(x + 2, x_n)
    for zh in range(zh_n):
        piece[zh, x] = own[:, zh]
        piece[zh, before] = back[:, zh]
        piece[zh, after] = ahead[:, zh]
        piece[zh, far, :half] = far_low[:, zh]
        piece[zh, far, half:] = far_high[:, zh]
    weight = piece[...].reshape(zh_n * x_n * y_n * rows, kt)
    raw_b[...] = dot(view[raw_b.shape[0] :], weight, 1, 0).astype(BF)


def project_a_body(view, weight, wide_a, raw_a):
    n, kt = raw_a.shape
    raw = dot(view[:n], weight[...].reshape(view.shape[1], kt), 1, 0).astype(BF)
    raw_a[...] = raw
    for i in range(wide_a.shape[0]):
        wide_a[i] = raw


def gram_body(big_a, big_b, out, tail):
    parts, rows, kt = big_a.shape
    block = parts * rows
    a = big_a[...].reshape(block, kt).astype(F32)
    b = big_b[...].reshape(block, kt).astype(F32)
    mean_a = jnp.sum(a, axis=0, keepdims=True) / block
    mean_b = jnp.sum(b, axis=0, keepdims=True) / block
    a = a - mean_a
    b = b - mean_b
    gram = dot(a.astype(BF), b.astype(BF), 0, 0).astype(BF)
    tail[...] = jnp.zeros_like(tail)
    pos = put_pieces(tail, 0, mean_a, 3)
    pos = put_pieces(tail, pos, jnp.sum(a * a, axis=0, keepdims=True), 3)
    pos = put_pieces(tail, pos, mean_b, 3)
    pos = put_pieces(tail, pos, jnp.sum(b * b, axis=0, keepdims=True), 3)
    put_pieces(tail, pos, jnp.sum(a * b, axis=0, keepdims=True), 3)
    deep = out.shape[1] - 16
    rows_out = tail[...].astype(BF)
    for i in range(out.shape[0]):
        out[i, :deep] = gram[i * deep : (i + 1) * deep]
        out[i, deep:] = rows_out


def merge_body(got, out):
    x_n, deep, _ = got.shape
    sub = deep - 16
    total = got[0, :sub].astype(F32)
    for x in range(1, x_n):
        total = total + got[x, :sub].astype(F32)
    out[:sub] = total.astype(BF)
    for x in range(x_n):
        out[sub + 16 * x : sub + 16 * (x + 1)] = got[x, sub:]


def mix_body(at, mine, theirs, mix, stats, table, offs, *, block):
    _, sub, kt = mix.shape
    each = (mine.shape[0] - sub) // 16
    sets = 2 * each
    total = block * sets
    low = at[5] == 0
    own, other = mine[sub:].astype(F32), theirs[sub:].astype(F32)
    raws = []
    for tails in (jnp.where(low, own, other), jnp.where(low, other, own)):
        for i in range(each):
            raws.append([joined(tails, 16 * i + 3 * j, 3) for j in range(5)])
    summed = [sum(r[i] for r in raws[1:]) + raws[0][i] for i in range(5)]
    mean_a, mean_b = summed[0] / sets, summed[2] / sets
    square_a, square_b, cross = summed[1], summed[3], summed[4]
    drift_a = jnp.zeros_like(mean_a)
    drift_b = jnp.zeros_like(mean_b)
    table[...] = jnp.zeros_like(table)
    for i, r in enumerate(raws):
        off_a, off_b = r[0] - mean_a, r[2] - mean_b
        square_a = square_a + block * off_a * off_a
        square_b = square_b + block * off_b * off_b
        cross = cross + block * off_a * off_b
        drift_a, drift_b = drift_a + off_a, drift_b + off_b
        table[i : i + 1, :] = off_a
        offs[i : i + 1, :] = block * off_b
    inv_a = lax.rsqrt(square_a / total + NORM_EPS)
    inv_b = lax.rsqrt(square_b / total + NORM_EPS)
    table[sets : sets + 1, :] = inv_a
    diag = cross * (inv_a * inv_b / total)
    coeff = -2.0 * (1.0 - diag) - 2.0 * LAMBDA_OFF * diag
    k_of = lax.broadcasted_iota(jnp.int32, (sub, kt), 0)
    l_of = lax.broadcasted_iota(jnp.int32, (sub, kt), 1)
    hot = (k_of + at[3] == l_of).astype(F32).astype(BF)
    chosen = sum(dot(hot, p, 1, 1) for p in thirds(table[...]))
    corr = mine[:sub].astype(F32) + theirs[:sub].astype(F32)
    corr = corr + exact(chosen[:, :sets], offs[...], 1, 0)
    corr = corr * (chosen[:, sets : sets + 1] * (inv_b / total))
    here = k_of + (at[3] + at[4]) == l_of
    out = jnp.where(here, coeff + 2.0 * LAMBDA_OFF * diag, 2.0 * LAMBDA_OFF * corr).astype(BF)
    for i in range(mix.shape[0]):
        mix[i] = out
    stats[0:1, :] = mean_a
    stats[1:2, :] = inv_a
    stats[2:3, :] = mean_b
    stats[3:4, :] = inv_b
    stats[4:5, :] = diag
    stats[5:6, :] = drift_a * inv_a / sets
    stats[6:7, :] = drift_b * inv_b / sets
    stats[7:8, :] = diag * (at[4] == 0).astype(F32)


def thirds(value):
    out = []
    for _ in range(3):
        out.append(value.astype(BF))
        value = value - out[-1].astype(F32)
    return out


def correlation(at, mix, stats):
    kt = mix.shape[0]
    k_of = lax.broadcasted_iota(jnp.int32, (kt, kt), 0)
    l_of = lax.broadcasted_iota(jnp.int32, (kt, kt), 1)
    return jnp.where(k_of + at[4] == l_of, stats[4:5, :], mix * (0.5 / LAMBDA_OFF))


def grad_b_body(at, mix4, big_a, stats, sent, kept, stats_out, grads, tail):
    c = at[2]
    parts, rows, kt = big_a.shape
    line = parts // 2
    mix = mix4[...].reshape(kt, kt)
    wide = mix.astype(F32)
    norm_a = (big_a[...].reshape(parts * rows, kt).astype(F32) - stats[0:1, :]) * stats[1:2, :]
    grads[...] = dot(norm_a.astype(BF), mix, 1, 0).reshape(parts, rows, kt)
    for z in range(line):
        sent[z * rows : (z + 1) * rows] = grads[z * 2 + (1 - c)].astype(BF)
        kept[z * rows : (z + 1) * rows] = grads[z * 2 + c]
    stats_out[...] = stats[...]
    second = jnp.sum(wide * correlation(at, wide, stats), axis=0, keepdims=True)
    first = sum(dot(p, mix, 1, 0) for p in thirds(stats[...]))[5:6]
    tail[...] = jnp.zeros_like(tail)
    pos = put_pieces(tail, 0, second, 3)
    put_pieces(tail, pos, first, 2)
    sent[line * rows :] = tail[...].astype(BF)
    kept[line * rows :] = jnp.zeros_like(tail)
    kept[line * rows : line * rows + 1] = second
    kept[line * rows + 1 : line * rows + 2] = first


def grad_a_body(at, mix4, big_b, stats, out, tail):
    parts, rows, kt = big_b.shape
    mix = mix4[...].reshape(kt, kt)
    wide = mix.astype(F32)
    norm_b = (big_b[...].reshape(parts * rows, kt).astype(F32) - stats[2:3, :]) * stats[3:4, :]
    grad = dot(norm_b.astype(BF), mix, 1, 1).astype(BF)
    k_of = lax.broadcasted_iota(jnp.int32, (kt, kt), 0)
    l_of = lax.broadcasted_iota(jnp.int32, (kt, kt), 1)
    square = jnp.where(k_of + at[4] == l_of, 0.0, wide * wide)
    ones = jnp.ones((8, kt), BF)
    square = sum(dot(ones, p, 1, 1) for p in thirds(square)[:2])[0:1]
    diag = stats[7:8, :]
    on = (at[4] == 0).astype(F32)
    coeff = -2.0 * (on - diag) - 2.0 * LAMBDA_OFF * diag
    centre = (coeff + 2.0 * LAMBDA_OFF * diag).astype(BF).astype(F32)
    pos = put_pieces(tail, 0, square * (0.5 / LAMBDA_OFF) + centre * diag, 2)
    pos = put_pieces(tail, pos, square * (0.25 / LAMBDA_OFF**2) + diag * diag, 2)
    pos = put_pieces(tail, pos, diag, 3)
    put_pieces(tail, pos, sum(dot(p, mix, 1, 1) for p in thirds(stats[...]))[6:7], 1)
    rows_out = tail[...].astype(BF)
    for i in range(parts):
        out[i, :rows] = grad[i * rows : (i + 1) * rows]
        out[i, rows:] = rows_out


def core_body(at, kept, got, own, out1, out2, out3, total, tail):
    zl = at[1]
    rows = own.shape[0] - 8
    deep = kept.shape[0] - 8
    total[...] = kept[:deep] + got[:deep].astype(F32)
    theirs = got[deep:].astype(F32)
    second = kept[deep : deep + 1] + joined(theirs, 0, 3)
    first = kept[deep + 1 : deep + 2] + joined(theirs, 3, 2)
    tail[...] = jnp.zeros_like(tail)
    pos = put_pieces(tail, 0, second, 3)
    put_pieces(tail, pos, first, 2)
    rows_out = tail[...].astype(BF)
    start = lambda step: pl.ds(pl.multiple_of((zl ^ step) * rows, rows), rows)
    for step, out in enumerate((out1, out2, out3), 1):
        out[:rows] = total[start(step), :].astype(BF)
        out[rows:] = rows_out
    own[:rows] = total[start(0), :]
    own[rows:] = jnp.zeros_like(tail)
    own[rows : rows + 1] = second
    own[rows + 1 : rows + 2] = first


def dz_b_body(own, got1, got2, got3, raw_b, stats, out):
    rows = out.shape[0]
    grad = own[:rows]
    second, first = own[rows : rows + 1], own[rows + 1 : rows + 2]
    for got in (got1, got2, got3):
        grad = grad + got[:rows].astype(F32)
        theirs = got[rows:].astype(F32)
        second = second + joined(theirs, 0, 3)
        first = first + joined(theirs, 3, 2)
    inv = stats[3:4, :]
    norm = ((raw_b[...].astype(F32) - stats[2:3, :]) * inv).astype(BF).astype(F32)
    out[...] = (inv * (grad - first - norm * second)).astype(BF)


def back_a_body(got, raw_a, stats, keep, weight, out, diag_out, power_out):
    parts, deep, kt = got.shape
    rows = deep - 8
    grad = got[0, :rows].astype(F32)
    tails = [got[i, rows:].astype(F32) for i in range(parts)]
    for i in range(1, parts):
        grad = grad + got[i, :rows].astype(F32)
    gather = lambda pos, count: sum(
        (joined(t, pos, count) for t in tails[1:]), joined(tails[0], pos, count)
    )
    second, power, diag, first = gather(0, 2), gather(2, 2), gather(4, 3), gather(7, 1)
    inv = stats[1:2, :]
    norm = ((raw_a[...].astype(F32) - stats[0:1, :]) * inv).astype(BF).astype(F32)
    dz = (inv * (grad - first - norm * second)).astype(BF)
    width = keep.shape[1]
    out[...] = keep[...] * dot(dz, weight[...].reshape(width, kt), 1, 1)
    diag_out[...] = diag
    power_out[...] = jnp.broadcast_to(jnp.sum(power, axis=1, keepdims=True), power_out.shape)


def back_b_body(part, dz, keep, weight, power, out, tail):
    rows, width = part.shape
    parts, _, chunk = out.shape
    both = part[...] + keep[...] * dot(dz[...], weight[...].reshape(width, dz.shape[1]), 1, 1)
    both = both.astype(BF)
    tail[...] = jnp.zeros_like(tail)
    put_pieces(tail, 0, power[...], 3)
    rows_out = tail[...].astype(BF)
    for i in range(parts):
        out[i, :rows] = both[:, i * chunk : (i + 1) * chunk]
        out[i, rows:] = rows_out


def end_body(got, out, power_out, *, scale, features):
    line, deep, _ = got.shape
    rows = deep - 8
    total = got[0, :rows].astype(F32)
    power = joined(got[0, rows:].astype(F32), 0, 3)
    for z in range(1, line):
        total = total + got[z, :rows].astype(F32)
        power = power + joined(got[z, rows:].astype(F32), 0, 3)
    out[...] = scale * total
    power_out[0, 0] = jnp.max(power[:, :128]) / features


def on_device(feats, jitter, mask_ids, weight):
    rows, width = feats.shape
    w_rows, kt = weight.shape
    zh_n, x_n, y_n = DP_SHAPE
    zl_n, c_n = TILE_SHAPE
    rows_n = zh_n * x_n
    tile_n = zl_n * c_n
    total = rows * rows_n * y_n
    block = rows * y_n
    sub = kt // x_n
    chunk = width // tile_n
    every = DP + TILE
    pairs = swap_pairs()

    y_at = lax.axis_index("y")
    tile_at = lax.axis_index(TILE)
    at = jnp.stack(
        [
            lax.axis_index("x"),
            lax.axis_index("zl"),
            lax.axis_index("c"),
            lax.axis_index("x") * sub,
            jnp.where(y_at == tile_at, 0, FAR),
            lax.axis_index("zh"),
        ]
    ).astype(jnp.int32)
    view, keep_a, keep_b = masked_views(feats, jitter, mask_ids)

    own = lax.all_gather(weight, "zh", axis=0, tiled=True)
    own = spread(own, "y").reshape(y_n, zh_n, w_rows, kt)
    half = y_n // 2
    back = shift(own, "x", 1)
    ahead = shift(own, "x", x_n - 1)
    far_low = shift(back[:half], "x", 1)
    far_high = shift(ahead[half:], "x", x_n - 1)
    piece, raw_b = call(
        project_b_body,
        "project_b",
        [((zh_n, x_n, y_n, w_rows, kt), BF), ((rows, kt), BF)],
        (at, view, own, back, ahead, far_low, far_high),
    )

    own_b = lax.ppermute(raw_b, every, pairs)
    wide_a, raw_a = call(
        project_a_body,
        "project_a",
        [((y_n, rows, kt), BF), ((rows, kt), BF)],
        (view, piece),
    )
    own_b, wide_a = lax.optimization_barrier((own_b, wide_a))
    big_a = lax.all_to_all(wide_a, "y", 0, 0, tiled=True)
    big_b = lax.all_gather(own_b, TILE, axis=0)
    (gram,) = call(
        gram_body, "gram", [((x_n, sub + 16, kt), BF)], (big_a, big_b), [((16, kt), F32)]
    )

    got = lax.all_to_all(gram, "x", 0, 0, tiled=True)
    (got,) = call(merge_body, "merge", [((sub + 16 * x_n, kt), BF)], (got,))
    mix, stats = call(
        lambda *refs: mix_body(*refs, block=block),
        "mix",
        [((x_n, sub, kt), BF), ((8, kt), F32)],
        (at, got, flip(got, "zh", 1)),
        [((16, kt), F32), ((rows_n, kt), F32)],
    )
    mix = lax.all_to_all(mix, "x", 0, 0, tiled=True)

    line_rows = zl_n * rows + 8
    sent, kept, stats_a = call(
        grad_b_body,
        "grad_b",
        [((line_rows, kt), BF), ((line_rows, kt), F32), ((8, kt), F32)],
        (at, mix, big_a, stats),
        [((tile_n, rows, kt), F32), ((8, kt), F32)],
    )
    got_b = flip(sent, "c", 1)
    (grad_a,) = call(
        grad_a_body, "grad_a", [((y_n, rows + 8, kt), BF)], (at, mix, big_b, stats_a), [((8, kt), F32)]
    )
    got_b, grad_a = lax.optimization_barrier((got_b, grad_a))
    got_a = lax.all_to_all(grad_a, "y", 0, 0, tiled=True)
    own, *outs = call(
        core_body,
        "core",
        [((rows + 8, kt), F32)] + [((rows + 8, kt), BF)] * 3,
        (at, kept, got_b),
        [((zl_n * rows, kt), F32), ((8, kt), F32)],
    )
    gots = [flip(o, "zl", step) for step, o in enumerate(outs, 1)]
    (dz_b,) = call(dz_b_body, "dz_b", [((rows, kt), BF)], (own, *gots, own_b, stats))
    dz_b = lax.ppermute(dz_b, every, pairs)
    part, diag_corr, power = call(
        back_a_body,
        "back_a",
        [((rows, width), F32), ((1, kt), F32), ((1, chunk), F32)],
        (got_a, raw_a, stats, keep_a, piece),
    )
    (share,) = call(
        back_b_body,
        "back_b",
        [((tile_n, rows + 8, chunk), BF)],
        (part, dz_b, keep_b, piece, power),
        [((8, chunk), F32)],
    )
    got = lax.all_to_all(share, TILE, 0, 0, tiled=True)
    feats_grad, cross_power = call(
        lambda *refs: end_body(*refs, scale=LOSS_SCALE / total, features=kt * tile_n),
        "end",
        [((rows, chunk), F32), ((1, 1), F32)],
        (got,),
    )
    return feats_grad, diag_corr.reshape(kt), cross_power.reshape(())


def solution(mesh):
    fine = Mesh(mesh.devices.reshape(DP_SHAPE + TILE_SHAPE), DP + TILE)
    in_specs = (P(DP, None), P(DP, None), P(DP, None), P(DP, TILE))
    out_specs = (P(DP, TILE), P(TILE), P())
    return jax.shard_map(
        on_device, mesh=fine, in_specs=in_specs, out_specs=out_specs, check_vma=False
    )
```
